32 devices in a mesh: fsdp: 4 (over x, core), ctx: 2 (over y), tp: 4 (over z).
Axes of the slice: x: 2, y: 2, z: 4, core: 2. Of those that a mesh axis runs over, the one named last changes fastest.
Arguments:
- tokens: bfloat16 [8, 1024, 2048], P('fsdp', 'ctx'), may hold values from -6 to 6
- attn_gain: bfloat16 [2048], P('fsdp'), may hold values from 0.5 to 1.5
- w_query: bfloat16 [2048, 1024], P('fsdp', 'tp'), may hold values from -0.125 to 0.125
- key_matrix: bfloat16 [2048, 256], P('fsdp', 'tp'), may hold values from -0.125 to 0.125
- value_matrix: bfloat16 [2048, 256], P('fsdp', 'tp'), may hold values from -0.125 to 0.125
- query_gain: bfloat16 [64], P('fsdp'), may hold values from 0.5 to 1.5
- key_gain: bfloat16 [64], P('fsdp'), may hold values from 0.5 to 1.5
- w_out: bfloat16 [1024, 2048], P('tp', 'fsdp'), may hold values from -6 to 6
- ffn_gain: bfloat16 [2048], P('fsdp'), may hold values from 0.5 to 1.5
- w_gate: bfloat16 [2048, 1024], P('fsdp', 'tp'), may hold values from -0.125 to 0.125
- w_up: bfloat16 [2048, 1024], P('fsdp', 'tp'), may hold values from -0.125 to 0.125
- w_down: bfloat16 [1024, 2048], P('tp', 'fsdp'), may hold values from -0.1875 to 0.1875
- prefix_len: int32 [8], P('fsdp'), may hold values from 102 to 512
- out_grad: bfloat16 [8, 1024, 2048], P('fsdp', 'ctx'), may hold values from -6 to 6
Outputs:
- layer_out: bfloat16 [8, 1024, 2048], P('fsdp', 'ctx')
- input_grad: bfloat16 [8, 1024, 2048], P('fsdp', 'ctx')
- grad_attn_gain: float32 [2048], P('fsdp')
- grad_query: float32 [2048, 1024], P('fsdp', 'tp')
- grad_key: float32 [2048, 256], P('fsdp', 'tp')
- grad_value: float32 [2048, 256], P('fsdp', 'tp')
- grad_query_gain: float32 [64], P('fsdp')
- grad_key_gain: float32 [64], P('fsdp')
- grad_out: float32 [1024, 2048], P('tp', 'fsdp')
- grad_ffn_gain: float32 [2048], P('fsdp')
- grad_gate: float32 [2048, 1024], P('fsdp', 'tp')
- grad_up: float32 [2048, 1024], P('fsdp', 'tp')
- grad_down: float32 [1024, 2048], P('tp', 'fsdp')
The draws below stay inside these ranges and needn't reach their ends.
All inputs are finite; a program needn't handle non-finite values.
Results may differ from the reference program's by a relative error of at most 0.025.
Values may be sent and summed in bfloat16 or wider, within the bound.
No kernel may reach another device: no remote copies, remote signals or barrier semaphores. Data moves between devices by JAX's collectives and lax.ppermute only.
A program may use at most 192 MiB of HBM per device.

```python
import math
import jax
import jax.numpy as jnp
from jax import lax

MODEL_WIDTH = 2048
QUERY_HEADS = 16
KEY_VALUE_HEADS = 4
HEAD_SIZE = 64
FF = 1024
SEQUENCE_TOKENS = 1024
SEQS = 8


def place_ends(values, stream_key, smallest, high):
    longest = values.shape.index(max(values.shape))
    spots = []
    for shift in (0, 1):
        where = [jax.random.randint(jax.random.fold_in(stream_key, axis), (), 0, length) for axis, length in enumerate(values.shape)]
        where[longest] = (where[longest] + shift) % values.shape[longest]
        spots.append(tuple(where))
    return values.at[spots[0]].set(smallest).at[spots[1]].set(high)


def block_scale(stream_key, shape, split, smallest, largest):
    def one(dim, parts):
        steps = jax.random.uniform(jax.random.fold_in(jax.random.fold_in(stream_key, 6), dim), (parts,), jnp.float32, smallest / len(split), largest / len(split))
        return jnp.repeat(jnp.exp(steps), shape[dim] // parts).reshape((-1,) + (1,) * (len(shape) - dim - 1))

    factor_of = one(*split[0])
    for cut in split[1:]:
        factor_of = factor_of * one(*cut)
    return factor_of


def bell_draw(stream_key, extent, width, most, cuts=(), kind=jnp.bfloat16):
    result = width * jax.random.normal(stream_key, extent, jnp.float32)
    if cuts:
        result = result * block_scale(stream_key, extent, cuts, -0.22, 0.18)
    return jnp.clip(result, -most, most).astype(kind)


def setup_inputs(seed: int = 0) -> dict:
    key_of = jax.random.split(jax.random.key(seed), 15)
    tokens = bell_draw(key_of[0], (SEQS, SEQUENCE_TOKENS, MODEL_WIDTH), 1.0, 6.0, ((0, 4), (1, 2)))
    attn_gain = jnp.clip(1.0 + 0.1 * jax.random.normal(key_of[1], (MODEL_WIDTH,), jnp.float32), 0.5, 1.5).astype(jnp.bfloat16)
    w_query = bell_draw(key_of[2], (MODEL_WIDTH, QUERY_HEADS * HEAD_SIZE), MODEL_WIDTH ** -0.5, 0.125, ((0, 4), (1, 4)))
    key_matrix = bell_draw(key_of[3], (MODEL_WIDTH, KEY_VALUE_HEADS * HEAD_SIZE), MODEL_WIDTH ** -0.5, 0.125, ((0, 4), (1, 4)))
    value_matrix = bell_draw(key_of[4], (MODEL_WIDTH, KEY_VALUE_HEADS * HEAD_SIZE), MODEL_WIDTH ** -0.5, 0.125, ((0, 4), (1, 4)))
    query_gain = jnp.clip(1.0 + 0.1 * jax.random.normal(key_of[5], (HEAD_SIZE,), jnp.float32), 0.5, 1.5).astype(jnp.bfloat16)
    key_gain = jnp.clip(1.0 + 0.1 * jax.random.normal(key_of[6], (HEAD_SIZE,), jnp.float32), 0.5, 1.5).astype(jnp.bfloat16)
    w_out = bell_draw(key_of[7], (QUERY_HEADS * HEAD_SIZE, MODEL_WIDTH), ((SEQUENCE_TOKENS // 4) ** 0.5 * (QUERY_HEADS * HEAD_SIZE) ** -0.5), 6.0, ((0, 4), (1, 4)))
    ffn_gain = jnp.clip(1.0 + 0.1 * jax.random.normal(key_of[8], (MODEL_WIDTH,), jnp.float32), 0.5, 1.5).astype(jnp.bfloat16)
    w_gate = bell_draw(key_of[9], (MODEL_WIDTH, FF), MODEL_WIDTH ** -0.5, 0.125, ((0, 4), (1, 4)))
    w_up = bell_draw(key_of[10], (MODEL_WIDTH, FF), MODEL_WIDTH ** -0.5, 0.125, ((0, 4), (1, 4)))
    w_down = bell_draw(key_of[11], (FF, MODEL_WIDTH), FF ** -0.5, 0.1875, ((0, 4), (1, 4)))
    prefix_len = place_ends(jax.random.randint(key_of[12], (SEQS,), SEQUENCE_TOKENS // 10, SEQUENCE_TOKENS // 2 + 1), jax.random.fold_in(key_of[12], 1), SEQUENCE_TOKENS // 10, (SEQUENCE_TOKENS // 2 + 1) - 1).astype(jnp.int32)
    out_grad = bell_draw(key_of[13], (SEQS, SEQUENCE_TOKENS, MODEL_WIDTH), 1.0, 6.0, ((0, 4), (1, 2)))
    return {"tokens": tokens, "attn_gain": attn_gain, "w_query": w_query, "key_matrix": key_matrix, "value_matrix": value_matrix, "query_gain": query_gain, "key_gain": key_gain, "w_out": w_out, "ffn_gain": ffn_gain, "w_gate": w_gate, "w_up": w_up, "w_down": w_down, "prefix_len": prefix_len, "out_grad": out_grad}


EPSILON = 1e-06
NEGATIVE = -1e+30
ROPE_BASE = 10000.0

@jax.custom_vjp
def reduced_precision(v):
    return lax.optimization_barrier(v.astype(jnp.bfloat16)).astype(jnp.float32)

@jax.custom_vjp
def reduced_backward(v):
    return v

def low_keep(v):
    return (reduced_precision(v), None)

def low_pass(kept, grad):
    return (grad,)

def back_keep(v):
    return (v, None)

def back_low(kept, grad):
    return (reduced_precision(grad),)
reduced_precision.defvjp(low_keep, low_pass)
reduced_backward.defvjp(back_keep, back_low)

def precise_product(left, right):
    return jnp.dot(left, right, precision=lax.Precision.HIGHEST, preferred_element_type=jnp.float32)

def rms_norm(values, gain):
    return values * lax.rsqrt(lax.optimization_barrier(jnp.mean(values * values, axis=-1, keepdims=True)) + EPSILON) * gain

def rotate(values, cos_table, sin_table):
    half_dim = values.shape[-1] // 2
    turned = jnp.concatenate([-values[..., half_dim:], values[..., :half_dim]], axis=-1)
    return values * cos_table + turned * sin_table

def rotary_tables(positions, head_dim):
    inverse_freq = ROPE_BASE ** (-jnp.arange(0, head_dim, 2).astype(jnp.float32) / head_dim)
    angles = positions.astype(jnp.float32)[:, None] * inverse_freq[None, :]
    cos_half = jnp.cos(angles)
    sin_half = jnp.sin(angles)
    return (jnp.concatenate([cos_half, cos_half], -1), jnp.concatenate([sin_half, sin_half], -1))

def layer_forward(inputs, params, prefix):
    attn_gain, w_query, key_matrix, value_matrix, query_gain, key_gain, w_out, ffn_gain, w_gate, w_up, w_down = params
    normalized_input = reduced_precision(rms_norm(inputs, attn_gain))
    query_raw = reduced_backward(precise_product(normalized_input, w_query)).reshape(SEQUENCE_TOKENS, QUERY_HEADS, HEAD_SIZE)
    unnormed_key = reduced_backward(precise_product(normalized_input, key_matrix)).reshape(SEQUENCE_TOKENS, KEY_VALUE_HEADS, HEAD_SIZE)
    value_reduced = reduced_precision(reduced_backward(precise_product(normalized_input, value_matrix))).reshape(SEQUENCE_TOKENS, KEY_VALUE_HEADS, HEAD_SIZE)
    cos_table, sin_table = rotary_tables(jnp.arange(SEQUENCE_TOKENS, dtype=jnp.int32), HEAD_SIZE)
    cos_wide = cos_table[:, None, :]
    sin_wide = sin_table[:, None, :]
    rotated_query = reduced_precision(rotate(rms_norm(query_raw, query_gain), cos_wide, sin_wide))
    key_rot = reduced_precision(rotate(rms_norm(unnormed_key, key_gain), cos_wide, sin_wide))
    rows_per_block = math.gcd(512, SEQUENCE_TOKENS)
    total_blocks = SEQUENCE_TOKENS // rows_per_block
    query_tiles = rotated_query.reshape(total_blocks, rows_per_block, KEY_VALUE_HEADS, QUERY_HEADS // KEY_VALUE_HEADS, HEAD_SIZE)
    block_starts = jnp.arange(total_blocks, dtype=jnp.int32) * rows_per_block
    key_pos = jnp.arange(SEQUENCE_TOKENS, dtype=jnp.int32)

    def attend(scan_item):
        query_part, start_row = scan_item
        query_pos = start_row + jnp.arange(rows_per_block, dtype=jnp.int32)
        scores = jnp.einsum('qkgd,jkd->kgqj', query_part, key_rot, precision=lax.Precision.HIGHEST, preferred_element_type=jnp.float32) * HEAD_SIZE ** (-0.5)
        scores = reduced_backward(scores)
        allowed = (key_pos[None, :] <= query_pos[:, None]) | (key_pos[None, :] < prefix)
        scores = jnp.where(allowed[None, None], scores, NEGATIVE)
        prob_low = reduced_precision(jax.nn.softmax(scores, axis=-1))
        return jnp.einsum('kgqj,jkd->qkgd', prob_low, value_reduced, precision=lax.Precision.HIGHEST, preferred_element_type=jnp.float32)
    attended = lax.map(jax.checkpoint(attend), (query_tiles, block_starts)).reshape(SEQUENCE_TOKENS, QUERY_HEADS * HEAD_SIZE)
    attended_low = reduced_precision(reduced_backward(attended))
    residual = inputs + reduced_backward(precise_product(attended_low, w_out))
    ffn_in = reduced_precision(rms_norm(residual, ffn_gain))
    gate_proj = reduced_backward(precise_product(ffn_in, w_gate))
    up_proj = reduced_backward(precise_product(ffn_in, w_up))
    hidden = reduced_precision(jax.nn.silu(gate_proj) * up_proj)
    return residual + reduced_backward(precise_product(hidden, w_down))

def reference(tokens, attn_gain, w_query, key_matrix, value_matrix, query_gain, key_gain, w_out, ffn_gain, w_gate, w_up, w_down, prefix_len, out_grad):
    params = tuple((weight_arg.astype(jnp.float32) for weight_arg in (attn_gain, w_query, key_matrix, value_matrix, query_gain, key_gain, w_out, ffn_gain, w_gate, w_up, w_down)))

    def per_sequence(summed, scan_item):
        inputs, cotangent, prefix = scan_item

        def forward(inputs_in, *weights):
            return layer_forward(inputs_in, weights, prefix)
        output, pull = jax.vjp(forward, inputs, *params)
        gradients = pull(cotangent)
        summed = tuple((total_now + gradient for total_now, gradient in zip(summed, gradients[1:])))
        return (summed, (output.astype(jnp.bfloat16), gradients[0].astype(jnp.bfloat16)))
    initial = tuple((jnp.zeros_like(param) for param in params))
    summed, (layer_out, input_grad) = lax.scan(per_sequence, initial, (tokens.astype(jnp.float32), out_grad.astype(jnp.float32), prefix_len))
    return (layer_out, input_grad, summed[0], summed[1], summed[2], summed[3], summed[4], summed[5], summed[6], summed[7], summed[8], summed[9], summed[10])
```

```python
import functools

import jax
import jax.numpy as jnp
from jax import lax
from jax.experimental import pallas as pl
from jax.experimental.pallas import tpu as pltpu
from jax.sharding import PartitionSpec as P

EPSILON = 1e-06
NEGATIVE = -1e30
ROPE_BASE = 10000.0
F32 = jnp.float32
BF16 = jnp.bfloat16
VMEM_LIMIT = 60 * 1024 * 1024


def rms_norm(values, gain):
    return values * lax.rsqrt(jnp.mean(values * values, axis=-1, keepdims=True) + EPSILON) * gain


def rotate(values, cos_table, sin_table):
    half_dim = values.shape[-1] // 2
    turned = jnp.concatenate([-values[..., half_dim:], values[..., :half_dim]], axis=-1)
    return values * cos_table + turned * sin_table


def rotary_tables(positions, head_dim):
    inverse_freq = ROPE_BASE ** (-jnp.arange(0, head_dim, 2).astype(F32) / head_dim)
    angles = positions.astype(F32)[:, None] * inverse_freq[None, :]
    cos_half = jnp.cos(angles)
    sin_half = jnp.sin(angles)
    return (jnp.concatenate([cos_half, cos_half], -1), jnp.concatenate([sin_half, sin_half], -1))


def head_post(raw, gain, cos_table, sin_table):
    return rotate(rms_norm(raw, gain), cos_table[None, :, None, :], sin_table[None, :, None, :])


def dot(left, right, dims):
    return lax.dot_general(left, right, (dims, ((), ())), preferred_element_type=F32)


def mm(left, right):
    return dot(left, right, ((1,), (0,)))


def mm_t(left, right):
    return dot(left, right, ((1,), (1,)))


def outer_sum(left, right):
    return dot(left, right, ((0,), (0,)))


def swap_over(axis, bit):
    size = lax.axis_size(axis)
    pairs = [(i, i ^ bit) for i in range(size)]
    return lambda value: lax.ppermute(value, axis, pairs)


def bits_of(size):
    return [1 << b for b in range(size.bit_length() - 1)]


def ring_gather(value, axis, dim):
    size = lax.axis_size(axis)
    me = lax.axis_index(axis)
    pairs = [(i, (i + 1) % size) for i in range(size)]
    width = value.shape[dim]
    shape = list(value.shape)
    shape[dim] = width * size
    whole = jnp.zeros(shape, value.dtype)
    piece = value
    for step in range(size):
        if step:
            piece = lax.ppermute(piece, axis, pairs)
        whole = lax.dynamic_update_slice_in_dim(whole, piece, ((me - step) % size) * width, dim)
    return whole


def cube_gather(value, axis, dim):
    size = lax.axis_size(axis)
    me = lax.axis_index(axis)
    pieces = [(0, value)]
    for bit in reversed(bits_of(size)):
        swap = swap_over(axis, bit)
        pieces = pieces + [(mask ^ bit, swap(piece)) for mask, piece in pieces]
    width = value.shape[dim]
    shape = list(value.shape)
    shape[dim] = width * size
    whole = jnp.zeros(shape, value.dtype)
    for mask, piece in pieces:
        whole = lax.dynamic_update_slice_in_dim(whole, piece, (me ^ mask) * width, dim)
    return whole


def cube_scatter_sum(value, axis):
    size = lax.axis_size(axis)
    me = lax.axis_index(axis)
    bits = bits_of(size)
    current = value.reshape((2,) * len(bits) + value.shape[1:])
    for bit in bits:
        place = current.ndim - (value.ndim - 1) - 1
        mine = jnp.where(me & bit, 1, 0)
        keep = lax.dynamic_index_in_dim(current, mine, place, keepdims=False)
        give = lax.dynamic_index_in_dim(current, 1 - mine, place, keepdims=False)
        got = swap_over(axis, bit)(give.astype(BF16))
        current = keep + got.astype(F32)
    return current


def cube_sum(value, axis):
    for bit in bits_of(lax.axis_size(axis)):
        low = value.astype(BF16)
        value = low.astype(F32) + swap_over(axis, bit)(low).astype(F32)
    return value


def allowed_t(key_count, query_count, query_start, prefix):
    key_pos = lax.broadcasted_iota(jnp.int32, (key_count, query_count), 0)
    query_pos = query_start + lax.broadcasted_iota(jnp.int32, (key_count, query_count), 1)
    return (key_pos <= query_pos) | (key_pos < prefix)


def attend_kernel(info, prefix, q_ref, k_ref, v_ref, out_ref, lse_ref, *, heads, head_dim, tile, scale):
    seq = pl.program_id(0)
    part = pl.program_id(1)
    keys = k_ref[0]
    values = v_ref[0]
    allowed = allowed_t(keys.shape[0], tile, info[0] + part * tile, prefix[seq])
    for head in range(heads):
        lanes = slice(head * head_dim, (head + 1) * head_dim)
        query = q_ref[0, :, lanes]
        scores = mm_t(keys, query) * scale
        scores = jnp.where(allowed, scores, NEGATIVE)
        top = jnp.max(scores, axis=0, keepdims=True)
        weight = jnp.exp(scores - top)
        total = jnp.sum(weight, axis=0, keepdims=True)
        probs = weight * (1.0 / total)
        out_ref[0, :, lanes] = outer_sum(probs.astype(BF16), values)
        lse_ref[0, head : head + 1, :] = top + jnp.log(total)


def attend(info, prefix, query, keys, values, heads, head_dim):
    seqs, rows, _ = query.shape
    length = keys.shape[1]
    tile = min(256, rows)
    scale = head_dim ** (-0.5)
    return pl.pallas_call(
        functools.partial(attend_kernel, heads=heads, head_dim=head_dim, tile=tile, scale=scale),
        grid_spec=pltpu.PrefetchScalarGridSpec(
            num_scalar_prefetch=2,
            grid=(seqs, rows // tile),
            in_specs=[
                pl.BlockSpec((1, tile, heads * head_dim), lambda s, i, *_: (s, i, 0)),
                pl.BlockSpec((1, length, head_dim), lambda s, i, *_: (s, 0, 0)),
                pl.BlockSpec((1, length, head_dim), lambda s, i, *_: (s, 0, 0)),
            ],
            out_specs=[
                pl.BlockSpec((1, tile, heads * head_dim), lambda s, i, *_: (s, i, 0)),
                pl.BlockSpec((1, heads, tile), lambda s, i, *_: (s, 0, i)),
            ],
        ),
        out_shape=[
            jax.ShapeDtypeStruct((seqs, rows, heads * head_dim), F32),
            jax.ShapeDtypeStruct((seqs, heads, rows), F32),
        ],
        compiler_params=pltpu.CompilerParams(vmem_limit_bytes=VMEM_LIMIT),
        cost_estimate=pl.CostEstimate(
            flops=4 * seqs * rows * length * heads * 256,
            bytes_accessed=seqs * rows * heads * head_dim * 8,
            transcendentals=seqs * rows * length * heads,
        ),
        name="attend",
    )(info, prefix, query, keys, values)


def attend_back_kernel(
    info, prefix, q_ref, k_ref, v_ref, d_ref, lse_ref, delta_ref, dq_ref, dk_ref, dv_ref,
    *, heads, head_dim, tile, scale
):
    seq = pl.program_id(0)
    part = pl.program_id(1)

    @pl.when(part == 0)
    def _():
        dk_ref[...] = jnp.zeros_like(dk_ref)
        dv_ref[...] = jnp.zeros_like(dv_ref)

    keys = k_ref[0]
    values = v_ref[0]
    allowed = allowed_t(keys.shape[0], tile, info[0] + part * tile, prefix[seq])
    for head in range(heads):
        lanes = slice(head * head_dim, (head + 1) * head_dim)
        query = q_ref[0, :, lanes]
        dout = d_ref[0, :, lanes]
        scores = mm_t(keys, query) * scale
        probs = jnp.where(allowed, jnp.exp(scores - lse_ref[0, head : head + 1, :]), 0.0)
        dprob = mm_t(values, dout)
        dscore = (probs * (dprob - delta_ref[0, head : head + 1, :])).astype(BF16)
        dv_ref[0] += mm(probs.astype(BF16), dout)
        dk_ref[0] += mm(dscore, query) * scale
        dq_ref[0, :, lanes] = outer_sum(dscore, keys) * scale


def attend_back(info, prefix, query, keys, values, dout, lse, delta, heads, head_dim):
    seqs, rows, _ = query.shape
    length = keys.shape[1]
    tile = min(256, rows)
    scale = head_dim ** (-0.5)
    row_block = pl.BlockSpec((1, tile, heads * head_dim), lambda s, i, *_: (s, i, 0))
    key_block = pl.BlockSpec((1, length, head_dim), lambda s, i, *_: (s, 0, 0))
    stat_block = pl.BlockSpec((1, heads, tile), lambda s, i, *_: (s, 0, i))
    return pl.pallas_call(
        functools.partial(attend_back_kernel, heads=heads, head_dim=head_dim, tile=tile, scale=scale),
        grid_spec=pltpu.PrefetchScalarGridSpec(
            num_scalar_prefetch=2,
            grid=(seqs, rows // tile),
            in_specs=[row_block, key_block, key_block, row_block, stat_block, stat_block],
            out_specs=[row_block, key_block, key_block],
        ),
        out_shape=[
            jax.ShapeDtypeStruct((seqs, rows, heads * head_dim), F32),
            jax.ShapeDtypeStruct((seqs, length, head_dim), F32),
            jax.ShapeDtypeStruct((seqs, length, head_dim), F32),
        ],
        compiler_params=pltpu.CompilerParams(vmem_limit_bytes=VMEM_LIMIT),
        cost_estimate=pl.CostEstimate(
            flops=10 * seqs * rows * length * heads * 256,
            bytes_accessed=seqs * rows * heads * head_dim * 12,
            transcendentals=seqs * rows * length * heads,
        ),
        name="attend_back",
    )(info, prefix, query, keys, values, dout, lse, delta)


def shards(
    tokens, attn_gain, w_query, key_matrix, value_matrix, query_gain, key_gain, w_out, ffn_gain,
    w_gate, w_up, w_down, prefix_len, out_grad,
):
    seqs, block_len, width = tokens.shape
    rows = seqs * block_len
    tp_index = lax.axis_index("tp")
    ctx_count = lax.axis_size("ctx")
    ctx_index = lax.axis_index("ctx")
    fsdp_count = lax.axis_size("fsdp")
    head_dim = query_gain.shape[0] * fsdp_count
    q_cols = w_query.shape[1]
    kv_cols = key_matrix.shape[1]
    heads = q_cols // head_dim
    ff_cols = w_gate.shape[1]

    gains = cube_gather(
        jnp.concatenate([attn_gain, ffn_gain, query_gain, key_gain])[None], "fsdp", 0
    ).astype(F32)
    cuts = [0, attn_gain.size, 2 * attn_gain.size, 2 * attn_gain.size + query_gain.size, gains.shape[1]]
    attn_gain32, ffn_gain32, query_gain32, key_gain32 = (
        gains[:, low:high].reshape(-1) for low, high in zip(cuts, cuts[1:])
    )
    w_qkv = jnp.concatenate([w_query, key_matrix, value_matrix], axis=1)
    own_qkv = cube_gather(w_qkv, "fsdp", 0)

    full_out = cube_gather(ring_gather(w_out, "tp", 0), "fsdp", 1)
    full_gate = cube_gather(ring_gather(w_gate, "tp", 1), "fsdp", 0)
    full_up = cube_gather(ring_gather(w_up, "tp", 1), "fsdp", 0)
    full_down = cube_gather(ring_gather(w_down, "tp", 0), "fsdp", 1)
    full_qkv = cube_gather(ring_gather(w_qkv, "tp", 1), "fsdp", 0)

    query_pos = ctx_index * block_len + jnp.arange(block_len, dtype=jnp.int32)
    cos_table, sin_table = rotary_tables(query_pos, head_dim)
    inputs = tokens.astype(F32).reshape(rows, width)
    normed = rms_norm(inputs, attn_gain32).astype(BF16)
    raw = mm(normed, own_qkv)
    query_raw = raw[:, :q_cols].reshape(seqs, block_len, heads, head_dim)
    key_raw = raw[:, q_cols : q_cols + kv_cols].reshape(seqs, block_len, kv_cols // head_dim, head_dim)
    value_low = raw[:, q_cols + kv_cols :].astype(BF16).reshape(seqs, block_len, kv_cols)
    post = functools.partial(head_post, cos_table=cos_table, sin_table=sin_table)
    query_rot, query_pull = jax.vjp(post, query_raw, query_gain32)
    key_rot, key_pull = jax.vjp(post, key_raw, key_gain32)
    query_low = query_rot.astype(BF16).reshape(seqs, block_len, q_cols)
    key_low = key_rot.astype(BF16).reshape(seqs, block_len, kv_cols)
    key_value = cube_gather(jnp.concatenate([key_low, value_low], axis=2), "ctx", 1)
    keys_all = key_value[:, :, :kv_cols]
    values_all = key_value[:, :, kv_cols:]
    info = (ctx_index * block_len).astype(jnp.int32).reshape(1)
    attended, lse = attend(info, prefix_len, query_low, keys_all, values_all, heads, head_dim)
    attended_own = attended.astype(BF16).reshape(rows, q_cols)
    attended_low = ring_gather(attended_own, "tp", 1)

    residual = inputs + mm(attended_low, full_out)
    ffn_in = rms_norm(residual, ffn_gain32).astype(BF16)
    gate_proj = mm(ffn_in, full_gate)
    up_proj = mm(ffn_in, full_up)
    sig = jax.nn.sigmoid(gate_proj)
    hidden = (gate_proj * sig * up_proj).astype(BF16)
    layer_low = (residual + mm(hidden, full_down)).astype(BF16)
    grad_low = out_grad.reshape(rows, width)
    dhidden = mm_t(grad_low, full_down)
    dgate = (dhidden * up_proj * sig * (1.0 + gate_proj * (1.0 - sig))).astype(BF16)
    dup = (dhidden * gate_proj * sig).astype(BF16)

    def own_cols(values, cols):
        return lax.dynamic_slice_in_dim(values, tp_index * cols, cols, 1)

    grad_down = outer_sum(own_cols(hidden, ff_cols), grad_low)
    grad_gate = outer_sum(ffn_in, own_cols(dgate, ff_cols))
    grad_up = outer_sum(ffn_in, own_cols(dup, ff_cols))
    dffn_in = mm_t(dgate, full_gate) + mm_t(dup, full_up)
    _, ffn_pull = jax.vjp(rms_norm, residual, ffn_gain32)
    dres_norm, grad_ffn_gain = ffn_pull(dffn_in)
    dresidual = grad_low.astype(F32) + dres_norm
    dres_low = dresidual.astype(BF16)
    grad_out = outer_sum(attended_own, dres_low)
    own_out = lax.dynamic_slice_in_dim(full_out, tp_index * q_cols, q_cols, 0)
    dattended = mm_t(dres_low, own_out).astype(BF16)
    delta = jnp.sum(
        (dattended.astype(F32) * attended.reshape(rows, q_cols)).reshape(seqs, block_len, heads, head_dim),
        axis=-1,
    )
    dquery_rot, dkeys, dvalues = attend_back(
        info, prefix_len, query_low, keys_all, values_all,
        dattended.reshape(seqs, block_len, q_cols), lse, jnp.moveaxis(delta, 1, 2), heads, head_dim,
    )
    parts = jnp.concatenate([dkeys, dvalues], axis=2).reshape(seqs, ctx_count, block_len, 2 * kv_cols)
    owned = cube_scatter_sum(jnp.moveaxis(parts, 1, 0), "ctx")
    dquery_raw, grad_query_gain = query_pull(dquery_rot.reshape(query_raw.shape))
    dkey_raw, grad_key_gain = key_pull(owned[:, :, :kv_cols].reshape(key_raw.shape))
    dqkv_own = jnp.concatenate(
        [
            dquery_raw.reshape(rows, q_cols).astype(BF16),
            dkey_raw.reshape(rows, kv_cols).astype(BF16),
            owned[:, :, kv_cols:].reshape(rows, kv_cols).astype(BF16),
        ],
        axis=1,
    )
    dqkv = ring_gather(dqkv_own, "tp", 1)
    grad_qkv = outer_sum(normed, dqkv_own)
    dnormed = mm_t(dqkv, full_qkv)
    _, attn_pull = jax.vjp(rms_norm, inputs, attn_gain32)
    dinput, grad_attn_gain = attn_pull(dnormed)
    input_grad = (dresidual + dinput).astype(BF16)

    def by_rows(gradient):
        return gradient.reshape((fsdp_count, -1) + gradient.shape[1:])

    def by_cols(gradient):
        return jnp.moveaxis(gradient.reshape(gradient.shape[0], fsdp_count, -1), 1, 0)

    def settle(parts):
        return cube_sum(cube_scatter_sum(parts, "fsdp"), "ctx")

    grad_down = settle(by_cols(grad_down))
    grad_gate = settle(by_rows(grad_gate))
    grad_up = settle(by_rows(grad_up))
    grad_out = settle(by_cols(grad_out))
    grad_qkv = settle(by_rows(grad_qkv))
    head_gains = jnp.concatenate([grad_query_gain, grad_key_gain])
    head_gains = lax.psum(head_gains, "tp")
    split = query_gain.size
    gain_parts = jnp.concatenate(
        [
            grad_attn_gain.reshape(fsdp_count, -1),
            grad_ffn_gain.reshape(fsdp_count, -1),
            head_gains[:head_dim].reshape(fsdp_count, -1),
            head_gains[head_dim:].reshape(fsdp_count, -1),
        ],
        axis=1,
    )
    gain_grads = lax.psum(gain_parts, ("fsdp", "ctx"))
    gain_grads = lax.dynamic_index_in_dim(gain_grads, lax.axis_index("fsdp"), 0, keepdims=False)
    return (
        layer_low.reshape(seqs, block_len, width),
        input_grad.reshape(seqs, block_len, width),
        gain_grads[cuts[0] : cuts[1]],
        grad_qkv[:, :q_cols],
        grad_qkv[:, q_cols : q_cols + kv_cols],
        grad_qkv[:, q_cols + kv_cols :],
        gain_grads[cuts[2] : cuts[3]],
        gain_grads[cuts[3] : cuts[4]],
        grad_out,
        gain_grads[cuts[1] : cuts[2]],
        grad_gate,
        grad_up,
        grad_down,
    )


def solution(mesh):
    columns = P("fsdp", "tp")
    across = P("tp", "fsdp")
    vector = P("fsdp")
    data = P("fsdp", "ctx", None)
    return jax.shard_map(
        shards,
        mesh=mesh,
        in_specs=(
            data, vector, columns, columns, columns, vector, vector, across, vector,
            columns, columns, across, vector, data,
        ),
        out_specs=(
            data, data, vector, columns, columns, columns, vector, vector, across, vector,
            columns, columns, across,
        ),
        check_vma=False,
    )
```

```python
import functools

import jax
import jax.numpy as jnp
from jax import lax
from jax.experimental import pallas as pl
from jax.experimental.pallas import tpu as pltpu
from jax.sharding import PartitionSpec as P

EPSILON = 1e-06
NEGATIVE = -1e30
ROPE_BASE = 10000.0
F32 = jnp.float32
BF16 = jnp.bfloat16
VMEM_LIMIT = 60 * 1024 * 1024
ANY = pl.BlockSpec(memory_space=pl.ANY)


def dot(left, right, dims, precision=None):
    return lax.dot_general(
        left, right, (dims, ((), ())), precision=precision, preferred_element_type=F32
    )


def mm(left, right):
    return dot(left, right, ((1,), (0,)))


def mm_t(left, right):
    return dot(left, right, ((1,), (1,)))


def outer_sum(left, right):
    return dot(left, right, ((0,), (0,)))


def params():
    return pltpu.CompilerParams(vmem_limit_bytes=VMEM_LIMIT)


def cost(flops, nbytes, exps=0):
    return pl.CostEstimate(flops=int(flops), bytes_accessed=int(nbytes), transcendentals=int(exps))


def rotary_tables(positions, head_dim):
    inverse_freq = ROPE_BASE ** (-jnp.arange(0, head_dim, 2).astype(F32) / head_dim)
    angles = positions.astype(F32)[:, None] * inverse_freq[None, :]
    return (jnp.cos(angles), jnp.sin(angles))


def swap(value, axis, bit):
    return lax.ppermute(value, axis, [(i, i ^ bit) for i in range(lax.axis_size(axis))])


def bits_of(size):
    return [1 << b for b in range(size.bit_length() - 1)]


def ring(value, axis):
    size = lax.axis_size(axis)
    pieces = [value]
    for _ in range(size - 1):
        pieces.append(lax.ppermute(pieces[-1], axis, [(i, (i + 1) % size) for i in range(size)]))
    return pieces


def cube(value, axis):
    stacked = value[None]
    for bit in bits_of(lax.axis_size(axis)):
        stacked = jnp.concatenate([stacked, swap(stacked, axis, bit)], axis=0)
    return stacked


def cube_sum(value, axis):
    for bit in bits_of(lax.axis_size(axis)):
        low = value.astype(BF16)
        value = low.astype(F32) + swap(low, axis, bit).astype(F32)
    return value


def cube_own(value, axis):
    for bit in reversed(bits_of(lax.axis_size(axis))):
        half = value.shape[0] // 2
        value = value[:half] + swap(value[half:].astype(BF16), axis, bit).astype(F32)
    return value[0]


def after(value, *others):
    return lax.optimization_barrier((value,) + others)[0]


def place_of():
    return jnp.stack(
        [lax.axis_index("fsdp"), lax.axis_index("ctx"), lax.axis_index("tp")]
    ).astype(jnp.int32)


class Pieces:
    def __init__(self, arrays, listing, shape, dims):
        self.arrays = arrays
        self.listing = listing
        self.shape = shape
        self.dims = dims

    def copies(self, place, refs, target, only_own=False):
        for number, index, where in self.listing:
            spot = where(place)
            if spot is None:
                continue
            row, col, own = spot
            if only_own and not own:
                continue
            rows, cols = self.shape
            if only_own:
                row = row - place[2] * self.dims
            yield (
                refs[number].at[index],
                target.at[pl.ds(pl.multiple_of(row, rows), rows), pl.ds(pl.multiple_of(col, cols), cols)],
            )


def gathered_columns(stack, lead, fsdp_count, tp_count, shape):
    rows, cols = shape
    listing = []
    for f in range(fsdp_count):
        for t in range(tp_count):
            listing.append(
                (0, (f * tp_count + t,) + lead, lambda place, f=f, t=t: (f * rows, t * cols, False))
            )
    return Pieces([stack], listing, shape, rows)


def gathered_rows(stack, lead, fsdp_count, tp_count, shape):
    rows, cols = shape
    listing = []
    for f in range(fsdp_count):
        for t in range(tp_count):
            listing.append(
                (0, (f * tp_count + t,) + lead, lambda place, f=f, t=t: (t * rows, f * cols, False))
            )
    return Pieces([stack], listing, shape, rows)


def travelled_rows(shard, tp_count):
    rows = shard.shape[0] // 2
    cols = shard.shape[1]
    half = lax.dynamic_slice_in_dim(shard, lax.axis_index("ctx") * rows, rows, 0)
    pair = jnp.stack([half, swap(half, "fsdp", 2)])
    mine = jnp.stack(ring(pair, "tp"))
    other = swap(mine, "ctx", 1)
    arrays = [mine, other, swap(mine, "fsdp", 1), swap(other, "fsdp", 1)]
    listing = []
    for number in range(4):
        for k in range(tp_count):
            for x in range(2):

                def where(place, number=number, k=k, x=x):
                    tp = lax.rem(place[2] + (tp_count - k), tp_count)
                    row = tp * (2 * rows) + (place[1] ^ (number & 1)) * rows
                    col = (place[0] ^ (2 * x + (number >> 1))) * cols
                    return (row, col, k == 0)

                listing.append((number, (k, x), where))
    return Pieces(arrays, listing, (rows, cols), 2 * rows)


def fetch(copies, sems, base=0):
    started = [pltpu.make_async_copy(src, dst, sems.at[base + i]) for i, (src, dst) in enumerate(copies)]
    for copy in started:
        copy.start()
    return started


def group_mean(values, head_dim):
    width = values.shape[1]
    row = lax.broadcasted_iota(jnp.int32, (width, width), 0) // head_dim
    col = lax.broadcasted_iota(jnp.int32, (width, width), 1) // head_dim
    ones = jnp.where(row == col, 1.0 / head_dim, 0.0)
    return dot(values, ones, ((1,), (0,)), precision=lax.Precision.HIGHEST)


def half_turn(values, head_dim):
    width = values.shape[1]
    half = head_dim // 2
    lane = lax.broadcasted_iota(jnp.int32, values.shape, 1)
    low = (lane & (head_dim - 1)) < half
    return jnp.where(low, pltpu.roll(values, width - half, 1), pltpu.roll(values, half, 1)), low


def project_kernel(
    place, tok_ref, gain_ref, hgain_ref, cos_ref, sin_ref, w_in, normed_ref, raw_ref, q_ref, kv_ref,
    w_ref, sems, *, head_dim, q_cols, rot_cols, chunk,
):
    shard = w_in.shape[1]
    tile = tok_ref.shape[1]

    @pl.when(pl.program_id(0) == 0)
    def _():
        moves = []
        for m in range(w_in.shape[0]):
            row = pl.multiple_of((place[0] ^ m) * shard, shard)
            moves.append((w_in.at[m], w_ref.at[pl.ds(row, shard), :]))
        for copy in fetch(moves, sems):
            copy.wait()

    def norm(i, carry):
        rows = pl.ds(pl.multiple_of(i * chunk, chunk), chunk)
        x = tok_ref[0, rows, :].astype(F32)
        r = lax.rsqrt(jnp.mean(x * x, axis=-1, keepdims=True) + EPSILON)
        normed_ref[0, rows, :] = (x * r * gain_ref[...]).astype(BF16)
        return carry

    lax.fori_loop(0, tile // chunk, norm, 0)
    raw = mm(normed_ref[0], w_ref[...])
    raw_ref[0] = raw
    scale = lax.rsqrt(group_mean(raw * raw, head_dim) + EPSILON)
    n = raw * scale * hgain_ref[...]
    turned, low = half_turn(n, head_dim)
    rot = n * cos_ref[...] + jnp.where(low, -turned, turned) * sin_ref[...]
    lane = lax.broadcasted_iota(jnp.int32, raw.shape, 1)
    out = jnp.where(lane < rot_cols, rot, raw).astype(BF16)
    q_ref[0] = out[:, :q_cols]
    kv_ref[0] = out[:, q_cols:]


def project(place, tokens, gain, hgain, cos, sin, w_in, head_dim, q_cols, rot_cols):
    seqs, rows, width = tokens.shape
    cols = w_in.shape[2]
    row_spec = lambda last: pl.BlockSpec((1, rows, last), lambda s, *_: (s, 0, 0))
    flat = lambda shape: pl.BlockSpec(shape, lambda s, *_: (0,) * len(shape))
    return pl.pallas_call(
        functools.partial(
            project_kernel, head_dim=head_dim, q_cols=q_cols, rot_cols=rot_cols, chunk=64
        ),
        grid_spec=pltpu.PrefetchScalarGridSpec(
            num_scalar_prefetch=1,
            grid=(seqs,),
            in_specs=[
                row_spec(width), flat((1, width)), flat((1, cols)), flat((rows, cols)), flat((rows, cols)), ANY,
            ],
            out_specs=[row_spec(width), row_spec(cols), row_spec(q_cols), row_spec(cols - q_cols)],
            scratch_shapes=[
                pltpu.VMEM((width, cols), BF16), pltpu.SemaphoreType.DMA((w_in.shape[0],)),
            ],
        ),
        out_shape=[
            jax.ShapeDtypeStruct((seqs, rows, width), BF16),
            jax.ShapeDtypeStruct((seqs, rows, cols), F32),
            jax.ShapeDtypeStruct((seqs, rows, q_cols), BF16),
            jax.ShapeDtypeStruct((seqs, rows, cols - q_cols), BF16),
        ],
        compiler_params=params(),
        cost_estimate=cost(2 * seqs * rows * width * cols, seqs * rows * width * 4),
        name="project",
    )(place, tokens, gain, hgain, cos, sin, w_in)


def allowed_t(place, prefix, part, key_count, block, tile):
    j = lax.broadcasted_iota(jnp.int32, (key_count, tile), 0)
    key_pos = (place ^ (j // block)) * block + (j & (block - 1))
    query_pos = place * block + part * tile + lax.broadcasted_iota(jnp.int32, (key_count, tile), 1)
    return (key_pos <= query_pos) | (key_pos < prefix)


def attend_kernel(place, prefix, q_ref, kv_ref, out_ref, lse_ref, *, heads, head_dim, tile, block):
    seq = pl.program_id(0)
    part = pl.program_id(1)
    pairs = kv_ref[:, 0].reshape(-1, 2 * head_dim)
    keys = pairs[:, :head_dim]
    values = pairs[:, head_dim:]
    allowed = allowed_t(place[1], prefix[seq], part, pairs.shape[0], block, tile)
    for head in range(heads):
        lanes = slice(head * head_dim, (head + 1) * head_dim)
        scores = mm_t(keys, q_ref[0, :, lanes]) * (head_dim ** (-0.5))
        scores = jnp.where(allowed, scores, NEGATIVE)
        top = jnp.max(scores, axis=0, keepdims=True)
        weight = jnp.exp(scores - top)
        total = jnp.sum(weight, axis=0, keepdims=True)
        probs = weight * (1.0 / total)
        out_ref[0, :, lanes] = outer_sum(probs.astype(BF16), values).astype(BF16)
        lse_ref[0, head : head + 1, :] = top + jnp.log(total)


def attention_specs(seqs, rows, q_cols, heads, kv_all):
    tile = min(256, rows)
    blocks, _, block, pair = kv_all.shape
    row_block = pl.BlockSpec((1, tile, q_cols), lambda s, i, *_: (s, i, 0))
    key_block = pl.BlockSpec((blocks, 1, block, pair), lambda s, i, *_: (0, s, 0, 0))
    stat_block = pl.BlockSpec((1, heads, tile), lambda s, i, *_: (s, 0, i))
    return tile, blocks, block, pair, row_block, key_block, stat_block


def attend(place, prefix, query, kv_all, heads, head_dim):
    seqs, rows, q_cols = query.shape
    tile, blocks, block, pair, row_block, key_block, stat_block = attention_specs(
        seqs, rows, q_cols, heads, kv_all
    )
    elements = seqs * rows * blocks * block * heads
    return pl.pallas_call(
        functools.partial(attend_kernel, heads=heads, head_dim=head_dim, tile=tile, block=block),
        grid_spec=pltpu.PrefetchScalarGridSpec(
            num_scalar_prefetch=2,
            grid=(seqs, rows // tile),
            in_specs=[row_block, key_block],
            out_specs=[row_block, stat_block],
        ),
        out_shape=[
            jax.ShapeDtypeStruct((seqs, rows, q_cols), BF16),
            jax.ShapeDtypeStruct((seqs, heads, rows), F32),
        ],
        compiler_params=params(),
        cost_estimate=cost(elements * 1024, query.size * 4, elements),
        name="attend",
    )(place, prefix, query, kv_all)


def attend_back_kernel(
    place, prefix, q_ref, kv_ref, d_ref, lse_ref, dq_ref, dkv_ref, *, heads, head_dim, tile, block
):
    seq = pl.program_id(0)
    part = pl.program_id(1)
    scale = head_dim ** (-0.5)
    pairs = kv_ref[:, 0].reshape(-1, 2 * head_dim)
    keys = pairs[:, :head_dim]
    values = pairs[:, head_dim:]
    allowed = allowed_t(place[1], prefix[seq], part, pairs.shape[0], block, tile)
    dkeys = None
    dvalues = None
    for head in range(heads):
        lanes = slice(head * head_dim, (head + 1) * head_dim)
        query = q_ref[0, :, lanes]
        dout = d_ref[0, :, lanes]
        scores = mm_t(keys, query) * scale
        probs = jnp.where(allowed, jnp.exp(scores - lse_ref[0, head : head + 1, :]), 0.0)
        weighted = probs * mm_t(values, dout)
        delta = jnp.sum(weighted, axis=0, keepdims=True)
        dscore = (weighted - probs * delta).astype(BF16)
        dv = mm(probs.astype(BF16), dout)
        dk = mm(dscore, query)
        dkeys = dk if dkeys is None else dkeys + dk
        dvalues = dv if dvalues is None else dvalues + dv
        dq_ref[0, :, lanes] = outer_sum(dscore, keys) * scale
    both = jnp.concatenate([dkeys * scale, dvalues], axis=1).reshape(dkv_ref.shape[0], block, -1)

    @pl.when(part == 0)
    def _():
        dkv_ref[:, 0] = both

    @pl.when(part > 0)
    def _():
        dkv_ref[:, 0] += both


def attend_back(place, prefix, query, kv_all, dout, lse, heads, head_dim):
    seqs, rows, q_cols = query.shape
    tile, blocks, block, pair, row_block, key_block, stat_block = attention_specs(
        seqs, rows, q_cols, heads, kv_all
    )
    elements = seqs * rows * blocks * block * heads
    return pl.pallas_call(
        functools.partial(attend_back_kernel, heads=heads, head_dim=head_dim, tile=tile, block=block),
        grid_spec=pltpu.PrefetchScalarGridSpec(
            num_scalar_prefetch=2,
            grid=(seqs, rows // tile),
            in_specs=[row_block, key_block, row_block, stat_block],
            out_specs=[row_block, key_block],
        ),
        out_shape=[
            jax.ShapeDtypeStruct((seqs, rows, q_cols), F32),
            jax.ShapeDtypeStruct((blocks, seqs, block, pair), F32),
        ],
        compiler_params=params(),
        cost_estimate=cost(elements * 2560, query.size * 8, elements),
        name="attend_back",
    )(place, prefix, query, kv_all, dout, lse)


def residual_kernel(*refs, tp_count, out_w, down_w, step):
    place, tok_ref, og_ref, gain_ref = refs[:4]
    refs = refs[4:]
    att_in, refs = refs[:tp_count], refs[tp_count:]
    out_in, refs = refs[: len(out_w.arrays)], refs[len(out_w.arrays) :]
    down_in, refs = refs[: len(down_w.arrays)], refs[len(down_w.arrays) :]
    res_ref, fin_ref, dh_ref, att, wo, wd, sems = refs
    seq = pl.program_id(0)
    tile = tok_ref.shape[1]
    width = tok_ref.shape[2]
    cols = att_in[0].shape[1]

    @pl.when(seq == 0)
    def _():
        moves = []
        for k in range(tp_count):
            col = lax.rem(place[2] + (tp_count - k), tp_count) * cols
            moves.append((att_in[k], att.at[:, pl.ds(pl.multiple_of(col, cols), cols)]))
        moves += list(out_w.copies(place, out_in, wo))
        first = fetch(moves, sems)
        second = fetch(list(down_w.copies(place, down_in, wd)), sems, len(first))
        for copy in first + second:
            copy.wait()

    base = pl.multiple_of(seq * tile, tile)

    def out_part(i, total):
        lanes = pl.ds(pl.multiple_of(i * step, step), step)
        res = tok_ref[0, :, lanes].astype(F32) + mm(att[pl.ds(base, tile), :], wo[:, lanes])
        res_ref[0, :, lanes] = res
        return total + res * res

    total = lax.fori_loop(0, width // step, out_part, jnp.zeros((tile, step), F32))
    r = lax.rsqrt(jnp.sum(total, axis=-1, keepdims=True) / width + EPSILON)

    def norm(i, carry):
        lanes = pl.ds(pl.multiple_of(i * step, step), step)
        fin_ref[0, :, lanes] = (res_ref[0, :, lanes] * r * gain_ref[:, lanes]).astype(BF16)
        return carry

    lax.fori_loop(0, width // step, norm, 0)

    def back(i, carry):
        part = pl.ds(pl.multiple_of(i * step, step), step)
        dh_ref[0, :, part] = mm_t(og_ref[0], wd[part, :])
        return carry

    lax.fori_loop(0, wd.shape[0] // step, back, 0)


def residual_part(place, tokens, out_grad, gain, att, out_w, down_w, hidden_cols):
    seqs, rows, width = tokens.shape
    inner = att[0].shape[1] * len(att)
    row_spec = lambda last: pl.BlockSpec((1, rows, last), lambda s, *_: (s, 0, 0))
    count = len(att) + len(out_w.listing) + len(down_w.listing)
    arrays = list(att) + out_w.arrays + down_w.arrays
    return pl.pallas_call(
        functools.partial(residual_kernel, tp_count=len(att), out_w=out_w, down_w=down_w, step=256),
        grid_spec=pltpu.PrefetchScalarGridSpec(
            num_scalar_prefetch=1,
            grid=(seqs,),
            in_specs=[row_spec(width), row_spec(width), pl.BlockSpec((1, width), lambda s, *_: (0, 0))]
            + [ANY] * len(arrays),
            out_specs=[row_spec(width), row_spec(width), row_spec(hidden_cols)],
            scratch_shapes=[
                pltpu.VMEM((seqs * rows, inner), BF16),
                pltpu.VMEM((inner, width), BF16),
                pltpu.VMEM((hidden_cols, width), BF16),
                pltpu.SemaphoreType.DMA((count,)),
            ],
        ),
        out_shape=[
            jax.ShapeDtypeStruct((seqs, rows, width), F32),
            jax.ShapeDtypeStruct((seqs, rows, width), BF16),
            jax.ShapeDtypeStruct((seqs, rows, hidden_cols), F32),
        ],
        compiler_params=params(),
        cost_estimate=cost(2 * seqs * rows * width * (inner + hidden_cols), seqs * rows * width * 12),
        name="residual_part",
    )(place, tokens, out_grad, gain, *arrays)


def ffn_kernel(*refs, gate_w, up_w, down_w, out_w, step, chunk, own_cols):
    place, res_ref, fin_ref, dh_ref, og_ref, gain_ref = refs[:6]
    refs = refs[6:]
    gate_in, refs = refs[: len(gate_w.arrays)], refs[len(gate_w.arrays) :]
    down_in, refs = refs[: len(down_w.arrays)], refs[len(down_w.arrays) :]
    out_in, refs = refs[: len(out_w.arrays)], refs[len(out_w.arrays) :]
    (
        lay_ref, dres_ref, hid_ref, dgate_ref, dup_ref, datt_ref, gsum_ref,
        wg, wu, wd, wo, hid, dgate, dup, lift, sems,
    ) = refs
    seq = pl.program_id(0)
    tile = res_ref.shape[1]
    width = res_ref.shape[2]
    ff = wd.shape[0]

    @pl.when(seq == 0)
    def _():
        moves = list(gate_w.copies(place, gate_in, wg)) + list(up_w.copies(place, gate_in, wu))
        moves += list(down_w.copies(place, down_in, wd)) + list(out_w.copies(place, out_in, wo, True))
        for copy in fetch(moves, sems):
            copy.wait()

    def square(i, total):
        lanes = pl.ds(pl.multiple_of(i * step, step), step)
        res = res_ref[0, :, lanes]
        return total + res * res

    total = lax.fori_loop(0, width // step, square, jnp.zeros((tile, step), F32))
    r = lax.rsqrt(jnp.sum(total, axis=-1, keepdims=True) / width + EPSILON)

    def inner(i, carry):
        lanes = pl.ds(pl.multiple_of(i * step, step), step)
        gate = mm(fin_ref[0], wg[:, lanes])
        up = mm(fin_ref[0], wu[:, lanes])
        grad = dh_ref[0, :, lanes]
        sig = 1.0 / (1.0 + jnp.exp(-gate))
        silu = gate * sig
        hid[:, lanes] = (silu * up).astype(BF16)
        dgate[:, lanes] = (grad * up * sig * (1.0 + gate * (1.0 - sig))).astype(BF16)
        dup[:, lanes] = (grad * silu).astype(BF16)
        return carry

    lax.fori_loop(0, ff // step, inner, 0)
    own = pl.ds(pl.multiple_of(place[2] * own_cols, own_cols), own_cols)
    hid_ref[0] = hid[:, own]
    dgate_ref[0] = dgate[:, own]
    dup_ref[0] = dup[:, own]

    def outer(i, total):
        lanes = pl.ds(pl.multiple_of(i * step, step), step)
        res = res_ref[0, :, lanes]
        lay_ref[0, :, lanes] = (res + mm(hid[...], wd[:, lanes])).astype(BF16)
        grad = mm_t(dgate[...], wg[lanes, :]) + mm_t(dup[...], wu[lanes, :])
        gsum = jnp.sum(grad * res * r, axis=0, keepdims=True)

        @pl.when(seq == 0)
        def _():
            gsum_ref[:, lanes] = gsum

        @pl.when(seq > 0)
        def _():
            gsum_ref[:, lanes] += gsum

        u = grad * gain_ref[:, lanes]
        lift[:, lanes] = u
        return total + res * u

    total = lax.fori_loop(0, width // step, outer, jnp.zeros((tile, step), F32))
    pull = r * r * r * (jnp.sum(total, axis=-1, keepdims=True) / width)

    def finish(i, carry):
        lanes = pl.ds(pl.multiple_of(i * step, step), step)
        grad = og_ref[0, :, lanes].astype(F32) + r * lift[:, lanes] - res_ref[0, :, lanes] * pull
        dres_ref[0, :, lanes] = grad.astype(BF16)
        return carry

    lax.fori_loop(0, width // step, finish, 0)
    datt_ref[0] = mm_t(dres_ref[0], wo[...]).astype(BF16)


def ffn(place, residual, ffn_in, dhidden, out_grad, gain, gate_w, up_w, down_w, out_w, own_cols, q_cols):
    seqs, rows, width = residual.shape
    hidden_cols = dhidden.shape[2]
    row_spec = lambda last: pl.BlockSpec((1, rows, last), lambda s, *_: (s, 0, 0))
    vec = pl.BlockSpec((1, width), lambda s, *_: (0, 0))
    arrays = gate_w.arrays + down_w.arrays + out_w.arrays
    count = len(gate_w.listing) * 2 + len(down_w.listing) + len(out_w.listing)
    once = dict(pipeline_mode=pl.Buffered(1))
    row_once = lambda last: pl.BlockSpec((1, rows, last), lambda s, *_: (s, 0, 0), **once)
    return pl.pallas_call(
        functools.partial(
            ffn_kernel, gate_w=gate_w, up_w=up_w, down_w=down_w, out_w=out_w, step=256, chunk=64,
            own_cols=own_cols,
        ),
        grid_spec=pltpu.PrefetchScalarGridSpec(
            num_scalar_prefetch=1,
            grid=(seqs,),
            in_specs=[row_spec(width), row_spec(width), row_spec(hidden_cols), row_spec(width), vec]
            + [ANY] * len(arrays),
            out_specs=[
                row_spec(width), row_spec(width), row_spec(own_cols), row_spec(own_cols), row_spec(own_cols),
                row_spec(q_cols), vec,
            ],
            scratch_shapes=[
                pltpu.VMEM((width, hidden_cols), BF16),
                pltpu.VMEM((width, hidden_cols), BF16),
                pltpu.VMEM((hidden_cols, width), BF16),
                pltpu.VMEM((q_cols, width), BF16),
                pltpu.VMEM((rows, hidden_cols), BF16),
                pltpu.VMEM((rows, hidden_cols), BF16),
                pltpu.VMEM((rows, hidden_cols), BF16),
                pltpu.VMEM((rows, width), F32),
                pltpu.SemaphoreType.DMA((count,)),
            ],
        ),
        out_shape=[
            jax.ShapeDtypeStruct((seqs, rows, width), BF16),
            jax.ShapeDtypeStruct((seqs, rows, width), BF16),
            jax.ShapeDtypeStruct((seqs, rows, own_cols), BF16),
            jax.ShapeDtypeStruct((seqs, rows, own_cols), BF16),
            jax.ShapeDtypeStruct((seqs, rows, own_cols), BF16),
            jax.ShapeDtypeStruct((seqs, rows, q_cols), BF16),
            jax.ShapeDtypeStruct((1, width), F32),
        ],
        compiler_params=params(),
        cost_estimate=cost(
            2 * seqs * rows * width * (5 * hidden_cols + q_cols), seqs * rows * width * 14
        ),
        name="ffn",
    )(place, residual, ffn_in, dhidden, out_grad, gain, *arrays)


def head_back_kernel(
    raw_ref, dq_ref, dkv_ref, hgain_ref, cos_ref, sin_ref, out_ref, gsum_ref, *, head_dim, rot_cols
):
    seq = pl.program_id(0)
    raw = raw_ref[0]
    grad = jnp.concatenate([dq_ref[0], dkv_ref[0]], axis=1)
    lane = lax.broadcasted_iota(jnp.int32, raw.shape, 1)
    turned, low = half_turn(grad * sin_ref[...], head_dim)
    dn = grad * cos_ref[...] + jnp.where(low, turned, -turned)
    r = lax.rsqrt(group_mean(raw * raw, head_dim) + EPSILON)
    u = dn * hgain_ref[...]
    mean = group_mean(raw * u, head_dim)
    draw = r * u - raw * (r * r * r * mean)
    out_ref[0] = jnp.where(lane < rot_cols, draw, grad).astype(BF16)
    gsum = jnp.sum(dn * raw * r, axis=0, keepdims=True)

    @pl.when(seq == 0)
    def _():
        gsum_ref[...] = gsum

    @pl.when(seq > 0)
    def _():
        gsum_ref[...] += gsum


def head_back(raw, dq, dkv, hgain, cos, sin, head_dim, rot_cols):
    seqs, rows, cols = raw.shape
    row_spec = lambda last: pl.BlockSpec((1, rows, last), lambda s: (s, 0, 0))
    flat = lambda shape: pl.BlockSpec(shape, lambda s: (0, 0))
    return pl.pallas_call(
        functools.partial(head_back_kernel, head_dim=head_dim, rot_cols=rot_cols),
        grid=(seqs,),
        in_specs=[
            row_spec(cols), row_spec(dq.shape[2]), row_spec(dkv.shape[2]), flat((1, cols)),
            flat((rows, cols)), flat((rows, cols)),
        ],
        out_specs=[row_spec(cols), flat((1, cols))],
        out_shape=[
            jax.ShapeDtypeStruct((seqs, rows, cols), BF16),
            jax.ShapeDtypeStruct((1, cols), F32),
        ],
        compiler_params=params(),
        cost_estimate=cost(seqs * rows * cols * cols * 8, seqs * rows * cols * 14),
        name="head_back",
    )(raw, dq, dkv, hgain, cos, sin)


def input_kernel(*refs, tp_count, qkv_w, step, chunk):
    place, tok_ref, dres_ref, gain_ref = refs[:4]
    refs = refs[4:]
    d_in, refs = refs[:tp_count], refs[tp_count:]
    w_in, refs = refs[: len(qkv_w.arrays)], refs[len(qkv_w.arrays) :]
    out_ref, gsum_ref, dall, w, lift, sems = refs
    seq = pl.program_id(0)
    tile = tok_ref.shape[1]
    width = tok_ref.shape[2]
    cols = d_in[0].shape[1]

    @pl.when(seq == 0)
    def _():
        moves = []
        for k in range(tp_count):
            col = lax.rem(place[2] + (tp_count - k), tp_count) * cols
            moves.append((d_in[k], dall.at[:, pl.ds(pl.multiple_of(col, cols), cols)]))
        moves += list(qkv_w.copies(place, w_in, w))
        for copy in fetch(moves, sems):
            copy.wait()

    base = pl.multiple_of(seq * tile, tile)

    def square(i, total):
        lanes = pl.ds(pl.multiple_of(i * step, step), step)
        x = tok_ref[0, :, lanes].astype(F32)
        return total + x * x

    total = lax.fori_loop(0, width // step, square, jnp.zeros((tile, step), F32))
    r = lax.rsqrt(jnp.sum(total, axis=-1, keepdims=True) / width + EPSILON)

    def outer(i, total):
        lanes = pl.ds(pl.multiple_of(i * step, step), step)
        x = tok_ref[0, :, lanes].astype(F32)
        grad = mm_t(dall[pl.ds(base, tile), :], w[lanes, :])
        gsum = jnp.sum(grad * x * r, axis=0, keepdims=True)

        @pl.when(seq == 0)
        def _():
            gsum_ref[:, lanes] = gsum

        @pl.when(seq > 0)
        def _():
            gsum_ref[:, lanes] += gsum

        u = grad * gain_ref[:, lanes]
        lift[:, lanes] = u
        return total + x * u

    total = lax.fori_loop(0, width // step, outer, jnp.zeros((tile, step), F32))
    pull = r * r * r * (jnp.sum(total, axis=-1, keepdims=True) / width)

    def finish(i, carry):
        lanes = pl.ds(pl.multiple_of(i * step, step), step)
        x = tok_ref[0, :, lanes].astype(F32)
        grad = dres_ref[0, :, lanes].astype(F32) + r * lift[:, lanes] - x * pull
        out_ref[0, :, lanes] = grad.astype(BF16)
        return carry

    lax.fori_loop(0, width // step, finish, 0)


def input_part(place, tokens, dres, gain, pieces, qkv_w):
    seqs, rows, width = tokens.shape
    inner = pieces[0].shape[1] * len(pieces)
    row_spec = lambda last: pl.BlockSpec((1, rows, last), lambda s, *_: (s, 0, 0))
    vec = pl.BlockSpec((1, width), lambda s, *_: (0, 0))
    arrays = list(pieces) + qkv_w.arrays
    return pl.pallas_call(
        functools.partial(input_kernel, tp_count=len(pieces), qkv_w=qkv_w, step=256, chunk=64),
        grid_spec=pltpu.PrefetchScalarGridSpec(
            num_scalar_prefetch=1,
            grid=(seqs,),
            in_specs=[row_spec(width), row_spec(width), vec] + [ANY] * len(arrays),
            out_specs=[row_spec(width), vec],
            scratch_shapes=[
                pltpu.VMEM((seqs * rows, inner), BF16),
                pltpu.VMEM((width, inner), BF16),
                pltpu.VMEM((rows, width), F32),
                pltpu.SemaphoreType.DMA((len(pieces) + len(qkv_w.listing),)),
            ],
        ),
        out_shape=[
            jax.ShapeDtypeStruct((seqs, rows, width), BF16),
            jax.ShapeDtypeStruct((1, width), F32),
        ],
        compiler_params=params(),
        cost_estimate=cost(2 * seqs * rows * width * inner, seqs * rows * width * 6),
        name="input_part",
    )(place, tokens, dres, gain, *arrays)


def weight_grad_kernel(place, *refs, count):
    keep_ref, give_ref = refs[-2:]
    step = pl.program_id(0)
    for i in range(count):
        grad = outer_sum(refs[2 * i][...], refs[2 * i + 1][...])

        @pl.when(step < 2)
        def _():
            keep_ref[0, i] = grad

        @pl.when(step >= 2)
        def _():
            give_ref[0, i] = grad.astype(BF16)


def weight_grad(place, pairs, cut_left, name):
    rows = pairs[0][0].shape[0]
    left_cols, right_cols = pairs[0][0].shape[1], pairs[0][1].shape[1]

    def piece(step, place):
        return place[0] ^ (2 * (step & 1) + (step >> 1))

    moving = lambda cols: pl.BlockSpec((rows, cols // 4), lambda m, place: (0, piece(m, place)))
    fixed = lambda cols: pl.BlockSpec((rows, cols), lambda m, place: (0, 0))
    if cut_left:
        specs = [moving(left_cols), fixed(right_cols)]
        shape = (left_cols // 4, right_cols)
    else:
        specs = [fixed(left_cols), moving(right_cols)]
        shape = (left_cols, right_cols // 4)
    count = len(pairs)
    block = (1, count) + shape
    return pl.pallas_call(
        functools.partial(weight_grad_kernel, count=count),
        grid_spec=pltpu.PrefetchScalarGridSpec(
            num_scalar_prefetch=1,
            grid=(4,),
            in_specs=specs * count,
            out_specs=[
                pl.BlockSpec(block, lambda m, place: (jnp.minimum(m, 1), 0, 0, 0)),
                pl.BlockSpec(block, lambda m, place: (jnp.maximum(m - 2, 0), 0, 0, 0)),
            ],
        ),
        out_shape=[
            jax.ShapeDtypeStruct((2,) + block[1:], F32),
            jax.ShapeDtypeStruct((2,) + block[1:], BF16),
        ],
        compiler_params=params(),
        cost_estimate=cost(2 * count * rows * left_cols * right_cols, count * rows * (left_cols + right_cols) * 2),
        name=name,
    )(place, *[array for pair in pairs for array in pair])


def settle(keep, give):
    total = keep + swap(give, "fsdp", 1).astype(F32)
    total = total[0] + swap(total[1].astype(BF16), "fsdp", 2).astype(F32)
    return cube_sum(total, "ctx")


def shards(
    tokens, attn_gain, w_query, key_matrix, value_matrix, query_gain, key_gain, w_out, ffn_gain,
    w_gate, w_up, w_down, prefix_len, out_grad,
):
    seqs, block_len, width = tokens.shape
    rows = seqs * block_len
    place = place_of()
    ctx_count = lax.axis_size("ctx")
    fsdp_count = lax.axis_size("fsdp")
    tp_count = lax.axis_size("tp")
    head_dim = query_gain.shape[0] * fsdp_count
    q_cols = w_query.shape[1]
    kv_cols = key_matrix.shape[1]
    heads = q_cols // head_dim
    own_ff = w_gate.shape[1]
    hidden_cols = own_ff * tp_count
    rot_cols = q_cols + kv_cols

    gains = lax.all_gather(
        jnp.concatenate([attn_gain, ffn_gain, query_gain, key_gain]), "fsdp", axis=0
    ).astype(F32)
    a, q = attn_gain.size, query_gain.size
    attn_gain32 = gains[:, :a].reshape(1, -1)
    ffn_gain32 = gains[:, a : 2 * a].reshape(1, -1)
    query_gain32 = gains[:, 2 * a : 2 * a + q].reshape(1, -1)
    key_gain32 = gains[:, 2 * a + q :].reshape(1, -1)
    hgain = jnp.concatenate(
        [query_gain32] * heads + [key_gain32] * (kv_cols // head_dim) + [jnp.ones((1, kv_cols), F32)], axis=1
    )
    query_pos = place[1] * block_len + jnp.arange(block_len, dtype=jnp.int32)
    cos_half, sin_half = rotary_tables(query_pos, head_dim)
    copies = 2 * (rot_cols + kv_cols) // head_dim
    cos = jnp.concatenate([cos_half] * copies, axis=1)
    sin = jnp.concatenate([sin_half] * copies, axis=1)

    w_qkv = jnp.concatenate([w_query, key_matrix, value_matrix], axis=1)
    near = jnp.stack([w_qkv, swap(w_qkv, "fsdp", 2)])
    far = swap(near, "fsdp", 1)
    own_qkv = jnp.stack([near[0], far[0], near[1], far[1]])

    gate_up = lax.all_gather(jnp.stack([w_gate, w_up]), ("fsdp", "tp"), axis=0)
    gate_w = gathered_columns(gate_up, (0,), fsdp_count, tp_count, w_gate.shape)
    up_w = gathered_columns(gate_up, (1,), fsdp_count, tp_count, w_up.shape)
    if ctx_count == 2:
        w_out_late = after(w_out, near)
        out_w = travelled_rows(w_out_late, tp_count)
        down_w = travelled_rows(after(w_down, out_w.arrays[0]), tp_count)
    else:
        out_down = lax.all_gather(jnp.stack([w_out, w_down]), ("fsdp", "tp"), axis=0)
        out_w = gathered_rows(out_down, (0,), fsdp_count, tp_count, w_out.shape)
        down_w = gathered_rows(out_down, (1,), fsdp_count, tp_count, w_down.shape)
    qkv_late = after(w_qkv, gate_up)
    qkv_all = lax.all_gather(qkv_late, ("fsdp", "tp"), axis=0)
    qkv_w = gathered_columns(qkv_all, (), fsdp_count, tp_count, w_qkv.shape)

    normed, raw, query_low, kv_low = project(
        place, tokens, attn_gain32, hgain, cos, sin, own_qkv, head_dim, q_cols, rot_cols
    )
    kv_all = cube(kv_low, "ctx")
    attended, lse = attend(place, prefix_len, query_low, kv_all, heads, head_dim)
    attended = attended.reshape(rows, q_cols)
    att = ring(attended, "tp")
    residual, ffn_in, dhidden = residual_part(
        place, tokens, out_grad, ffn_gain32, att, out_w, down_w, hidden_cols
    )
    if ctx_count == 2:
        own_out_w = out_w
    else:
        own_out = lax.all_gather(w_out, "fsdp", axis=0)
        own_out_w = Pieces(
            [own_out],
            [(0, (f,), lambda p, f=f: (p[2] * w_out.shape[0], f * w_out.shape[1], True)) for f in range(fsdp_count)],
            w_out.shape,
            w_out.shape[0],
        )
    layer_low, dres_low, hidden, dgate, dup, dattended, gsum_ffn = ffn(
        place, residual, ffn_in, dhidden, out_grad, ffn_gain32, gate_w, up_w, down_w, own_out_w, own_ff, q_cols
    )
    dquery, dkv = attend_back(place, prefix_len, query_low, kv_all, dattended, lse, heads, head_dim)
    flat = lambda value: value.reshape(rows, -1)
    down_out = weight_grad(
        place, [(flat(hidden), flat(out_grad)), (attended, flat(dres_low))], False, "grad_down_out"
    )
    gate_up_grad = weight_grad(
        place, [(flat(ffn_in), flat(dgate)), (flat(ffn_in), flat(dup))], True, "grad_gate_up"
    )
    owned = cube_own(dkv, "ctx")
    dqkv, gsum_head = head_back(raw, dquery, owned, hgain, cos, sin, head_dim, rot_cols)
    dqkv = flat(dqkv)
    pieces = ring(dqkv, "tp")
    qkv_grad = weight_grad(place, [(flat(normed), dqkv)], True, "grad_qkv")
    input_grad, gsum_attn = input_part(place, tokens, dres_low, attn_gain32, pieces, qkv_w)

    down_out = settle(*down_out)
    gate_up_grad = settle(*gate_up_grad)
    qkv_grad = settle(*qkv_grad)[0]
    head_sum = gsum_head.reshape(-1, head_dim)
    query_sum = jnp.sum(head_sum[:heads], axis=0)
    key_sum = jnp.sum(head_sum[heads : heads + kv_cols // head_dim], axis=0)
    head_gains = jnp.concatenate([query_sum, key_sum])[None]
    head_gains = lax.psum(head_gains, "tp")[0]
    gain_grads = jnp.concatenate([gsum_attn[0], gsum_ffn[0], head_gains])
    gain_grads = cube_sum(cube_sum(gain_grads, "fsdp"), "ctx")
    member = lax.axis_index("fsdp")

    def share(low, high):
        size = (high - low) // fsdp_count
        return lax.dynamic_slice_in_dim(gain_grads[low:high], member * size, size, 0)

    ends = [0, width, 2 * width, 2 * width + head_dim, 2 * width + 2 * head_dim]
    return (
        layer_low,
        input_grad,
        share(ends[0], ends[1]),
        qkv_grad[:, :q_cols],
        qkv_grad[:, q_cols : q_cols + kv_cols],
        qkv_grad[:, q_cols + kv_cols :],
        share(ends[2], ends[3]),
        share(ends[3], ends[4]),
        down_out[1],
        share(ends[1], ends[2]),
        gate_up_grad[0],
        gate_up_grad[1],
        down_out[0],
    )


def solution(mesh):
    columns = P("fsdp", "tp")
    across = P("tp", "fsdp")
    vector = P("fsdp")
    data = P("fsdp", "ctx", None)
    return jax.shard_map(
        shards,
        mesh=mesh,
        in_specs=(
            data, vector, columns, columns, columns, vector, vector, across, vector,
            columns, columns, across, vector, data,
        ),
        out_specs=(
            data, data, vector, columns, columns, columns, vector, vector, across, vector,
            columns, columns, across,
        ),
        check_vma=False,
    )
```

```python
import functools

import jax
import jax.numpy as jnp
from jax import lax
from jax.experimental import pallas as pl
from jax.experimental.pallas import tpu as pltpu
from jax.sharding import PartitionSpec as P

EPSILON = 1e-06
NEGATIVE = -1e30
ROPE_BASE = 10000.0
F32 = jnp.float32
BF16 = jnp.bfloat16
VMEM_LIMIT = 60 * 1024 * 1024
SPARE = 16
ANY = pl.BlockSpec(memory_space=pl.ANY)


def dot(left, right, dims, precision=None):
    return lax.dot_general(
        left, right, (dims, ((), ())), precision=precision, preferred_element_type=F32
    )


def mm(left, right):
    return dot(left, right, ((1,), (0,)))


def mm_t(left, right):
    return dot(left, right, ((1,), (1,)))


def outer_sum(left, right):
    return dot(left, right, ((0,), (0,)))


def params():
    return pltpu.CompilerParams(vmem_limit_bytes=VMEM_LIMIT)


def cost(flops, nbytes, exps=0, part=1e-3):
    return pl.CostEstimate(
        flops=int(flops * part), bytes_accessed=int(nbytes * part), transcendentals=int(exps * part)
    )


def rotary_tables(positions, head_dim):
    inverse_freq = ROPE_BASE ** (-jnp.arange(0, head_dim, 2).astype(F32) / head_dim)
    angles = positions.astype(F32)[:, None] * inverse_freq[None, :]
    return (jnp.cos(angles), jnp.sin(angles))


def swap(value, axis, bit):
    return lax.ppermute(value, axis, [(i, i ^ bit) for i in range(lax.axis_size(axis))])


def bits_of(size):
    return [1 << b for b in range(size.bit_length() - 1)]


def ring(value, axis):
    size = lax.axis_size(axis)
    pieces = [value]
    for _ in range(size - 1):
        pieces.append(lax.ppermute(pieces[-1], axis, [(i, (i + 1) % size) for i in range(size)]))
    return pieces


def send_all(value, axis):
    size = lax.axis_size(axis)
    return [value] + [
        lax.ppermute(value, axis, [(i, (i + k) % size) for i in range(size)]) for k in range(1, size)
    ]


def paired_sum(pieces):
    while len(pieces) > 1:
        half = len(pieces) // 2
        pieces = [pieces[i] + pieces[i + half] for i in range(half)]
    return pieces[0]


def in_order(stack, axis):
    me = lax.axis_index(axis)
    size = stack.shape[0]
    rows = []
    for member in range(size):
        rows.append(sum(jnp.where((me ^ m) == member, stack[m : m + 1], 0) for m in range(size)))
    return jnp.concatenate(rows, axis=0)


def cube(value, axis):
    stacked = value[None]
    for bit in bits_of(lax.axis_size(axis)):
        stacked = jnp.concatenate([stacked, swap(stacked, axis, bit)], axis=0)
    return stacked


def cube_sum(value, axis):
    for bit in bits_of(lax.axis_size(axis)):
        low = value.astype(BF16)
        value = low.astype(F32) + swap(low, axis, bit).astype(F32)
    return value


def cube_own(value, axis):
    for bit in reversed(bits_of(lax.axis_size(axis))):
        half = value.shape[0] // 2
        value = value[:half] + swap(value[half:].astype(BF16), axis, bit).astype(F32)
    return value[0]


def launch(deps, kernel, *, grid_spec, **options):
    deps = list(deps)

    def run(*operands):
        count = len(operands)

        def body(*refs):
            return kernel(*refs[:count], *refs[count + len(deps) :])

        spec = pltpu.PrefetchScalarGridSpec(
            num_scalar_prefetch=grid_spec.num_scalar_prefetch,
            grid=grid_spec.grid,
            in_specs=list(grid_spec.in_specs) + [ANY] * len(deps),
            out_specs=grid_spec.out_specs,
            scratch_shapes=grid_spec.scratch_shapes,
        )
        return pl.pallas_call(body, grid_spec=spec, **options)(*operands, *deps)

    return run


def gate_kernel(value_ref, out_ref):
    pass


def gate(value, deps):
    return launch(
        deps,
        gate_kernel,
        grid_spec=pltpu.PrefetchScalarGridSpec(num_scalar_prefetch=0, grid=(1,), in_specs=[ANY], out_specs=ANY),
        out_shape=jax.ShapeDtypeStruct(value.shape, value.dtype),
        input_output_aliases={0: 0},
        compiler_params=params(),
        cost_estimate=cost(1, 1),
        name="gate",
    )(value)


def place_of():
    return jnp.stack(
        [lax.axis_index("fsdp"), lax.axis_index("ctx"), lax.axis_index("tp")]
    ).astype(jnp.int32)


class Pieces:
    def __init__(self, arrays, listing, shape, dims):
        self.arrays = arrays
        self.listing = listing
        self.shape = shape
        self.dims = dims

    def copies(self, place, refs, target, only_own=False):
        for number, index, where in self.listing:
            spot = where(place)
            if spot is None:
                continue
            row, col, own = spot
            if only_own and not own:
                continue
            rows, cols = self.shape
            if only_own:
                row = row - place[2] * self.dims
            yield (
                refs[number].at[index],
                target.at[pl.ds(pl.multiple_of(row, rows), rows), pl.ds(pl.multiple_of(col, cols), cols)],
            )


def gathered_columns(stack, lead, fsdp_count, tp_count, shape):
    rows, cols = shape
    listing = []
    for f in range(fsdp_count):
        for t in range(tp_count):
            listing.append(
                (0, (f * tp_count + t,) + lead, lambda place, f=f, t=t: (f * rows, t * cols, False))
            )
    return Pieces([stack], listing, shape, rows)


def gathered_rows(stack, lead, fsdp_count, tp_count, shape):
    rows, cols = shape
    listing = []
    for f in range(fsdp_count):
        for t in range(tp_count):
            listing.append(
                (0, (f * tp_count + t,) + lead, lambda place, f=f, t=t: (t * rows, f * cols, False))
            )
    return Pieces([stack], listing, shape, rows)


def travelled_rows(quarters, which, tp_count):
    rows, cols = quarters[0].shape[2:]
    arrays = list(quarters) + [swap(array, "fsdp", 1) for array in quarters]
    weights = []
    for weight in which:
        listing = []
        for number in range(8):
            for k in range(tp_count):

                def where(place, number=number, k=k):
                    tp = lax.rem(place[2] + (tp_count - k), tp_count)
                    row = tp * (2 * rows) + (place[1] ^ (number // 2 % 2)) * rows
                    col = (place[0] ^ (2 * (number % 2) + number // 4)) * cols
                    return (row, col, False)

                listing.append((number, (k, weight), where))
        weights.append(Pieces(arrays, listing, (rows, cols), 2 * rows))
    return weights


def fetch(copies, sems, base=0):
    started = [pltpu.make_async_copy(src, dst, sems.at[base + i]) for i, (src, dst) in enumerate(copies)]
    for copy in started:
        copy.start()
    return started


def group_mean(values, head_dim):
    width = values.shape[1]
    row = lax.broadcasted_iota(jnp.int32, (width, width), 0) // head_dim
    col = lax.broadcasted_iota(jnp.int32, (width, width), 1) // head_dim
    ones = jnp.where(row == col, 1.0 / head_dim, 0.0).astype(BF16)
    high = values.astype(BF16)
    rest = values - high.astype(F32)
    mid = rest.astype(BF16)
    low = (rest - mid.astype(F32)).astype(BF16)
    return mm(high, ones) + mm(mid, ones) + mm(low, ones)


def half_turn(values, head_dim):
    width = values.shape[1]
    half = head_dim // 2
    lane = lax.broadcasted_iota(jnp.int32, values.shape, 1)
    low = (lane & (head_dim - 1)) < half
    return jnp.where(low, pltpu.roll(values, width - half, 1), pltpu.roll(values, half, 1)), low


def project_kernel(
    place, tok_ref, gain_ref, hgain_ref, cos_ref, sin_ref, w_in, normed_ref, raw_ref, q_ref, kv_ref,
    w_ref, sems, *, head_dim, q_cols, rot_cols, chunk,
):
    shard = w_ref.shape[0] // w_in.shape[0]
    tile = tok_ref.shape[1]

    @pl.when(pl.program_id(0) == 0)
    def _():
        moves = []
        for m in range(w_in.shape[0]):
            row = pl.multiple_of((place[0] ^ m) * shard, shard)
            moves.append((w_in.at[m, pl.ds(0, shard)], w_ref.at[pl.ds(row, shard), :]))
        for copy in fetch(moves, sems):
            copy.wait()

    def norm(i, carry):
        rows = pl.ds(pl.multiple_of(i * chunk, chunk), chunk)
        x = tok_ref[0, rows, :].astype(F32)
        r = lax.rsqrt(jnp.mean(x * x, axis=-1, keepdims=True) + EPSILON)
        normed_ref[0, rows, :] = (x * r * gain_ref[...]).astype(BF16)
        return carry

    lax.fori_loop(0, tile // chunk, norm, 0)
    raw = mm(normed_ref[0], w_ref[...])
    raw_ref[0] = raw
    scale = lax.rsqrt(group_mean(raw * raw, head_dim) + EPSILON)
    n = raw * scale * hgain_ref[...]
    turned, low = half_turn(n, head_dim)
    rot = n * cos_ref[...] + jnp.where(low, -turned, turned) * sin_ref[...]
    lane = lax.broadcasted_iota(jnp.int32, raw.shape, 1)
    out = jnp.where(lane < rot_cols, rot, raw).astype(BF16)
    q_ref[0] = out[:, :q_cols]
    kv_ref[0] = out[:, q_cols:]


def project(place, tokens, gain, hgain, cos, sin, w_in, head_dim, q_cols, rot_cols, deps):
    seqs, rows, width = tokens.shape
    cols = w_in.shape[2]
    row_spec = lambda last: pl.BlockSpec((1, rows, last), lambda s, *_: (s, 0, 0))
    flat = lambda shape: pl.BlockSpec(shape, lambda s, *_: (0,) * len(shape))
    return launch(
        deps,
        functools.partial(
            project_kernel, head_dim=head_dim, q_cols=q_cols, rot_cols=rot_cols, chunk=64
        ),
        grid_spec=pltpu.PrefetchScalarGridSpec(
            num_scalar_prefetch=1,
            grid=(seqs,),
            in_specs=[
                row_spec(width), flat((1, width)), flat((1, cols)), flat((rows, cols)), flat((rows, cols)), ANY,
            ],
            out_specs=[row_spec(width), row_spec(cols), row_spec(q_cols), row_spec(cols - q_cols)],
            scratch_shapes=[
                pltpu.VMEM((width, cols), BF16), pltpu.SemaphoreType.DMA((w_in.shape[0],)),
            ],
        ),
        out_shape=[
            jax.ShapeDtypeStruct((seqs, rows, width), BF16),
            jax.ShapeDtypeStruct((seqs, rows, cols), F32),
            jax.ShapeDtypeStruct((seqs, rows, q_cols), BF16),
            jax.ShapeDtypeStruct((seqs, rows, cols - q_cols), BF16),
        ],
        compiler_params=params(),
        cost_estimate=cost(2 * seqs * rows * width * cols, seqs * rows * width * 4),
        name="project",
    )(place, tokens, gain, hgain, cos, sin, w_in)


def allowed_t(place, prefix, part, key_count, block, tile):
    j = lax.broadcasted_iota(jnp.int32, (key_count, tile), 0)
    key_pos = (place ^ (j // block)) * block + (j & (block - 1))
    query_pos = place * block + part * tile + lax.broadcasted_iota(jnp.int32, (key_count, tile), 1)
    return (key_pos <= query_pos) | (key_pos < prefix)


def attend_kernel(
    place, prefix, q_ref, kv_ref, out_ref, lse_ref, *, seq, heads, head_dim, tile, block
):
    part = pl.program_id(0)
    pairs = kv_ref[:, 0].reshape(-1, 2 * head_dim)
    keys = pairs[:, :head_dim]
    values = pairs[:, head_dim:]
    allowed = allowed_t(place[1], prefix[seq], part, pairs.shape[0], block, tile)
    for head in range(heads):
        lanes = slice(head * head_dim, (head + 1) * head_dim)
        scores = mm_t(keys, q_ref[0, :, lanes]) * (head_dim ** (-0.5))
        scores = jnp.where(allowed, scores, NEGATIVE)
        top = jnp.max(scores, axis=0, keepdims=True)
        weight = jnp.exp(scores - top)
        total = jnp.sum(weight, axis=0, keepdims=True)
        probs = weight * (1.0 / total)
        out_ref[0, :, lanes] = outer_sum(probs.astype(BF16), values).astype(BF16)
        lse_ref[0, head : head + 1, :] = top + jnp.log(total)


def attention_specs(seq, rows, q_cols, heads, kv_all):
    tile = min(256, rows)
    blocks, _, block, pair = kv_all.shape
    row_block = pl.BlockSpec((1, tile, q_cols), lambda i, *_: (seq, i, 0))
    own_block = pl.BlockSpec((1, tile, q_cols), lambda i, *_: (0, i, 0))
    key_block = pl.BlockSpec((blocks, 1, block, pair), lambda i, *_: (0, seq, 0, 0))
    stat_block = pl.BlockSpec((1, heads, tile), lambda i, *_: (0, 0, i))
    return tile, blocks, block, pair, row_block, own_block, key_block, stat_block


def attend(place, prefix, query, kv_all, heads, head_dim, seq, deps):
    _, rows, q_cols = query.shape
    tile, blocks, block, pair, row_block, own_block, key_block, stat_block = attention_specs(
        seq, rows, q_cols, heads, kv_all
    )
    elements = rows * blocks * block * heads
    return launch(
        deps,
        functools.partial(
            attend_kernel, seq=seq, heads=heads, head_dim=head_dim, tile=tile, block=block
        ),
        grid_spec=pltpu.PrefetchScalarGridSpec(
            num_scalar_prefetch=2,
            grid=(rows // tile,),
            in_specs=[row_block, key_block],
            out_specs=[own_block, stat_block],
        ),
        out_shape=[
            jax.ShapeDtypeStruct((1, rows, q_cols), BF16),
            jax.ShapeDtypeStruct((1, heads, rows), F32),
        ],
        compiler_params=params(),
        cost_estimate=cost(elements * 1024, query.size * 4, elements),
        name="attend",
    )(place, prefix, query, kv_all)


def attend_back_kernel(
    place, prefix, q_ref, kv_ref, d_ref, lse_ref, dq_ref, dkv_ref, *, seq, heads, head_dim, tile, block
):
    part = pl.program_id(0)
    scale = head_dim ** (-0.5)
    pairs = kv_ref[:, 0].reshape(-1, 2 * head_dim)
    keys = pairs[:, :head_dim]
    values = pairs[:, head_dim:]
    allowed = allowed_t(place[1], prefix[seq], part, pairs.shape[0], block, tile)
    dkeys = None
    dvalues = None
    for head in range(heads):
        lanes = slice(head * head_dim, (head + 1) * head_dim)
        query = q_ref[0, :, lanes]
        dout = d_ref[0, :, lanes]
        scores = mm_t(keys, query) * scale
        probs = jnp.where(allowed, jnp.exp(scores - lse_ref[0, head : head + 1, :]), 0.0)
        weighted = probs * mm_t(values, dout)
        delta = jnp.sum(weighted, axis=0, keepdims=True)
        dscore = (weighted - probs * delta).astype(BF16)
        dv = mm(probs.astype(BF16), dout)
        dk = mm(dscore, query)
        dkeys = dk if dkeys is None else dkeys + dk
        dvalues = dv if dvalues is None else dvalues + dv
        dq_ref[0, :, lanes] = outer_sum(dscore, keys) * scale
    both = jnp.concatenate([dkeys * scale, dvalues], axis=1).reshape(dkv_ref.shape[0], block, -1)

    @pl.when(part == 0)
    def _():
        dkv_ref[:, 0] = both

    @pl.when(part > 0)
    def _():
        dkv_ref[:, 0] += both


def attend_back(place, prefix, query, kv_all, dout, lse, heads, head_dim, seq, deps):
    _, rows, q_cols = query.shape
    tile, blocks, block, pair, row_block, own_block, key_block, stat_block = attention_specs(
        seq, rows, q_cols, heads, kv_all
    )
    elements = rows * blocks * block * heads
    return launch(
        deps,
        functools.partial(
            attend_back_kernel, seq=seq, heads=heads, head_dim=head_dim, tile=tile, block=block
        ),
        grid_spec=pltpu.PrefetchScalarGridSpec(
            num_scalar_prefetch=2,
            grid=(rows // tile,),
            in_specs=[row_block, key_block, row_block, stat_block],
            out_specs=[own_block, pl.BlockSpec((blocks, 1, block, pair), lambda i, *_: (0, 0, 0, 0))],
        ),
        out_shape=[
            jax.ShapeDtypeStruct((1, rows, q_cols), F32),
            jax.ShapeDtypeStruct((blocks, 1, block, pair), F32),
        ],
        compiler_params=params(),
        cost_estimate=cost(elements * 2560, query.size * 8, elements),
        name="attend_back",
    )(place, prefix, query, kv_all, dout, lse)


def layer_kernel(*refs, seq, tp_count, gate_w, down_w, out_w, up_w, out_count, step, own_cols):
    place, gain_ref, tok_in, og_in = refs[:4]
    refs = refs[4:]
    att_in, refs = refs[:tp_count], refs[tp_count:]
    gate_in, refs = refs[: len(gate_w.arrays)], refs[len(gate_w.arrays) :]
    down_in, refs = refs[: len(down_w.arrays)], refs[len(down_w.arrays) :]
    out_in = down_in
    outs, refs = refs[-out_count - 22 :][: out_count + 1], refs[-21:]
    token_ref = outs[-1]
    lay_out, dres_out, fin_out, hid_out, dgu_out, datt_out = outs[:-1]
    (
        tok, og, att, wo, wg, wu, wd, res, fin, hid, dgate, dup, lift, lay, dres, own_hid, own_dgu, datt,
        sems, more, final,
    ) = refs
    tile, width = tok.shape
    ff = wd.shape[0]
    cols = att_in[0].shape[1]

    moves = [(tok_in.at[seq], tok)]
    for k in range(tp_count):
        col = lax.rem(place[2] + (tp_count - k), tp_count) * cols
        moves.append((att_in[k], att.at[:, pl.ds(pl.multiple_of(col, cols), cols)]))
    moves += list(out_w.copies(place, out_in, wo))
    first = fetch(moves, sems)
    base = len(first)
    second = fetch(list(gate_w.copies(place, gate_in, wg)) + list(up_w.copies(place, gate_in, wu)), sems, base)
    base += len(second)
    third = fetch([(og_in.at[seq], og)] + list(down_w.copies(place, down_in, wd)), sems, base)
    for copy in first:
        copy.wait()

    def lanes_of(i):
        return pl.ds(pl.multiple_of(i * step, step), step)

    def out_part(i, total):
        lanes = lanes_of(i)
        row = tok[:, lanes].astype(F32) + mm(att[...], wo[:, lanes])
        res[:, lanes] = row
        return total + row * row

    total = lax.fori_loop(0, width // step, out_part, jnp.zeros((tile, step), F32))
    r = lax.rsqrt(jnp.sum(total, axis=-1, keepdims=True) / width + EPSILON)

    def norm(i, carry):
        lanes = lanes_of(i)
        fin[:, lanes] = (res[:, lanes] * r * gain_ref[:, lanes]).astype(BF16)
        return carry

    lax.fori_loop(0, width // step, norm, 0)
    leave_fin = pltpu.make_async_copy(fin, fin_out.at[seq], final.at[0])
    leave_fin.start()
    for copy in second + third:
        copy.wait()

    def inner(i, carry):
        lanes = lanes_of(i)
        gate = mm(fin[...], wg[:, lanes])
        up = mm(fin[...], wu[:, lanes])
        grad = mm_t(og[...], wd[lanes, :])
        sig = 1.0 / (1.0 + jnp.exp(-gate))
        silu = gate * sig
        hid[:, lanes] = (silu * up).astype(BF16)
        dgate[:, lanes] = (grad * up * sig * (1.0 + gate * (1.0 - sig))).astype(BF16)
        dup[:, lanes] = (grad * silu).astype(BF16)
        return carry

    lax.fori_loop(0, ff // step, inner, 0)
    own = pl.ds(pl.multiple_of(place[2] * own_cols, own_cols), own_cols)
    own_hid[...] = hid[:, own]
    own_dgu[:, :own_cols] = dgate[:, own]
    own_dgu[:, own_cols:] = dup[:, own]
    leave_own = [
        pltpu.make_async_copy(own_hid, hid_out.at[seq], final.at[1]),
        pltpu.make_async_copy(own_dgu, dgu_out.at[seq], final.at[2]),
    ]
    for copy in leave_own:
        copy.start()

    def outer(i, total):
        lanes = lanes_of(i)
        row = res[:, lanes]
        lay[:, lanes] = (row + mm(hid[...], wd[:, lanes])).astype(BF16)
        grad = mm_t(dgate[...], wg[lanes, :]) + mm_t(dup[...], wu[lanes, :])
        u = grad * gain_ref[:, lanes]
        lift[:, lanes] = u
        return total + row * u

    token_ref[...] = jnp.zeros_like(token_ref)
    total = lax.fori_loop(0, width // step, outer, jnp.zeros((tile, step), F32))
    leave_lay = pltpu.make_async_copy(lay, lay_out.at[seq], final.at[3])
    leave_lay.start()
    pull = r * r * r * (jnp.sum(total, axis=-1, keepdims=True) / width)

    def finish(i, carry):
        lanes = lanes_of(i)
        grad = og[:, lanes].astype(F32) + r * lift[:, lanes] - res[:, lanes] * pull
        dres[:, lanes] = grad.astype(BF16)
        return carry

    lax.fori_loop(0, width // step, finish, 0)
    leave_dres = pltpu.make_async_copy(dres, dres_out.at[seq], final.at[4])
    leave_dres.start()
    own_rows = pl.ds(pl.multiple_of(place[2] * cols, cols), cols)
    datt[...] = mm_t(dres[...], wo[own_rows, :]).astype(BF16)
    leave_datt = pltpu.make_async_copy(datt, datt_out.at[seq], final.at[5])
    leave_datt.start()
    for copy in leave_own + [leave_fin, leave_lay, leave_dres, leave_datt]:
        copy.wait()


def layer(place, tokens, out_grad, gain, att, gate_w, up_w, down_w, out_w, own_cols, seq, before, deps):
    seqs, rows, width = tokens.shape
    q_cols = att[0].shape[1]
    inner = q_cols * len(att)
    ff = own_cols * len(att)
    arrays = list(att) + gate_w.arrays + down_w.arrays
    count = 2 + len(att) + 2 * len(gate_w.listing) + len(down_w.listing) + len(out_w.listing)
    vec = pl.BlockSpec((1, width), lambda *_: (0, 0))
    outs = [
        jax.ShapeDtypeStruct((seqs, rows, last), BF16)
        for last in (width, width, width, own_cols, 2 * own_cols, q_cols)
    ]
    prior = list(before) if before is not None else []
    start = 4 + len(arrays)
    return launch(
        deps,
        functools.partial(
            layer_kernel, seq=seq, tp_count=len(att), gate_w=gate_w, up_w=up_w, down_w=down_w, out_w=out_w,
            out_count=len(outs), step=512, own_cols=own_cols,
        ),
        grid_spec=pltpu.PrefetchScalarGridSpec(
            num_scalar_prefetch=1,
            grid=(1,),
            in_specs=[vec, ANY, ANY] + [ANY] * (len(arrays) + len(prior)),
            out_specs=[ANY] * len(outs) + [pl.BlockSpec((8, 128), lambda *_: (0, 0))],
            scratch_shapes=[
                pltpu.VMEM((rows, width), BF16),
                pltpu.VMEM((rows, width), BF16),
                pltpu.VMEM((rows, inner), BF16),
                pltpu.VMEM((inner, width), BF16),
                pltpu.VMEM((width, ff), BF16),
                pltpu.VMEM((width, ff), BF16),
                pltpu.VMEM((ff, width), BF16),
                pltpu.VMEM((rows, width), F32),
                pltpu.VMEM((rows, width), BF16),
                pltpu.VMEM((rows, ff), BF16),
                pltpu.VMEM((rows, ff), BF16),
                pltpu.VMEM((rows, ff), BF16),
                pltpu.VMEM((rows, width), F32),
                pltpu.VMEM((rows, width), BF16),
                pltpu.VMEM((rows, width), BF16),
                pltpu.VMEM((rows, own_cols), BF16),
                pltpu.VMEM((rows, 2 * own_cols), BF16),
                pltpu.VMEM((rows, q_cols), BF16),
                pltpu.SemaphoreType.DMA((count,)),
                pltpu.SemaphoreType.DMA((1,)),
                pltpu.SemaphoreType.DMA((6,)),
            ],
        ),
        out_shape=outs + [jax.ShapeDtypeStruct((8, 128), F32)],
        input_output_aliases={start + i: i for i in range(len(prior))},
        compiler_params=params(),
        cost_estimate=cost(2 * rows * width * (6 * ff + inner + q_cols), rows * width * 12 + 8 * width * ff),
        name="layer",
    )(place, gain, tokens, out_grad, *arrays, *prior)


def head_back_kernel(
    raw_ref, dq_ref, dkv_ref, hgain_ref, cos_ref, sin_ref, out_ref, gsum_ref, *, head_dim, rot_cols
):
    raw = raw_ref[0]
    grad = jnp.concatenate([dq_ref[0], dkv_ref[0]], axis=1)
    lane = lax.broadcasted_iota(jnp.int32, raw.shape, 1)
    turned, low = half_turn(grad * sin_ref[...], head_dim)
    dn = grad * cos_ref[...] + jnp.where(low, turned, -turned)
    r = lax.rsqrt(group_mean(raw * raw, head_dim) + EPSILON)
    u = dn * hgain_ref[...]
    mean = group_mean(raw * u, head_dim)
    draw = r * u - raw * (r * r * r * mean)
    out_ref[...] = jnp.where(lane < rot_cols, draw, grad).astype(BF16)
    gsum_ref[...] = jnp.broadcast_to(jnp.sum(dn * raw * r, axis=0, keepdims=True), gsum_ref.shape)


def head_back(raw, dq, dkv, hgain, cos, sin, head_dim, rot_cols, seq, deps):
    _, rows, cols = raw.shape
    row_spec = lambda last, at: pl.BlockSpec((1, rows, last), lambda i: (at, 0, 0))
    flat = lambda shape: pl.BlockSpec(shape, lambda i: (0, 0))
    return launch(
        deps,
        functools.partial(head_back_kernel, head_dim=head_dim, rot_cols=rot_cols),
        grid_spec=pltpu.PrefetchScalarGridSpec(
            num_scalar_prefetch=0,
            grid=(1,),
            in_specs=[
                row_spec(cols, seq), row_spec(dq.shape[2], 0), row_spec(dkv.shape[2], 0), flat((1, cols)),
                flat((rows, cols)), flat((rows, cols)),
            ],
            out_specs=[flat((rows, cols)), flat((SPARE, cols))],
        ),
        out_shape=[jax.ShapeDtypeStruct((rows, cols), BF16), jax.ShapeDtypeStruct((SPARE, cols), F32)],
        compiler_params=params(),
        cost_estimate=cost(rows * cols * cols * 12, rows * cols * 14),
        name="head_back",
    )(raw, dq, dkv, hgain, cos, sin)


def input_kernel(*refs, tp_count, qkv_w, step):
    place, tok_ref, dres_ref, gain_ref = refs[:4]
    refs = refs[4:]
    d_in, refs = refs[:tp_count], refs[tp_count:]
    w_in, refs = refs[: len(qkv_w.arrays)], refs[len(qkv_w.arrays) :]
    out_ref, token_ref, dall, w, lift, sems = refs[-6:]
    tile, width = lift.shape
    cols = d_in[0].shape[1]
    moves = []
    for k in range(tp_count):
        col = lax.rem(place[2] + (tp_count - k), tp_count) * cols
        moves.append((d_in[k], dall.at[:, pl.ds(pl.multiple_of(col, cols), cols)]))
    moves += list(qkv_w.copies(place, w_in, w))
    started = fetch(moves, sems)

    def lanes_of(i):
        return pl.ds(pl.multiple_of(i * step, step), step)

    token_ref[...] = jnp.zeros_like(token_ref)

    def square(i, total):
        x = tok_ref[0, :, lanes_of(i)].astype(F32)
        return total + x * x

    total = lax.fori_loop(0, width // step, square, jnp.zeros((tile, step), F32))
    r = lax.rsqrt(jnp.sum(total, axis=-1, keepdims=True) / width + EPSILON)
    for copy in started:
        copy.wait()

    def outer(i, total):
        lanes = lanes_of(i)
        x = tok_ref[0, :, lanes].astype(F32)
        grad = mm_t(dall[...], w[lanes, :])
        u = grad * gain_ref[:, lanes]
        lift[:, lanes] = u
        return total + x * u

    total = lax.fori_loop(0, width // step, outer, jnp.zeros((tile, step), F32))
    pull = r * r * r * (jnp.sum(total, axis=-1, keepdims=True) / width)

    def finish(i, carry):
        lanes = lanes_of(i)
        x = tok_ref[0, :, lanes].astype(F32)
        grad = dres_ref[0, :, lanes].astype(F32) + r * lift[:, lanes] - x * pull
        out_ref[0, :, lanes] = grad.astype(BF16)
        return carry

    lax.fori_loop(0, width // step, finish, 0)


def input_part(place, tokens, dres, gain, pieces, qkv_w, seq, before, deps):
    seqs, rows, width = tokens.shape
    inner = pieces[0].shape[1] * len(pieces)
    row_spec = pl.BlockSpec((1, rows, width), lambda *_: (seq, 0, 0))
    vec = pl.BlockSpec((1, width), lambda *_: (0, 0))
    arrays = list(pieces) + qkv_w.arrays
    prior = [] if before is None else [before]
    return launch(
        deps,
        functools.partial(input_kernel, tp_count=len(pieces), qkv_w=qkv_w, step=512),
        grid_spec=pltpu.PrefetchScalarGridSpec(
            num_scalar_prefetch=1,
            grid=(1,),
            in_specs=[row_spec, row_spec, vec] + [ANY] * (len(arrays) + len(prior)),
            out_specs=[row_spec, pl.BlockSpec((8, 128), lambda *_: (0, 0))],
            scratch_shapes=[
                pltpu.VMEM((rows, inner), BF16),
                pltpu.VMEM((width, inner), BF16),
                pltpu.VMEM((rows, width), F32),
                pltpu.SemaphoreType.DMA((len(pieces) + len(qkv_w.listing),)),
            ],
        ),
        out_shape=[
            jax.ShapeDtypeStruct((seqs, rows, width), BF16),
            jax.ShapeDtypeStruct((8, 128), F32),
        ],
        input_output_aliases={4 + len(arrays): 0} if prior else {},
        compiler_params=params(),
        cost_estimate=cost(2 * rows * width * inner, rows * width * 6 + width * inner * 2),
        name="input_part",
    )(place, tokens, dres, gain, *arrays, *prior)


def weight_grad_kernel(place, *refs, count, tails):
    keep_ref, give_ref = refs[-2:]
    step = pl.program_id(0)
    for i in range(count):
        grad = outer_sum(refs[2 * i][...], refs[2 * i + 1][...])
        if tails:
            grad = jnp.concatenate([grad, sum(ref[...] for ref in refs[2 * count : -2])], axis=0)

        @pl.when(step < 2)
        def _():
            keep_ref[0, i] = grad

        @pl.when(step >= 2)
        def _():
            give_ref[0, i] = grad.astype(BF16)


def weight_grad(place, pairs, cut_left, name, deps, tails=()):
    rows = pairs[0][0].shape[0]
    left_cols, right_cols = pairs[0][0].shape[1], pairs[0][1].shape[1]

    def piece(step, place):
        return place[0] ^ (2 * (step & 1) + (step >> 1))

    moving = lambda cols: pl.BlockSpec((rows, cols // 4), lambda m, place: (0, piece(m, place)))
    fixed = lambda cols: pl.BlockSpec((rows, cols), lambda m, place: (0, 0))
    if cut_left:
        specs = [moving(left_cols), fixed(right_cols)]
        shape = (left_cols // 4 + (SPARE if tails else 0), right_cols)
    else:
        specs = [fixed(left_cols), moving(right_cols)]
        shape = (left_cols, right_cols // 4)
    count = len(pairs)
    block = (1, count) + shape
    return launch(
        deps,
        functools.partial(weight_grad_kernel, count=count, tails=len(tails)),
        grid_spec=pltpu.PrefetchScalarGridSpec(
            num_scalar_prefetch=1,
            grid=(4,),
            in_specs=specs * count + [pl.BlockSpec(tail.shape, lambda m, place: (0, 0)) for tail in tails],
            out_specs=[
                pl.BlockSpec(block, lambda m, place: (jnp.minimum(m, 1), 0, 0, 0)),
                pl.BlockSpec(block, lambda m, place: (jnp.maximum(m - 2, 0), 0, 0, 0)),
            ],
        ),
        out_shape=[
            jax.ShapeDtypeStruct((2,) + block[1:], F32),
            jax.ShapeDtypeStruct((2,) + block[1:], BF16),
        ],
        compiler_params=params(),
        cost_estimate=cost(2 * count * rows * left_cols * right_cols, count * rows * (left_cols + right_cols) * 2),
        name=name,
    )(place, *[array for pair in pairs for array in pair], *tails)


def join_core(parts):
    keep, give = parts
    got = swap(give, "fsdp", 1)
    return got, keep + got.astype(F32)


def join_far(total, deps=()):
    give = total[1].astype(BF16)
    got = swap(gate(give, deps) if deps else give, "fsdp", 2)
    return got, total[0] + got.astype(F32)


def join_ctx(value, before, after=()):
    for bit in bits_of(lax.axis_size("ctx")):
        low = gate(value.astype(BF16), before)
        got = swap(low, "ctx", bit)
        if after:
            got = gate(got, after)
        value = low.astype(F32) + got.astype(F32)
    return value


def shards(
    tokens, attn_gain, w_query, key_matrix, value_matrix, query_gain, key_gain, w_out, ffn_gain,
    w_gate, w_up, w_down, prefix_len, out_grad,
):
    seqs, block_len, width = tokens.shape
    rows = seqs * block_len
    place = place_of()
    ctx_count = lax.axis_size("ctx")
    fsdp_count = lax.axis_size("fsdp")
    tp_count = lax.axis_size("tp")
    head_dim = query_gain.shape[0] * fsdp_count
    q_cols = w_query.shape[1]
    kv_cols = key_matrix.shape[1]
    cols = q_cols + 2 * kv_cols
    heads = q_cols // head_dim
    own_ff = w_gate.shape[1]
    rot_cols = q_cols + kv_cols
    shard_rows = w_query.shape[0]

    gains = jnp.concatenate([attn_gain, ffn_gain, query_gain, key_gain])
    gain_rows = -(-gains.size // cols)
    extra = jnp.pad(gains, (0, gain_rows * cols - gains.size)).reshape(gain_rows, cols)
    w_qkv = jnp.concatenate([w_query, key_matrix, value_matrix], axis=1)
    carried = jnp.concatenate([w_qkv, jnp.pad(extra, ((0, 16 - gain_rows), (0, 0)))], axis=0)
    from_x = swap(carried, "fsdp", 2)
    near = jnp.stack([carried, from_x])
    if ctx_count == 2:
        half = w_out.shape[0] // 2
        halves = jnp.stack([lax.dynamic_slice_in_dim(w, place[1] * half, half, 0) for w in (w_out, w_down)])
        sent = send_all(halves, "tp")
        near = gate(near, sent[1:2])
    far = swap(near, "fsdp", 1)
    own_qkv = jnp.stack([near[0], far[0], near[1], far[1]])

    gate_up = lax.all_gather(jnp.stack([w_gate, w_up]), ("fsdp", "tp"), axis=0)
    gate_w = gathered_columns(gate_up, (0,), fsdp_count, tp_count, w_gate.shape)
    up_w = gathered_columns(gate_up, (1,), fsdp_count, tp_count, w_up.shape)

    gains = in_order(own_qkv[:, shard_rows : shard_rows + gain_rows].reshape(fsdp_count, -1), "fsdp").astype(F32)
    a, q = attn_gain.size, query_gain.size
    attn_gain32 = gains[:, :a].reshape(1, -1)
    ffn_gain32 = gains[:, a : 2 * a].reshape(1, -1)
    query_gain32 = gains[:, 2 * a : 2 * a + q].reshape(1, -1)
    key_gain32 = gains[:, 2 * a + q : 2 * a + 2 * q].reshape(1, -1)
    hgain = jnp.concatenate(
        [query_gain32] * heads + [key_gain32] * (kv_cols // head_dim) + [jnp.ones((1, kv_cols), F32)], axis=1
    )
    query_pos = place[1] * block_len + jnp.arange(block_len, dtype=jnp.int32)
    cos_half, sin_half = rotary_tables(query_pos, head_dim)
    copies = 2 * cols // head_dim
    cos = jnp.concatenate([cos_half] * copies, axis=1)
    sin = jnp.concatenate([sin_half] * copies, axis=1)

    normed, raw, query_low, kv_low = project(
        place, tokens, attn_gain32, hgain, cos, sin, own_qkv, head_dim, q_cols, rot_cols, []
    )
    kv_all = cube(kv_low, "ctx")
    att_own, lse, att = [None] * seqs, [None] * seqs, [None] * seqs
    whole_y, deps = [], []
    if ctx_count == 2:
        near_x = jnp.stack(sent[:1] + [gate(piece, [kv_low]) for piece in sent[1:]])
        far_x = swap(near_x, "fsdp", 2)
        near_y = swap(near_x, "ctx", 1)
    for seq in range(seqs):
        att_own[seq], lse[seq] = attend(place, prefix_len, query_low, kv_all, heads, head_dim, seq, deps)
        att[seq] = send_all(att_own[seq][0], "tp")
        deps = [lse[seq]] + att[seq][1:]
        if seq == 0 and ctx_count == 2:
            far_x = gate(far_x, deps)
            far_y = swap(far_x, "ctx", 1)
            whole_y = [near_y, far_y]
            deps = deps + [far_x]

    if ctx_count == 2:
        out_w, down_w = travelled_rows([near_x, far_x, near_y, far_y], range(2), tp_count)
    else:
        out_down = lax.all_gather(jnp.stack([w_out, w_down]), ("fsdp", "tp"), axis=0)
        out_w = gathered_rows(out_down, (0,), fsdp_count, tp_count, w_out.shape)
        down_w = gathered_rows(out_down, (1,), fsdp_count, tp_count, w_down.shape)
    w_later = gate(w_qkv, [lse[-1]] + whole_y)
    qkv_all = lax.all_gather(w_later, ("fsdp", "tp"), axis=0)
    qkv_w = gathered_columns(qkv_all, (), fsdp_count, tp_count, w_qkv.shape)

    results = None
    dquery, owned, dqkv, head_sums, pieces = ([None] * seqs for _ in range(5))

    def finish_heads(seq, deps):
        dqkv[seq], head_sums[seq] = head_back(
            raw, dquery[seq], owned[seq], hgain, cos, sin, head_dim, rot_cols, seq, deps
        )
        pieces[seq] = send_all(dqkv[seq], "tp")

    deps = [w_later]
    for seq in range(seqs):
        *results, done = layer(
            place, tokens, out_grad, ffn_gain32, att[seq], gate_w, up_w, down_w, out_w, own_ff, seq, results, deps
        )
        deps = [done]
        if seq + 1 < seqs:
            deps = deps + att[seq + 1][1:]
        layer_low, dres_low, ffn_in, hidden, dgate_up, dattended = results
        dquery[seq], dkv = attend_back(
            place, prefix_len, query_low, kv_all, dattended, lse[seq], heads, head_dim, seq, deps
        )
        owned[seq] = cube_own(dkv, "ctx")
        deps = [dquery[seq]]
        if seq + 1 < seqs:
            finish_heads(seq, deps)
            deps = [head_sums[seq]]
    flat = lambda value: value.reshape(rows, -1)
    gate_up_parts = weight_grad(
        place, [(flat(ffn_in), flat(dgate_up))], True, "grad_gate_up",
        deps + [qkv_all] + [array for piece in pieces[:-1] for array in piece[1:]],
    )
    gate_up_got, gate_up_sum = join_core(gate_up_parts)
    finish_heads(seqs - 1, [gate_up_parts[0]])
    attended = jnp.concatenate([value[0] for value in att_own], axis=0)
    joined = jnp.concatenate(dqkv, axis=0)
    qkv_parts = weight_grad(place, [(flat(normed), joined)], True, "grad_qkv", [head_sums[-1]], head_sums)
    qkv_got, qkv_sum = join_core(qkv_parts)
    down_out_parts = weight_grad(
        place, [(flat(hidden), flat(out_grad)), (attended, flat(dres_low))], False, "grad_down_out",
        [qkv_parts[0], qkv_got, gate_up_got],
    )
    down_out_got, down_out_sum = join_core(down_out_parts)
    gate_up_far, gate_up_sum = join_far(gate_up_sum)
    qkv_far, qkv_sum = join_far(qkv_sum)
    deps = [down_out_parts[0], down_out_got]
    input_grad, done = None, [None] * seqs
    for seq in range(seqs):
        input_grad, done[seq] = input_part(
            place, tokens, dres_low, attn_gain32, pieces[seq], qkv_w, seq, input_grad, deps
        )
        deps = [done[seq], gate_up_far, qkv_far]
    gate_up_grad = join_ctx(gate_up_sum, done[:1], done[-1:])[0]
    qkv_grad = join_ctx(qkv_sum, done[:1], done[-1:])[0]
    down_out = join_ctx(join_far(down_out_sum)[1], done[-1:])

    head_sum = qkv_grad[shard_rows].reshape(-1, head_dim)
    qkv_grad = qkv_grad[:shard_rows]
    weighted = lambda weight, grad: jnp.sum(weight.astype(F32) * grad, axis=1)
    grad_gate, grad_up = gate_up_grad[:, :own_ff], gate_up_grad[:, own_ff:]
    sums = jnp.concatenate(
        [
            weighted(w_qkv, qkv_grad),
            weighted(w_gate, grad_gate) + weighted(w_up, grad_up),
            jnp.sum(head_sum[:heads], axis=0),
            jnp.sum(head_sum[heads : heads + kv_cols // head_dim], axis=0),
        ]
    )
    sums = paired_sum(send_all(sums.reshape(1, -1), "tp"))[0]
    member = lax.axis_index("fsdp")
    head_share = lambda start: lax.dynamic_slice_in_dim(sums, start + member * q, q, 0)
    return (
        layer_low,
        input_grad,
        sums[:a] / attn_gain.astype(F32),
        qkv_grad[:, :q_cols],
        qkv_grad[:, q_cols : q_cols + kv_cols],
        qkv_grad[:, q_cols + kv_cols :],
        head_share(2 * a),
        head_share(2 * a + head_dim),
        down_out[1],
        sums[a : 2 * a] / ffn_gain.astype(F32),
        grad_gate,
        grad_up,
        down_out[0],
    )


def solution(mesh):
    columns = P("fsdp", "tp")
    across = P("tp", "fsdp")
    vector = P("fsdp")
    data = P("fsdp", "ctx", None)
    return jax.shard_map(
        shards,
        mesh=mesh,
        in_specs=(
            data, vector, columns, columns, columns, vector, vector, across, vector,
            columns, columns, across, vector, data,
        ),
        out_specs=(
            data, data, vector, columns, columns, columns, vector, vector, across, vector,
            columns, columns, across,
        ),
        check_vma=False,
    )
```

```python
import functools

import jax
import jax.numpy as jnp
from jax import lax
from jax.experimental import pallas as pl
from jax.experimental.pallas import tpu as pltpu
from jax.sharding import PartitionSpec as P

EPSILON = 1e-06
NEGATIVE = -1e30
ROPE_BASE = 10000.0
F32 = jnp.float32
BF16 = jnp.bfloat16
VMEM_LIMIT = 60 * 1024 * 1024
SPARE = 16
ANY = pl.BlockSpec(memory_space=pl.ANY)


def dot(left, right, dims, precision=None):
    return lax.dot_general(
        left, right, (dims, ((), ())), precision=precision, preferred_element_type=F32
    )


def mm(left, right):
    return dot(left, right, ((1,), (0,)))


def mm_t(left, right):
    return dot(left, right, ((1,), (1,)))


def outer_sum(left, right):
    return dot(left, right, ((0,), (0,)))


def params():
    return pltpu.CompilerParams(vmem_limit_bytes=VMEM_LIMIT)


def cost(flops, nbytes, exps=0, part=1e-3):
    return pl.CostEstimate(
        flops=int(flops * part), bytes_accessed=int(nbytes * part), transcendentals=int(exps * part)
    )


def rotary_tables(positions, head_dim):
    inverse_freq = ROPE_BASE ** (-jnp.arange(0, head_dim, 2).astype(F32) / head_dim)
    angles = positions.astype(F32)[:, None] * inverse_freq[None, :]
    return (jnp.cos(angles), jnp.sin(angles))


def swap(value, axis, bit):
    return lax.ppermute(value, axis, [(i, i ^ bit) for i in range(lax.axis_size(axis))])


def bits_of(size):
    return [1 << b for b in range(size.bit_length() - 1)]


def ring(value, axis):
    size = lax.axis_size(axis)
    pieces = [value]
    for _ in range(size - 1):
        pieces.append(lax.ppermute(pieces[-1], axis, [(i, (i + 1) % size) for i in range(size)]))
    return pieces


def send_all(value, axis):
    size = lax.axis_size(axis)
    return [value] + [
        lax.ppermute(value, axis, [(i, (i + k) % size) for i in range(size)]) for k in range(1, size)
    ]


def paired_sum(pieces):
    while len(pieces) > 1:
        half = len(pieces) // 2
        pieces = [pieces[i] + pieces[i + half] for i in range(half)]
    return pieces[0]


def in_order(stack, axis):
    me = lax.axis_index(axis)
    size = stack.shape[0]
    rows = []
    for member in range(size):
        rows.append(sum(jnp.where((me ^ m) == member, stack[m : m + 1], 0) for m in range(size)))
    return jnp.concatenate(rows, axis=0)


def cube(value, axis):
    stacked = value[None]
    for bit in bits_of(lax.axis_size(axis)):
        stacked = jnp.concatenate([stacked, swap(stacked, axis, bit)], axis=0)
    return stacked


def cube_sum(value, axis):
    for bit in bits_of(lax.axis_size(axis)):
        low = value.astype(BF16)
        value = low.astype(F32) + swap(low, axis, bit).astype(F32)
    return value


def cube_own(value, axis):
    for bit in reversed(bits_of(lax.axis_size(axis))):
        half = value.shape[0] // 2
        value = value[:half] + swap(value[half:].astype(BF16), axis, bit).astype(F32)
    return value[0]


def launch(deps, kernel, *, grid_spec, **options):
    deps = list(deps)

    def run(*operands):
        count = len(operands)

        def body(*refs):
            return kernel(*refs[:count], *refs[count + len(deps) :])

        spec = pltpu.PrefetchScalarGridSpec(
            num_scalar_prefetch=grid_spec.num_scalar_prefetch,
            grid=grid_spec.grid,
            in_specs=list(grid_spec.in_specs) + [ANY] * len(deps),
            out_specs=grid_spec.out_specs,
            scratch_shapes=grid_spec.scratch_shapes,
        )
        return pl.pallas_call(body, grid_spec=spec, **options)(*operands, *deps)

    return run


def gate_kernel(value_ref, out_ref):
    pass


def gate(value, deps):
    return launch(
        deps,
        gate_kernel,
        grid_spec=pltpu.PrefetchScalarGridSpec(num_scalar_prefetch=0, grid=(1,), in_specs=[ANY], out_specs=ANY),
        out_shape=jax.ShapeDtypeStruct(value.shape, value.dtype),
        input_output_aliases={0: 0},
        compiler_params=params(),
        cost_estimate=cost(1, 1),
        name="gate",
    )(value)


def place_of():
    return jnp.stack(
        [lax.axis_index("fsdp"), lax.axis_index("ctx"), lax.axis_index("tp")]
    ).astype(jnp.int32)


class Pieces:
    def __init__(self, arrays, listing, shape, dims):
        self.arrays = arrays
        self.listing = listing
        self.shape = shape
        self.dims = dims

    def copies(self, place, refs, target, only_own=False):
        for number, index, where in self.listing:
            spot = where(place)
            if spot is None:
                continue
            row, col, own = spot
            if only_own and not own:
                continue
            rows, cols = self.shape
            if only_own:
                row = row - place[2] * self.dims
            yield (
                refs[number].at[index],
                target.at[pl.ds(pl.multiple_of(row, rows), rows), pl.ds(pl.multiple_of(col, cols), cols)],
            )


def gathered_columns(stack, lead, fsdp_count, tp_count, shape):
    rows, cols = shape
    listing = []
    for f in range(fsdp_count):
        for t in range(tp_count):
            listing.append(
                (0, (f * tp_count + t,) + lead, lambda place, f=f, t=t: (f * rows, t * cols, False))
            )
    return Pieces([stack], listing, shape, rows)


def gathered_rows(stack, lead, fsdp_count, tp_count, shape):
    rows, cols = shape
    listing = []
    for f in range(fsdp_count):
        for t in range(tp_count):
            listing.append(
                (0, (f * tp_count + t,) + lead, lambda place, f=f, t=t: (t * rows, f * cols, False))
            )
    return Pieces([stack], listing, shape, rows)


def travelled_rows(quarters, which, tp_count):
    rows, cols = quarters[0].shape[2:]
    arrays = list(quarters) + [swap(array, "fsdp", 1) for array in quarters]
    weights = []
    for weight in which:
        listing = []
        for number in range(8):
            for k in range(tp_count):

                def where(place, number=number, k=k):
                    tp = lax.rem(place[2] + (tp_count - k), tp_count)
                    row = tp * (2 * rows) + (place[1] ^ (number // 2 % 2)) * rows
                    col = (place[0] ^ (2 * (number % 2) + number // 4)) * cols
                    return (row, col, False)

                listing.append((number, (k, weight), where))
        weights.append(Pieces(arrays, listing, (rows, cols), 2 * rows))
    return weights


def fetch(copies, sems, base=0):
    started = [pltpu.make_async_copy(src, dst, sems.at[base + i]) for i, (src, dst) in enumerate(copies)]
    for copy in started:
        copy.start()
    return started


def group_mean(values, head_dim):
    width = values.shape[1]
    row = lax.broadcasted_iota(jnp.int32, (width, width), 0) // head_dim
    col = lax.broadcasted_iota(jnp.int32, (width, width), 1) // head_dim
    ones = jnp.where(row == col, 1.0 / head_dim, 0.0).astype(BF16)
    high = values.astype(BF16)
    rest = values - high.astype(F32)
    mid = rest.astype(BF16)
    low = (rest - mid.astype(F32)).astype(BF16)
    return mm(high, ones) + mm(mid, ones) + mm(low, ones)


def half_turn(values, head_dim):
    width = values.shape[1]
    half = head_dim // 2
    lane = lax.broadcasted_iota(jnp.int32, values.shape, 1)
    low = (lane & (head_dim - 1)) < half
    return jnp.where(low, pltpu.roll(values, width - half, 1), pltpu.roll(values, half, 1)), low


def project_kernel(
    place, tok_ref, gain_ref, hgain_ref, cos_ref, sin_ref, w_in, normed_ref, raw_ref, q_ref, kv_ref,
    w_ref, sems, *, head_dim, q_cols, rot_cols, chunk,
):
    shard = w_ref.shape[0] // w_in.shape[0]
    tile = tok_ref.shape[1]

    @pl.when(pl.program_id(0) == 0)
    def _():
        moves = []
        for m in range(w_in.shape[0]):
            row = pl.multiple_of((place[0] ^ m) * shard, shard)
            moves.append((w_in.at[m, pl.ds(0, shard)], w_ref.at[pl.ds(row, shard), :]))
        for copy in fetch(moves, sems):
            copy.wait()

    def norm(i, carry):
        rows = pl.ds(pl.multiple_of(i * chunk, chunk), chunk)
        x = tok_ref[0, rows, :].astype(F32)
        r = lax.rsqrt(jnp.mean(x * x, axis=-1, keepdims=True) + EPSILON)
        normed_ref[0, rows, :] = (x * r * gain_ref[...]).astype(BF16)
        return carry

    lax.fori_loop(0, tile // chunk, norm, 0)
    raw = mm(normed_ref[0], w_ref[...])
    raw_ref[0] = raw
    scale = lax.rsqrt(group_mean(raw * raw, head_dim) + EPSILON)
    n = raw * scale * hgain_ref[...]
    turned, low = half_turn(n, head_dim)
    rot = n * cos_ref[...] + jnp.where(low, -turned, turned) * sin_ref[...]
    lane = lax.broadcasted_iota(jnp.int32, raw.shape, 1)
    out = jnp.where(lane < rot_cols, rot, raw).astype(BF16)
    q_ref[0] = out[:, :q_cols]
    kv_ref[0] = out[:, q_cols:]


def project(place, tokens, gain, hgain, cos, sin, w_in, head_dim, q_cols, rot_cols, deps):
    seqs, rows, width = tokens.shape
    cols = w_in.shape[2]
    row_spec = lambda last: pl.BlockSpec((1, rows, last), lambda s, *_: (s, 0, 0))
    flat = lambda shape: pl.BlockSpec(shape, lambda s, *_: (0,) * len(shape))
    return launch(
        deps,
        functools.partial(
            project_kernel, head_dim=head_dim, q_cols=q_cols, rot_cols=rot_cols, chunk=64
        ),
        grid_spec=pltpu.PrefetchScalarGridSpec(
            num_scalar_prefetch=1,
            grid=(seqs,),
            in_specs=[
                row_spec(width), flat((1, width)), flat((1, cols)), flat((rows, cols)), flat((rows, cols)), ANY,
            ],
            out_specs=[row_spec(width), row_spec(cols), row_spec(q_cols), row_spec(cols - q_cols)],
            scratch_shapes=[
                pltpu.VMEM((width, cols), BF16), pltpu.SemaphoreType.DMA((w_in.shape[0],)),
            ],
        ),
        out_shape=[
            jax.ShapeDtypeStruct((seqs, rows, width), BF16),
            jax.ShapeDtypeStruct((seqs, rows, cols), F32),
            jax.ShapeDtypeStruct((seqs, rows, q_cols), BF16),
            jax.ShapeDtypeStruct((seqs, rows, cols - q_cols), BF16),
        ],
        compiler_params=params(),
        cost_estimate=cost(2 * seqs * rows * width * cols, seqs * rows * width * 4),
        name="project",
    )(place, tokens, gain, hgain, cos, sin, w_in)


def allowed_t(place, prefix, part, key_count, block, tile):
    j = lax.broadcasted_iota(jnp.int32, (key_count, tile), 0)
    key_pos = (place ^ (j // block)) * block + (j & (block - 1))
    query_pos = place * block + part * tile + lax.broadcasted_iota(jnp.int32, (key_count, tile), 1)
    return (key_pos <= query_pos) | (key_pos < prefix)


def attend_kernel(
    place, prefix, q_ref, kv_ref, out_ref, lse_ref, *, seq, heads, head_dim, tile, block
):
    part = pl.program_id(0)
    pairs = kv_ref[:, 0].reshape(-1, 2 * head_dim)
    keys = pairs[:, :head_dim]
    values = pairs[:, head_dim:]
    allowed = allowed_t(place[1], prefix[seq], part, pairs.shape[0], block, tile)
    for head in range(heads):
        lanes = slice(head * head_dim, (head + 1) * head_dim)
        scores = mm_t(keys, q_ref[0, :, lanes]) * (head_dim ** (-0.5))
        scores = jnp.where(allowed, scores, NEGATIVE)
        top = jnp.max(scores, axis=0, keepdims=True)
        weight = jnp.exp(scores - top)
        total = jnp.sum(weight, axis=0, keepdims=True)
        probs = weight * (1.0 / total)
        out_ref[0, :, lanes] = outer_sum(probs.astype(BF16), values).astype(BF16)
        lse_ref[0, head : head + 1, :] = top + jnp.log(total)


def attention_specs(seq, rows, q_cols, heads, kv_all):
    tile = min(256, rows)
    blocks, _, block, pair = kv_all.shape
    row_block = pl.BlockSpec((1, tile, q_cols), lambda i, *_: (seq, i, 0))
    own_block = pl.BlockSpec((1, tile, q_cols), lambda i, *_: (0, i, 0))
    key_block = pl.BlockSpec((blocks, 1, block, pair), lambda i, *_: (0, seq, 0, 0))
    stat_block = pl.BlockSpec((1, heads, tile), lambda i, *_: (0, 0, i))
    return tile, blocks, block, pair, row_block, own_block, key_block, stat_block


def attend(place, prefix, query, kv_all, heads, head_dim, seq, deps):
    _, rows, q_cols = query.shape
    tile, blocks, block, pair, row_block, own_block, key_block, stat_block = attention_specs(
        seq, rows, q_cols, heads, kv_all
    )
    elements = rows * blocks * block * heads
    return launch(
        deps,
        functools.partial(
            attend_kernel, seq=seq, heads=heads, head_dim=head_dim, tile=tile, block=block
        ),
        grid_spec=pltpu.PrefetchScalarGridSpec(
            num_scalar_prefetch=2,
            grid=(rows // tile,),
            in_specs=[row_block, key_block],
            out_specs=[own_block, stat_block],
        ),
        out_shape=[
            jax.ShapeDtypeStruct((1, rows, q_cols), BF16),
            jax.ShapeDtypeStruct((1, heads, rows), F32),
        ],
        compiler_params=params(),
        cost_estimate=cost(elements * 1024, query.size * 4, elements),
        name="attend",
    )(place, prefix, query, kv_all)


def attend_back_kernel(
    place, prefix, q_ref, kv_ref, d_ref, lse_ref, dq_ref, dkv_ref, *, seq, heads, head_dim, tile, block
):
    part = pl.program_id(0)
    scale = head_dim ** (-0.5)
    pairs = kv_ref[:, 0].reshape(-1, 2 * head_dim)
    keys = pairs[:, :head_dim]
    values = pairs[:, head_dim:]
    allowed = allowed_t(place[1], prefix[seq], part, pairs.shape[0], block, tile)

    @pl.when(part == 0)
    def _():
        dkv_ref[...] = jnp.zeros_like(dkv_ref)

    def two_heads(pair, carry):
        lanes = pl.ds(pl.multiple_of(pair * 2 * head_dim, 2 * head_dim), 2 * head_dim)
        queries, douts = q_ref[0, :, lanes], d_ref[0, :, lanes]
        dkeys, dvalues, dqs = 0.0, 0.0, []
        for half in range(2):
            mine = slice(half * head_dim, (half + 1) * head_dim)
            query, dout = queries[:, mine], douts[:, mine]
            scores = mm_t(keys, query) * scale
            probs = jnp.where(allowed, jnp.exp(scores - lse_ref[0, pl.ds(2 * pair + half, 1), :]), 0.0)
            weighted = probs * mm_t(values, dout)
            delta = jnp.sum(weighted, axis=0, keepdims=True)
            dscore = (weighted - probs * delta).astype(BF16)
            dvalues += mm(probs.astype(BF16), dout)
            dkeys += mm(dscore, query)
            dqs.append(outer_sum(dscore, keys) * scale)
        dq_ref[0, :, lanes] = jnp.concatenate(dqs, axis=1)
        both = jnp.concatenate([dkeys * scale, dvalues], axis=1)
        dkv_ref[:, 0] += both.reshape(dkv_ref.shape[0], block, -1)
        return carry

    lax.fori_loop(0, heads // 2, two_heads, 0)


def attend_back(place, prefix, query, kv_all, dout, lse, heads, head_dim, seq, deps):
    _, rows, q_cols = query.shape
    tile, blocks, block, pair, row_block, own_block, key_block, stat_block = attention_specs(
        seq, rows, q_cols, heads, kv_all
    )
    elements = rows * blocks * block * heads
    return launch(
        deps,
        functools.partial(
            attend_back_kernel, seq=seq, heads=heads, head_dim=head_dim, tile=tile, block=block
        ),
        grid_spec=pltpu.PrefetchScalarGridSpec(
            num_scalar_prefetch=2,
            grid=(rows // tile,),
            in_specs=[row_block, key_block, row_block, stat_block],
            out_specs=[own_block, pl.BlockSpec((blocks, 1, block, pair), lambda i, *_: (0, 0, 0, 0))],
        ),
        out_shape=[
            jax.ShapeDtypeStruct((1, rows, q_cols), F32),
            jax.ShapeDtypeStruct((blocks, 1, block, pair), F32),
        ],
        compiler_params=params(),
        cost_estimate=cost(elements * 2560, query.size * 8, elements),
        name="attend_back",
    )(place, prefix, query, kv_all, dout, lse)


def layer_kernel(*refs, seq, tp_count, gate_w, down_w, out_w, up_w, out_count, step, own_cols):
    place, gain_ref, tok_in, og_in = refs[:4]
    refs = refs[4:]
    att_in, refs = refs[:tp_count], refs[tp_count:]
    gate_in, refs = refs[: len(gate_w.arrays)], refs[len(gate_w.arrays) :]
    down_in, refs = refs[: len(down_w.arrays)], refs[len(down_w.arrays) :]
    out_in = down_in
    outs, refs = refs[-out_count - 22 :][: out_count + 1], refs[-21:]
    token_ref = outs[-1]
    lay_out, dres_out, fin_out, hid_out, dgu_out, datt_out = outs[:-1]
    (
        tok, og, att, wo, wg, wu, wd, res, fin, hid, dgate, dup, lift, lay, dres, own_hid, own_dgu, datt,
        sems, more, final,
    ) = refs
    tile, width = tok.shape
    ff = wd.shape[0]
    cols = att_in[0].shape[1]

    moves = [(tok_in.at[seq], tok)]
    for k in range(tp_count):
        col = lax.rem(place[2] + (tp_count - k), tp_count) * cols
        moves.append((att_in[k], att.at[:, pl.ds(pl.multiple_of(col, cols), cols)]))
    moves += list(out_w.copies(place, out_in, wo))
    first = fetch(moves, sems)
    base = len(first)
    second = fetch(list(gate_w.copies(place, gate_in, wg)) + list(up_w.copies(place, gate_in, wu)), sems, base)
    base += len(second)
    third = fetch([(og_in.at[seq], og)] + list(down_w.copies(place, down_in, wd)), sems, base)
    for copy in first:
        copy.wait()

    def lanes_of(i):
        return pl.ds(pl.multiple_of(i * step, step), step)

    def out_part(i, total):
        lanes = lanes_of(i)
        row = tok[:, lanes].astype(F32) + mm(att[...], wo[:, lanes])
        res[:, lanes] = row
        return total + row * row

    total = lax.fori_loop(0, width // step, out_part, jnp.zeros((tile, step), F32))
    r = lax.rsqrt(jnp.sum(total, axis=-1, keepdims=True) / width + EPSILON)

    def norm(i, carry):
        lanes = lanes_of(i)
        fin[:, lanes] = (res[:, lanes] * r * gain_ref[:, lanes]).astype(BF16)
        return carry

    lax.fori_loop(0, width // step, norm, 0)
    leave_fin = pltpu.make_async_copy(fin, fin_out.at[seq], final.at[0])
    leave_fin.start()
    for copy in second + third:
        copy.wait()

    def inner(i, carry):
        lanes = lanes_of(i)
        gate = mm(fin[...], wg[:, lanes])
        up = mm(fin[...], wu[:, lanes])
        grad = mm_t(og[...], wd[lanes, :])
        sig = 1.0 / (1.0 + jnp.exp(-gate))
        silu = gate * sig
        hid[:, lanes] = (silu * up).astype(BF16)
        dgate[:, lanes] = (grad * up * sig * (1.0 + gate * (1.0 - sig))).astype(BF16)
        dup[:, lanes] = (grad * silu).astype(BF16)
        return carry

    lax.fori_loop(0, ff // step, inner, 0)
    own = pl.ds(pl.multiple_of(place[2] * own_cols, own_cols), own_cols)
    own_hid[...] = hid[:, own]
    own_dgu[:, :own_cols] = dgate[:, own]
    own_dgu[:, own_cols:] = dup[:, own]
    leave_own = [
        pltpu.make_async_copy(own_hid, hid_out.at[seq], final.at[1]),
        pltpu.make_async_copy(own_dgu, dgu_out.at[seq], final.at[2]),
    ]
    for copy in leave_own:
        copy.start()

    def outer(i, total):
        lanes = lanes_of(i)
        row = res[:, lanes]
        lay[:, lanes] = (row + mm(hid[...], wd[:, lanes])).astype(BF16)
        grad = mm_t(dgate[...], wg[lanes, :]) + mm_t(dup[...], wu[lanes, :])
        u = grad * gain_ref[:, lanes]
        lift[:, lanes] = u
        return total + row * u

    token_ref[...] = jnp.zeros_like(token_ref)
    total = lax.fori_loop(0, width // step, outer, jnp.zeros((tile, step), F32))
    leave_lay = pltpu.make_async_copy(lay, lay_out.at[seq], final.at[3])
    leave_lay.start()
    pull = r * r * r * (jnp.sum(total, axis=-1, keepdims=True) / width)

    def finish(i, carry):
        lanes = lanes_of(i)
        grad = og[:, lanes].astype(F32) + r * lift[:, lanes] - res[:, lanes] * pull
        dres[:, lanes] = grad.astype(BF16)
        return carry

    lax.fori_loop(0, width // step, finish, 0)
    leave_dres = pltpu.make_async_copy(dres, dres_out.at[seq], final.at[4])
    leave_dres.start()
    own_rows = pl.ds(pl.multiple_of(place[2] * cols, cols), cols)
    datt[...] = mm_t(dres[...], wo[own_rows, :]).astype(BF16)
    leave_datt = pltpu.make_async_copy(datt, datt_out.at[seq], final.at[5])
    leave_datt.start()
    for copy in leave_own + [leave_fin, leave_lay, leave_dres, leave_datt]:
        copy.wait()


def layer(place, tokens, out_grad, gain, att, gate_w, up_w, down_w, out_w, own_cols, seq, before, deps):
    seqs, rows, width = tokens.shape
    q_cols = att[0].shape[1]
    inner = q_cols * len(att)
    ff = own_cols * len(att)
    arrays = list(att) + gate_w.arrays + down_w.arrays
    count = 2 + len(att) + 2 * len(gate_w.listing) + len(down_w.listing) + len(out_w.listing)
    vec = pl.BlockSpec((1, width), lambda *_: (0, 0))
    outs = [
        jax.ShapeDtypeStruct((seqs, rows, last), BF16)
        for last in (width, width, width, own_cols, 2 * own_cols, q_cols)
    ]
    prior = list(before) if before is not None else []
    start = 4 + len(arrays)
    return launch(
        deps,
        functools.partial(
            layer_kernel, seq=seq, tp_count=len(att), gate_w=gate_w, up_w=up_w, down_w=down_w, out_w=out_w,
            out_count=len(outs), step=256, own_cols=own_cols,
        ),
        grid_spec=pltpu.PrefetchScalarGridSpec(
            num_scalar_prefetch=1,
            grid=(1,),
            in_specs=[vec, ANY, ANY] + [ANY] * (len(arrays) + len(prior)),
            out_specs=[ANY] * len(outs) + [pl.BlockSpec((8, 128), lambda *_: (0, 0))],
            scratch_shapes=[
                pltpu.VMEM((rows, width), BF16),
                pltpu.VMEM((rows, width), BF16),
                pltpu.VMEM((rows, inner), BF16),
                pltpu.VMEM((inner, width), BF16),
                pltpu.VMEM((width, ff), BF16),
                pltpu.VMEM((width, ff), BF16),
                pltpu.VMEM((ff, width), BF16),
                pltpu.VMEM((rows, width), F32),
                pltpu.VMEM((rows, width), BF16),
                pltpu.VMEM((rows, ff), BF16),
                pltpu.VMEM((rows, ff), BF16),
                pltpu.VMEM((rows, ff), BF16),
                pltpu.VMEM((rows, width), F32),
                pltpu.VMEM((rows, width), BF16),
                pltpu.VMEM((rows, width), BF16),
                pltpu.VMEM((rows, own_cols), BF16),
                pltpu.VMEM((rows, 2 * own_cols), BF16),
                pltpu.VMEM((rows, q_cols), BF16),
                pltpu.SemaphoreType.DMA((count,)),
                pltpu.SemaphoreType.DMA((1,)),
                pltpu.SemaphoreType.DMA((6,)),
            ],
        ),
        out_shape=outs + [jax.ShapeDtypeStruct((8, 128), F32)],
        input_output_aliases={start + i: i for i in range(len(prior))},
        compiler_params=params(),
        cost_estimate=cost(2 * rows * width * (6 * ff + inner + q_cols), rows * width * 12 + 8 * width * ff),
        name="layer",
    )(place, gain, tokens, out_grad, *arrays, *prior)


def head_back_kernel(
    raw_ref, dq_ref, dkv_ref, hgain_ref, cos_ref, sin_ref, out_ref, gsum_ref, *, head_dim, rot_cols
):
    raw = raw_ref[0]
    grad = jnp.concatenate([dq_ref[0], dkv_ref[0]], axis=1)
    lane = lax.broadcasted_iota(jnp.int32, raw.shape, 1)
    turned, low = half_turn(grad * sin_ref[...], head_dim)
    dn = grad * cos_ref[...] + jnp.where(low, turned, -turned)
    r = lax.rsqrt(group_mean(raw * raw, head_dim) + EPSILON)
    u = dn * hgain_ref[...]
    mean = group_mean(raw * u, head_dim)
    draw = r * u - raw * (r * r * r * mean)
    out_ref[...] = jnp.where(lane < rot_cols, draw, grad).astype(BF16)
    gsum_ref[...] = jnp.broadcast_to(jnp.sum(dn * raw * r, axis=0, keepdims=True), gsum_ref.shape)


def head_back(raw, dq, dkv, hgain, cos, sin, head_dim, rot_cols, seq, deps):
    _, rows, cols = raw.shape
    row_spec = lambda last, at: pl.BlockSpec((1, rows, last), lambda i: (at, 0, 0))
    flat = lambda shape: pl.BlockSpec(shape, lambda i: (0, 0))
    return launch(
        deps,
        functools.partial(head_back_kernel, head_dim=head_dim, rot_cols=rot_cols),
        grid_spec=pltpu.PrefetchScalarGridSpec(
            num_scalar_prefetch=0,
            grid=(1,),
            in_specs=[
                row_spec(cols, seq), row_spec(dq.shape[2], 0), row_spec(dkv.shape[2], 0), flat((1, cols)),
                flat((rows, cols)), flat((rows, cols)),
            ],
            out_specs=[flat((rows, cols)), flat((SPARE, cols))],
        ),
        out_shape=[jax.ShapeDtypeStruct((rows, cols), BF16), jax.ShapeDtypeStruct((SPARE, cols), F32)],
        compiler_params=params(),
        cost_estimate=cost(rows * cols * cols * 12, rows * cols * 14),
        name="head_back",
    )(raw, dq, dkv, hgain, cos, sin)


def input_kernel(*refs, tp_count, qkv_w, step):
    place, tok_ref, dres_ref, gain_ref = refs[:4]
    refs = refs[4:]
    d_in, refs = refs[:tp_count], refs[tp_count:]
    w_in, refs = refs[: len(qkv_w.arrays)], refs[len(qkv_w.arrays) :]
    out_ref, token_ref, dall, w, lift, sems = refs[-6:]
    tile, width = lift.shape
    cols = d_in[0].shape[1]
    moves = []
    for k in range(tp_count):
        col = lax.rem(place[2] + (tp_count - k), tp_count) * cols
        moves.append((d_in[k], dall.at[:, pl.ds(pl.multiple_of(col, cols), cols)]))
    moves += list(qkv_w.copies(place, w_in, w))
    started = fetch(moves, sems)

    def lanes_of(i):
        return pl.ds(pl.multiple_of(i * step, step), step)

    token_ref[...] = jnp.zeros_like(token_ref)

    def square(i, total):
        x = tok_ref[0, :, lanes_of(i)].astype(F32)
        return total + x * x

    total = lax.fori_loop(0, width // step, square, jnp.zeros((tile, step), F32))
    r = lax.rsqrt(jnp.sum(total, axis=-1, keepdims=True) / width + EPSILON)
    for copy in started:
        copy.wait()

    def outer(i, total):
        lanes = lanes_of(i)
        x = tok_ref[0, :, lanes].astype(F32)
        grad = mm_t(dall[...], w[lanes, :])
        u = grad * gain_ref[:, lanes]
        lift[:, lanes] = u
        return total + x * u

    total = lax.fori_loop(0, width // step, outer, jnp.zeros((tile, step), F32))
    pull = r * r * r * (jnp.sum(total, axis=-1, keepdims=True) / width)

    def finish(i, carry):
        lanes = lanes_of(i)
        x = tok_ref[0, :, lanes].astype(F32)
        grad = dres_ref[0, :, lanes].astype(F32) + r * lift[:, lanes] - x * pull
        out_ref[0, :, lanes] = grad.astype(BF16)
        return carry

    lax.fori_loop(0, width // step, finish, 0)


def input_part(place, tokens, dres, gain, pieces, qkv_w, seq, before, deps):
    seqs, rows, width = tokens.shape
    inner = pieces[0].shape[1] * len(pieces)
    row_spec = pl.BlockSpec((1, rows, width), lambda *_: (seq, 0, 0))
    vec = pl.BlockSpec((1, width), lambda *_: (0, 0))
    arrays = list(pieces) + qkv_w.arrays
    prior = [] if before is None else [before]
    return launch(
        deps,
        functools.partial(input_kernel, tp_count=len(pieces), qkv_w=qkv_w, step=256),
        grid_spec=pltpu.PrefetchScalarGridSpec(
            num_scalar_prefetch=1,
            grid=(1,),
            in_specs=[row_spec, row_spec, vec] + [ANY] * (len(arrays) + len(prior)),
            out_specs=[row_spec, pl.BlockSpec((8, 128), lambda *_: (0, 0))],
            scratch_shapes=[
                pltpu.VMEM((rows, inner), BF16),
                pltpu.VMEM((width, inner), BF16),
                pltpu.VMEM((rows, width), F32),
                pltpu.SemaphoreType.DMA((len(pieces) + len(qkv_w.listing),)),
            ],
        ),
        out_shape=[
            jax.ShapeDtypeStruct((seqs, rows, width), BF16),
            jax.ShapeDtypeStruct((8, 128), F32),
        ],
        input_output_aliases={4 + len(arrays): 0} if prior else {},
        compiler_params=params(),
        cost_estimate=cost(2 * rows * width * inner, rows * width * 6 + width * inner * 2),
        name="input_part",
    )(place, tokens, dres, gain, *arrays, *prior)


def weight_grad_kernel(place, *refs, count, tails):
    keep_ref, give_ref = refs[-2:]
    step = pl.program_id(0)
    for i in range(count):
        grad = outer_sum(refs[2 * i][...], refs[2 * i + 1][...])
        if tails:
            grad = jnp.concatenate([grad, sum(ref[...] for ref in refs[2 * count : -2])], axis=0)

        @pl.when(step < 2)
        def _():
            keep_ref[0, i] = grad

        @pl.when(step >= 2)
        def _():
            give_ref[0, i] = grad.astype(BF16)


def weight_grad(place, pairs, cut_left, name, deps, tails=()):
    rows = pairs[0][0].shape[0]
    left_cols, right_cols = pairs[0][0].shape[1], pairs[0][1].shape[1]

    def piece(step, place):
        return place[0] ^ (2 * (step & 1) + (step >> 1))

    moving = lambda cols: pl.BlockSpec((rows, cols // 4), lambda m, place: (0, piece(m, place)))
    fixed = lambda cols: pl.BlockSpec((rows, cols), lambda m, place: (0, 0))
    if cut_left:
        specs = [moving(left_cols), fixed(right_cols)]
        shape = (left_cols // 4 + (SPARE if tails else 0), right_cols)
    else:
        specs = [fixed(left_cols), moving(right_cols)]
        shape = (left_cols, right_cols // 4)
    count = len(pairs)
    block = (1, count) + shape
    return launch(
        deps,
        functools.partial(weight_grad_kernel, count=count, tails=len(tails)),
        grid_spec=pltpu.PrefetchScalarGridSpec(
            num_scalar_prefetch=1,
            grid=(4,),
            in_specs=specs * count + [pl.BlockSpec(tail.shape, lambda m, place: (0, 0)) for tail in tails],
            out_specs=[
                pl.BlockSpec(block, lambda m, place: (jnp.minimum(m, 1), 0, 0, 0)),
                pl.BlockSpec(block, lambda m, place: (jnp.maximum(m - 2, 0), 0, 0, 0)),
            ],
        ),
        out_shape=[
            jax.ShapeDtypeStruct((2,) + block[1:], F32),
            jax.ShapeDtypeStruct((2,) + block[1:], BF16),
        ],
        compiler_params=params(),
        cost_estimate=cost(2 * count * rows * left_cols * right_cols, count * rows * (left_cols + right_cols) * 2),
        name=name,
    )(place, *[array for pair in pairs for array in pair], *tails)


def join_core(parts):
    keep, give = parts
    got = swap(give, "fsdp", 1)
    return got, keep + got.astype(F32)


def join_far(total, deps=()):
    give = total[1].astype(BF16)
    got = swap(gate(give, deps) if deps else give, "fsdp", 2)
    return got, total[0] + got.astype(F32)


def join_ctx(value, before, after=()):
    for bit in bits_of(lax.axis_size("ctx")):
        low = gate(value.astype(BF16), before) if before else value.astype(BF16)
        got = swap(low, "ctx", bit)
        if after:
            got = gate(got, after)
        value = low.astype(F32) + got.astype(F32)
    return value


def shards(
    tokens, attn_gain, w_query, key_matrix, value_matrix, query_gain, key_gain, w_out, ffn_gain,
    w_gate, w_up, w_down, prefix_len, out_grad,
):
    seqs, block_len, width = tokens.shape
    rows = seqs * block_len
    place = place_of()
    ctx_count = lax.axis_size("ctx")
    fsdp_count = lax.axis_size("fsdp")
    tp_count = lax.axis_size("tp")
    head_dim = query_gain.shape[0] * fsdp_count
    q_cols = w_query.shape[1]
    kv_cols = key_matrix.shape[1]
    cols = q_cols + 2 * kv_cols
    heads = q_cols // head_dim
    own_ff = w_gate.shape[1]
    rot_cols = q_cols + kv_cols
    shard_rows = w_query.shape[0]

    gains = jnp.concatenate([attn_gain, ffn_gain, query_gain, key_gain])
    gain_rows = -(-gains.size // cols)
    extra = jnp.pad(gains, (0, gain_rows * cols - gains.size)).reshape(gain_rows, cols)
    w_qkv = jnp.concatenate([w_query, key_matrix, value_matrix], axis=1)
    carried = jnp.concatenate([w_qkv, jnp.pad(extra, ((0, 16 - gain_rows), (0, 0)))], axis=0)
    from_x = swap(carried, "fsdp", 2)
    near = jnp.stack([carried, from_x])
    if ctx_count == 2:
        half = w_out.shape[0] // 2
        halves = jnp.stack([lax.dynamic_slice_in_dim(w, place[1] * half, half, 0) for w in (w_out, w_down)])
        sent = send_all(halves, "tp")
        near = gate(near, sent[1:2])
    far = swap(near, "fsdp", 1)
    own_qkv = jnp.stack([near[0], far[0], near[1], far[1]])

    gate_up = lax.all_gather(jnp.stack([w_gate, w_up]), ("fsdp", "tp"), axis=0)
    gate_w = gathered_columns(gate_up, (0,), fsdp_count, tp_count, w_gate.shape)
    up_w = gathered_columns(gate_up, (1,), fsdp_count, tp_count, w_up.shape)

    gains = in_order(own_qkv[:, shard_rows : shard_rows + gain_rows].reshape(fsdp_count, -1), "fsdp").astype(F32)
    a, q = attn_gain.size, query_gain.size
    attn_gain32 = gains[:, :a].reshape(1, -1)
    ffn_gain32 = gains[:, a : 2 * a].reshape(1, -1)
    query_gain32 = gains[:, 2 * a : 2 * a + q].reshape(1, -1)
    key_gain32 = gains[:, 2 * a + q : 2 * a + 2 * q].reshape(1, -1)
    hgain = jnp.concatenate(
        [query_gain32] * heads + [key_gain32] * (kv_cols // head_dim) + [jnp.ones((1, kv_cols), F32)], axis=1
    )
    query_pos = place[1] * block_len + jnp.arange(block_len, dtype=jnp.int32)
    cos_half, sin_half = rotary_tables(query_pos, head_dim)
    copies = 2 * cols // head_dim
    cos = jnp.concatenate([cos_half] * copies, axis=1)
    sin = jnp.concatenate([sin_half] * copies, axis=1)

    normed, raw, query_low, kv_low = project(
        place, tokens, attn_gain32, hgain, cos, sin, own_qkv, head_dim, q_cols, rot_cols, []
    )
    kv_all = cube(kv_low, "ctx")
    att_own, lse, att = [None] * seqs, [None] * seqs, [None] * seqs
    whole_y, deps = [], []
    if ctx_count == 2:
        near_x = jnp.stack(sent[:1] + [gate(piece, [kv_low]) for piece in sent[1:]])
        far_x = swap(near_x, "fsdp", 2)
        near_y = swap(gate(near_x, [kv_all]), "ctx", 1)
    for seq in range(seqs):
        att_own[seq], lse[seq] = attend(place, prefix_len, query_low, kv_all, heads, head_dim, seq, deps)
        att[seq] = send_all(att_own[seq][0], "tp")
        deps = [lse[seq]] + att[seq][1:]
        if seq == 0 and ctx_count == 2:
            far_x = gate(far_x, deps + [near_y])
            far_y = swap(far_x, "ctx", 1)
            whole_y = [near_y, far_y]
            deps = deps + [far_x]

    if ctx_count == 2:
        out_w, down_w = travelled_rows([near_x, far_x, near_y, far_y], range(2), tp_count)
    else:
        out_down = lax.all_gather(jnp.stack([w_out, w_down]), ("fsdp", "tp"), axis=0)
        out_w = gathered_rows(out_down, (0,), fsdp_count, tp_count, w_out.shape)
        down_w = gathered_rows(out_down, (1,), fsdp_count, tp_count, w_down.shape)
    w_later = gate(w_qkv, [lse[-1]] + whole_y)
    qkv_all = lax.all_gather(w_later, ("fsdp", "tp"), axis=0)
    qkv_w = gathered_columns(qkv_all, (), fsdp_count, tp_count, w_qkv.shape)

    results = None
    dquery, owned, dqkv, head_sums, pieces = ([None] * seqs for _ in range(5))

    def finish_heads(seq, deps):
        dqkv[seq], head_sums[seq] = head_back(
            raw, dquery[seq], owned[seq], hgain, cos, sin, head_dim, rot_cols, seq, deps
        )
        pieces[seq] = send_all(dqkv[seq], "tp")

    deps = [w_later]
    for seq in range(seqs):
        *results, done = layer(
            place, tokens, out_grad, ffn_gain32, att[seq], gate_w, up_w, down_w, out_w, own_ff, seq, results, deps
        )
        deps = [done]
        if seq + 1 < seqs:
            deps = deps + att[seq + 1][1:]
        layer_low, dres_low, ffn_in, hidden, dgate_up, dattended = results
        dquery[seq], dkv = attend_back(
            place, prefix_len, query_low, kv_all, dattended, lse[seq], heads, head_dim, seq, deps
        )
        owned[seq] = cube_own(dkv, "ctx")
        deps = [dquery[seq]]
        if seq + 1 < seqs:
            finish_heads(seq, deps)
            deps = [head_sums[seq]]
    flat = lambda value: value.reshape(rows, -1)
    gate_up_parts = weight_grad(
        place, [(flat(ffn_in), flat(dgate_up))], True, "grad_gate_up",
        deps + [qkv_all] + [array for piece in pieces[:-1] for array in piece[1:]],
    )
    gate_up_got, gate_up_sum = join_core(gate_up_parts)
    finish_heads(seqs - 1, [gate_up_parts[0]])
    attended = jnp.concatenate([value[0] for value in att_own], axis=0)
    joined = jnp.concatenate(dqkv, axis=0)
    qkv_parts = weight_grad(place, [(flat(normed), joined)], True, "grad_qkv", [head_sums[-1]], head_sums)
    qkv_got, qkv_sum = join_core(qkv_parts)
    down_out_parts = weight_grad(
        place, [(flat(hidden), flat(out_grad)), (attended, flat(dres_low))], False, "grad_down_out",
        [qkv_parts[0], qkv_got, gate_up_got],
    )
    down_out_got, down_out_sum = join_core(down_out_parts)
    gate_up_far, gate_up_sum = join_far(gate_up_sum)
    qkv_far, qkv_sum = join_far(qkv_sum)
    deps = [down_out_parts[0], down_out_got]
    input_grad, done = None, [None] * seqs
    for seq in range(seqs):
        input_grad, done[seq] = input_part(
            place, tokens, dres_low, attn_gain32, pieces[seq], qkv_w, seq, input_grad, deps
        )
        deps = [done[seq], gate_up_far, qkv_far]
    gate_up_grad = join_ctx(gate_up_sum, done[:1], done[-1:])[0]
    qkv_grad = join_ctx(qkv_sum, done[:1], done[-1:])[0]
    down_low = gate(join_far(down_out_sum)[1].astype(BF16), done[-1:])
    down_out = join_ctx(down_low, ())

    head_sum = qkv_grad[shard_rows].reshape(-1, head_dim)
    qkv_grad = qkv_grad[:shard_rows]
    weighted = lambda weight, grad: jnp.sum(weight.astype(F32) * grad, axis=1)
    grad_gate, grad_up = gate_up_grad[:, :own_ff], gate_up_grad[:, own_ff:]
    sums = jnp.concatenate(
        [
            weighted(w_qkv, qkv_grad),
            weighted(w_gate, grad_gate) + weighted(w_up, grad_up),
            jnp.sum(head_sum[:heads], axis=0),
            jnp.sum(head_sum[heads : heads + kv_cols // head_dim], axis=0),
        ]
    )
    sums = paired_sum(send_all(gate(sums.reshape(1, -1), [down_low]), "tp"))[0]
    member = lax.axis_index("fsdp")
    head_share = lambda start: lax.dynamic_slice_in_dim(sums, start + member * q, q, 0)
    return (
        layer_low,
        input_grad,
        sums[:a] / attn_gain.astype(F32),
        qkv_grad[:, :q_cols],
        qkv_grad[:, q_cols : q_cols + kv_cols],
        qkv_grad[:, q_cols + kv_cols :],
        head_share(2 * a),
        head_share(2 * a + head_dim),
        down_out[1],
        sums[a : 2 * a] / ffn_gain.astype(F32),
        grad_gate,
        grad_up,
        down_out[0],
    )


def solution(mesh):
    columns = P("fsdp", "tp")
    across = P("tp", "fsdp")
    vector = P("fsdp")
    data = P("fsdp", "ctx", None)
    return jax.shard_map(
        shards,
        mesh=mesh,
        in_specs=(
            data, vector, columns, columns, columns, vector, vector, across, vector,
            columns, columns, across, vector, data,
        ),
        out_specs=(
            data, data, vector, columns, columns, columns, vector, vector, across, vector,
            columns, columns, across,
        ),
        check_vma=False,
    )
```

```python
import functools

import jax
import jax.numpy as jnp
from jax import lax
from jax.experimental import pallas as pl
from jax.experimental.pallas import tpu as pltpu
from jax.sharding import PartitionSpec as P

EPSILON = 1e-06
NEGATIVE = -1e30
ROPE_BASE = 10000.0
F32 = jnp.float32
BF16 = jnp.bfloat16
VMEM_LIMIT = 60 * 1024 * 1024
SPARE = 16
ANY = pl.BlockSpec(memory_space=pl.ANY)


def dot(left, right, dims, precision=None):
    return lax.dot_general(
        left, right, (dims, ((), ())), precision=precision, preferred_element_type=F32
    )


def mm(left, right):
    return dot(left, right, ((1,), (0,)))


def mm_t(left, right):
    return dot(left, right, ((1,), (1,)))


def outer_sum(left, right):
    return dot(left, right, ((0,), (0,)))


def params():
    return pltpu.CompilerParams(vmem_limit_bytes=VMEM_LIMIT)


def cost(flops, nbytes, exps=0, part=1e-3):
    return pl.CostEstimate(
        flops=int(flops * part), bytes_accessed=int(nbytes * part), transcendentals=int(exps * part)
    )


def rotary_tables(positions, head_dim):
    inverse_freq = ROPE_BASE ** (-jnp.arange(0, head_dim, 2).astype(F32) / head_dim)
    angles = positions.astype(F32)[:, None] * inverse_freq[None, :]
    return (jnp.cos(angles), jnp.sin(angles))


def swap(value, axis, bit):
    return lax.ppermute(value, axis, [(i, i ^ bit) for i in range(lax.axis_size(axis))])


def bits_of(size):
    return [1 << b for b in range(size.bit_length() - 1)]


def ring(value, axis):
    size = lax.axis_size(axis)
    pieces = [value]
    for _ in range(size - 1):
        pieces.append(lax.ppermute(pieces[-1], axis, [(i, (i + 1) % size) for i in range(size)]))
    return pieces


def send_all(value, axis):
    size = lax.axis_size(axis)
    return [value] + [
        lax.ppermute(value, axis, [(i, (i + k) % size) for i in range(size)]) for k in range(1, size)
    ]


def paired_sum(pieces):
    while len(pieces) > 1:
        half = len(pieces) // 2
        pieces = [pieces[i] + pieces[i + half] for i in range(half)]
    return pieces[0]


def in_order(stack, axis):
    me = lax.axis_index(axis)
    size = stack.shape[0]
    rows = []
    for member in range(size):
        rows.append(sum(jnp.where((me ^ m) == member, stack[m : m + 1], 0) for m in range(size)))
    return jnp.concatenate(rows, axis=0)


def cube(value, axis):
    stacked = value[None]
    for bit in bits_of(lax.axis_size(axis)):
        stacked = jnp.concatenate([stacked, swap(stacked, axis, bit)], axis=0)
    return stacked


def cube_sum(value, axis):
    for bit in bits_of(lax.axis_size(axis)):
        low = value.astype(BF16)
        value = low.astype(F32) + swap(low, axis, bit).astype(F32)
    return value


def cube_own(value, axis):
    for bit in reversed(bits_of(lax.axis_size(axis))):
        half = value.shape[0] // 2
        value = value[:half] + swap(value[half:].astype(BF16), axis, bit).astype(F32)
    return value[0]


def launch(deps, kernel, *, grid_spec, **options):
    deps = list(deps)

    def run(*operands):
        count = len(operands)

        def body(*refs):
            return kernel(*refs[:count], *refs[count + len(deps) :])

        spec = pltpu.PrefetchScalarGridSpec(
            num_scalar_prefetch=grid_spec.num_scalar_prefetch,
            grid=grid_spec.grid,
            in_specs=list(grid_spec.in_specs) + [ANY] * len(deps),
            out_specs=grid_spec.out_specs,
            scratch_shapes=grid_spec.scratch_shapes,
        )
        return pl.pallas_call(body, grid_spec=spec, **options)(*operands, *deps)

    return run


def gate_kernel(value_ref, out_ref):
    pass


def gate(value, deps):
    return launch(
        deps,
        gate_kernel,
        grid_spec=pltpu.PrefetchScalarGridSpec(num_scalar_prefetch=0, grid=(1,), in_specs=[ANY], out_specs=ANY),
        out_shape=jax.ShapeDtypeStruct(value.shape, value.dtype),
        input_output_aliases={0: 0},
        compiler_params=params(),
        cost_estimate=cost(1, 1),
        name="gate",
    )(value)


def place_of():
    return jnp.stack(
        [lax.axis_index("fsdp"), lax.axis_index("ctx"), lax.axis_index("tp")]
    ).astype(jnp.int32)


class Pieces:
    def __init__(self, arrays, listing, shape, dims):
        self.arrays = arrays
        self.listing = listing
        self.shape = shape
        self.dims = dims

    def copies(self, place, refs, target, only_own=False):
        for number, index, where in self.listing:
            spot = where(place)
            if spot is None:
                continue
            row, col, own = spot
            if only_own and not own:
                continue
            rows, cols = self.shape
            if only_own:
                row = row - place[2] * self.dims
            yield (
                refs[number].at[index],
                target.at[pl.ds(pl.multiple_of(row, rows), rows), pl.ds(pl.multiple_of(col, cols), cols)],
            )


def gathered_columns(stack, lead, fsdp_count, tp_count, shape):
    rows, cols = shape
    listing = []
    for f in range(fsdp_count):
        for t in range(tp_count):
            listing.append(
                (0, (f * tp_count + t,) + lead, lambda place, f=f, t=t: (f * rows, t * cols, False))
            )
    return Pieces([stack], listing, shape, rows)


def gathered_rows(stack, lead, fsdp_count, tp_count, shape):
    rows, cols = shape
    listing = []
    for f in range(fsdp_count):
        for t in range(tp_count):
            listing.append(
                (0, (f * tp_count + t,) + lead, lambda place, f=f, t=t: (t * rows, f * cols, False))
            )
    return Pieces([stack], listing, shape, rows)


def travelled_rows(quarters, which, tp_count):
    rows, cols = quarters[0].shape[2:]
    arrays = list(quarters) + [swap(array, "fsdp", 1) for array in quarters]
    weights = []
    for weight in which:
        listing = []
        for number in range(8):
            for k in range(tp_count):

                def where(place, number=number, k=k):
                    tp = lax.rem(place[2] + (tp_count - k), tp_count)
                    row = tp * (2 * rows) + (place[1] ^ (number // 2 % 2)) * rows
                    col = (place[0] ^ (2 * (number % 2) + number // 4)) * cols
                    return (row, col, False)

                listing.append((number, (k, weight), where))
        weights.append(Pieces(arrays, listing, (rows, cols), 2 * rows))
    return weights


def fetch(copies, sems, base=0):
    started = [pltpu.make_async_copy(src, dst, sems.at[base + i]) for i, (src, dst) in enumerate(copies)]
    for copy in started:
        copy.start()
    return started


def group_mean(values, head_dim):
    width = values.shape[1]
    row = lax.broadcasted_iota(jnp.int32, (width, width), 0) // head_dim
    col = lax.broadcasted_iota(jnp.int32, (width, width), 1) // head_dim
    ones = jnp.where(row == col, 1.0 / head_dim, 0.0).astype(BF16)
    high = values.astype(BF16)
    rest = values - high.astype(F32)
    mid = rest.astype(BF16)
    low = (rest - mid.astype(F32)).astype(BF16)
    return mm(high, ones) + mm(mid, ones) + mm(low, ones)


def half_turn(values, head_dim):
    width = values.shape[1]
    half = head_dim // 2
    lane = lax.broadcasted_iota(jnp.int32, values.shape, 1)
    low = (lane & (head_dim - 1)) < half
    return jnp.where(low, pltpu.roll(values, width - half, 1), pltpu.roll(values, half, 1)), low


def project_kernel(
    place, tok_ref, gain_ref, hgain_ref, cos_ref, sin_ref, w_in, normed_ref, raw_ref, q_ref, kv_ref,
    w_ref, sems, *, head_dim, q_cols, rot_cols, chunk,
):
    shard = w_ref.shape[0] // w_in.shape[0]
    tile = tok_ref.shape[1]

    @pl.when(pl.program_id(0) == 0)
    def _():
        moves = []
        for m in range(w_in.shape[0]):
            row = pl.multiple_of((place[0] ^ m) * shard, shard)
            moves.append((w_in.at[m, pl.ds(0, shard)], w_ref.at[pl.ds(row, shard), :]))
        for copy in fetch(moves, sems):
            copy.wait()

    def norm(i, carry):
        rows = pl.ds(pl.multiple_of(i * chunk, chunk), chunk)
        x = tok_ref[0, rows, :].astype(F32)
        r = lax.rsqrt(jnp.mean(x * x, axis=-1, keepdims=True) + EPSILON)
        normed_ref[0, rows, :] = (x * r * gain_ref[...]).astype(BF16)
        return carry

    lax.fori_loop(0, tile // chunk, norm, 0)
    raw = mm(normed_ref[0], w_ref[...])
    raw_ref[0] = raw
    scale = lax.rsqrt(group_mean(raw * raw, head_dim) + EPSILON)
    n = raw * scale * hgain_ref[...]
    turned, low = half_turn(n, head_dim)
    rot = n * cos_ref[...] + jnp.where(low, -turned, turned) * sin_ref[...]
    lane = lax.broadcasted_iota(jnp.int32, raw.shape, 1)
    out = jnp.where(lane < rot_cols, rot, raw).astype(BF16)
    q_ref[0] = out[:, :q_cols]
    kv_ref[0] = out[:, q_cols:]


def project(place, tokens, gain, hgain, cos, sin, w_in, head_dim, q_cols, rot_cols, deps):
    seqs, rows, width = tokens.shape
    cols = w_in.shape[2]
    row_spec = lambda last: pl.BlockSpec((1, rows, last), lambda s, *_: (s, 0, 0))
    flat = lambda shape: pl.BlockSpec(shape, lambda s, *_: (0,) * len(shape))
    return launch(
        deps,
        functools.partial(
            project_kernel, head_dim=head_dim, q_cols=q_cols, rot_cols=rot_cols, chunk=64
        ),
        grid_spec=pltpu.PrefetchScalarGridSpec(
            num_scalar_prefetch=1,
            grid=(seqs,),
            in_specs=[
                row_spec(width), flat((1, width)), flat((1, cols)), flat((rows, cols)), flat((rows, cols)), ANY,
            ],
            out_specs=[row_spec(width), row_spec(cols), row_spec(q_cols), row_spec(cols - q_cols)],
            scratch_shapes=[
                pltpu.VMEM((width, cols), BF16), pltpu.SemaphoreType.DMA((w_in.shape[0],)),
            ],
        ),
        out_shape=[
            jax.ShapeDtypeStruct((seqs, rows, width), BF16),
            jax.ShapeDtypeStruct((seqs, rows, cols), F32),
            jax.ShapeDtypeStruct((seqs, rows, q_cols), BF16),
            jax.ShapeDtypeStruct((seqs, rows, cols - q_cols), BF16),
        ],
        compiler_params=params(),
        cost_estimate=cost(2 * seqs * rows * width * cols, seqs * rows * width * 4),
        name="project",
    )(place, tokens, gain, hgain, cos, sin, w_in)


def allowed_t(place, prefix, part, key_count, block, tile):
    j = lax.broadcasted_iota(jnp.int32, (key_count, tile), 0)
    key_pos = (place ^ (j // block)) * block + (j & (block - 1))
    query_pos = place * block + part * tile + lax.broadcasted_iota(jnp.int32, (key_count, tile), 1)
    return (key_pos <= query_pos) | (key_pos < prefix)


def attend_kernel(
    place, prefix, q_ref, kv_ref, out_ref, lse_ref, *, seq, heads, head_dim, tile, block
):
    part = pl.program_id(0)
    pairs = kv_ref[:, 0].reshape(-1, 2 * head_dim)
    keys = pairs[:, :head_dim]
    values = pairs[:, head_dim:]
    allowed = allowed_t(place[1], prefix[seq], part, pairs.shape[0], block, tile)
    for head in range(heads):
        lanes = slice(head * head_dim, (head + 1) * head_dim)
        scores = mm_t(keys, q_ref[0, :, lanes]) * (head_dim ** (-0.5))
        scores = jnp.where(allowed, scores, NEGATIVE)
        top = jnp.max(scores, axis=0, keepdims=True)
        weight = jnp.exp(scores - top)
        total = jnp.sum(weight, axis=0, keepdims=True)
        probs = weight * (1.0 / total)
        out_ref[0, :, lanes] = outer_sum(probs.astype(BF16), values).astype(BF16)
        lse_ref[0, head : head + 1, :] = top + jnp.log(total)


def attention_specs(seq, rows, q_cols, heads, kv_all):
    tile = min(256, rows)
    blocks, _, block, pair = kv_all.shape
    row_block = pl.BlockSpec((1, tile, q_cols), lambda i, *_: (seq, i, 0))
    own_block = pl.BlockSpec((1, tile, q_cols), lambda i, *_: (0, i, 0))
    key_block = pl.BlockSpec((blocks, 1, block, pair), lambda i, *_: (0, seq, 0, 0))
    stat_block = pl.BlockSpec((1, heads, tile), lambda i, *_: (0, 0, i))
    return tile, blocks, block, pair, row_block, own_block, key_block, stat_block


def attend(place, prefix, query, kv_all, heads, head_dim, seq, deps):
    _, rows, q_cols = query.shape
    tile, blocks, block, pair, row_block, own_block, key_block, stat_block = attention_specs(
        seq, rows, q_cols, heads, kv_all
    )
    elements = rows * blocks * block * heads
    return launch(
        deps,
        functools.partial(
            attend_kernel, seq=seq, heads=heads, head_dim=head_dim, tile=tile, block=block
        ),
        grid_spec=pltpu.PrefetchScalarGridSpec(
            num_scalar_prefetch=2,
            grid=(rows // tile,),
            in_specs=[row_block, key_block],
            out_specs=[own_block, stat_block],
        ),
        out_shape=[
            jax.ShapeDtypeStruct((1, rows, q_cols), BF16),
            jax.ShapeDtypeStruct((1, heads, rows), F32),
        ],
        compiler_params=params(),
        cost_estimate=cost(elements * 1024, query.size * 4, elements),
        name="attend",
    )(place, prefix, query, kv_all)


def attend_back_kernel(
    place, prefix, q_ref, kv_ref, d_ref, lse_ref, dq_ref, dkv_ref, *, seq, heads, head_dim, tile, block
):
    part = pl.program_id(0)
    scale = head_dim ** (-0.5)
    pairs = kv_ref[:, 0].reshape(-1, 2 * head_dim)
    keys = pairs[:, :head_dim]
    values = pairs[:, head_dim:]
    allowed = allowed_t(place[1], prefix[seq], part, pairs.shape[0], block, tile)
    dkeys = None
    dvalues = None
    for head in range(heads):
        lanes = slice(head * head_dim, (head + 1) * head_dim)
        query = q_ref[0, :, lanes]
        dout = d_ref[0, :, lanes]
        scores = mm_t(keys, query) * scale
        probs = jnp.where(allowed, jnp.exp(scores - lse_ref[0, head : head + 1, :]), 0.0)
        weighted = probs * mm_t(values, dout)
        delta = jnp.sum(weighted, axis=0, keepdims=True)
        dscore = (weighted - probs * delta).astype(BF16)
        dv = mm(probs.astype(BF16), dout)
        dk = mm(dscore, query)
        dkeys = dk if dkeys is None else dkeys + dk
        dvalues = dv if dvalues is None else dvalues + dv
        dq_ref[0, :, lanes] = outer_sum(dscore, keys) * scale
    both = jnp.concatenate([dkeys * scale, dvalues], axis=1).reshape(dkv_ref.shape[0], block, -1)

    @pl.when(part == 0)
    def _():
        dkv_ref[:, 0] = both

    @pl.when(part > 0)
    def _():
        dkv_ref[:, 0] += both


def attend_back(place, prefix, query, kv_all, dout, lse, heads, head_dim, seq, deps):
    _, rows, q_cols = query.shape
    tile, blocks, block, pair, row_block, own_block, key_block, stat_block = attention_specs(
        seq, rows, q_cols, heads, kv_all
    )
    elements = rows * blocks * block * heads
    return launch(
        deps,
        functools.partial(
            attend_back_kernel, seq=seq, heads=heads, head_dim=head_dim, tile=tile, block=block
        ),
        grid_spec=pltpu.PrefetchScalarGridSpec(
            num_scalar_prefetch=2,
            grid=(rows // tile,),
            in_specs=[row_block, key_block, row_block, stat_block],
            out_specs=[own_block, pl.BlockSpec((blocks, 1, block, pair), lambda i, *_: (0, 0, 0, 0))],
        ),
        out_shape=[
            jax.ShapeDtypeStruct((1, rows, q_cols), F32),
            jax.ShapeDtypeStruct((blocks, 1, block, pair), F32),
        ],
        compiler_params=params(),
        cost_estimate=cost(elements * 2560, query.size * 8, elements),
        name="attend_back",
    )(place, prefix, query, kv_all, dout, lse)


def layer_kernel(*refs, seq, tp_count, gate_w, down_w, out_w, up_w, out_count, step, own_cols):
    place, gain_ref, tok_in, og_in = refs[:4]
    refs = refs[4:]
    att_in, refs = refs[:tp_count], refs[tp_count:]
    gate_in, refs = refs[: len(gate_w.arrays)], refs[len(gate_w.arrays) :]
    down_in, refs = refs[: len(down_w.arrays)], refs[len(down_w.arrays) :]
    out_in = down_in
    outs, refs = refs[-out_count - 22 :][: out_count + 1], refs[-21:]
    token_ref = outs[-1]
    lay_out, dres_out, fin_out, hid_out, dgu_out, datt_out = outs[:-1]
    (
        tok, og, att, wo, wg, wu, wd, res, fin, hid, dgate, dup, lift, lay, dres, own_hid, own_dgu, datt,
        sems, more, final,
    ) = refs
    tile, width = tok.shape
    ff = wd.shape[0]
    cols = att_in[0].shape[1]

    moves = [(tok_in.at[seq], tok)]
    for k in range(tp_count):
        col = lax.rem(place[2] + (tp_count - k), tp_count) * cols
        moves.append((att_in[k], att.at[:, pl.ds(pl.multiple_of(col, cols), cols)]))
    moves += list(out_w.copies(place, out_in, wo))
    first = fetch(moves, sems)
    base = len(first)
    second = fetch(list(gate_w.copies(place, gate_in, wg)) + list(up_w.copies(place, gate_in, wu)), sems, base)
    base += len(second)
    third = fetch([(og_in.at[seq], og)] + list(down_w.copies(place, down_in, wd)), sems, base)
    for copy in first:
        copy.wait()

    def lanes_of(i):
        return pl.ds(pl.multiple_of(i * step, step), step)

    def out_part(i, total):
        lanes = lanes_of(i)
        row = tok[:, lanes].astype(F32) + mm(att[...], wo[:, lanes])
        res[:, lanes] = row
        return total + row * row

    total = lax.fori_loop(0, width // step, out_part, jnp.zeros((tile, step), F32))
    r = lax.rsqrt(jnp.sum(total, axis=-1, keepdims=True) / width + EPSILON)

    def norm(i, carry):
        lanes = lanes_of(i)
        fin[:, lanes] = (res[:, lanes] * r * gain_ref[:, lanes]).astype(BF16)
        return carry

    lax.fori_loop(0, width // step, norm, 0)
    leave_fin = pltpu.make_async_copy(fin, fin_out.at[seq], final.at[0])
    leave_fin.start()
    for copy in second + third:
        copy.wait()

    def inner(i, carry):
        lanes = lanes_of(i)
        gate = mm(fin[...], wg[:, lanes])
        up = mm(fin[...], wu[:, lanes])
        grad = mm_t(og[...], wd[lanes, :])
        sig = 1.0 / (1.0 + jnp.exp(-gate))
        silu = gate * sig
        hid[:, lanes] = (silu * up).astype(BF16)
        dgate[:, lanes] = (grad * up * sig * (1.0 + gate * (1.0 - sig))).astype(BF16)
        dup[:, lanes] = (grad * silu).astype(BF16)
        return carry

    lax.fori_loop(0, ff // step, inner, 0)
    own = pl.ds(pl.multiple_of(place[2] * own_cols, own_cols), own_cols)
    own_hid[...] = hid[:, own]
    own_dgu[:, :own_cols] = dgate[:, own]
    own_dgu[:, own_cols:] = dup[:, own]
    leave_own = [
        pltpu.make_async_copy(own_hid, hid_out.at[seq], final.at[1]),
        pltpu.make_async_copy(own_dgu, dgu_out.at[seq], final.at[2]),
    ]
    for copy in leave_own:
        copy.start()

    def outer(i, total):
        lanes = lanes_of(i)
        row = res[:, lanes]
        lay[:, lanes] = (row + mm(hid[...], wd[:, lanes])).astype(BF16)
        grad = mm_t(dgate[...], wg[lanes, :]) + mm_t(dup[...], wu[lanes, :])
        u = grad * gain_ref[:, lanes]
        lift[:, lanes] = u
        return total + row * u

    token_ref[...] = jnp.zeros_like(token_ref)
    total = lax.fori_loop(0, width // step, outer, jnp.zeros((tile, step), F32))
    leave_lay = pltpu.make_async_copy(lay, lay_out.at[seq], final.at[3])
    leave_lay.start()
    pull = r * r * r * (jnp.sum(total, axis=-1, keepdims=True) / width)

    def finish(i, carry):
        lanes = lanes_of(i)
        grad = og[:, lanes].astype(F32) + r * lift[:, lanes] - res[:, lanes] * pull
        dres[:, lanes] = grad.astype(BF16)
        return carry

    lax.fori_loop(0, width // step, finish, 0)
    leave_dres = pltpu.make_async_copy(dres, dres_out.at[seq], final.at[4])
    leave_dres.start()
    own_rows = pl.ds(pl.multiple_of(place[2] * cols, cols), cols)
    datt[...] = mm_t(dres[...], wo[own_rows, :]).astype(BF16)
    leave_datt = pltpu.make_async_copy(datt, datt_out.at[seq], final.at[5])
    leave_datt.start()
    for copy in leave_own + [leave_fin, leave_lay, leave_dres, leave_datt]:
        copy.wait()


def layer(place, tokens, out_grad, gain, att, gate_w, up_w, down_w, out_w, own_cols, seq, before, deps):
    seqs, rows, width = tokens.shape
    q_cols = att[0].shape[1]
    inner = q_cols * len(att)
    ff = own_cols * len(att)
    arrays = list(att) + gate_w.arrays + down_w.arrays
    count = 2 + len(att) + 2 * len(gate_w.listing) + len(down_w.listing) + len(out_w.listing)
    vec = pl.BlockSpec((1, width), lambda *_: (0, 0))
    outs = [
        jax.ShapeDtypeStruct((seqs, rows, last), BF16)
        for last in (width, width, width, own_cols, 2 * own_cols, q_cols)
    ]
    prior = list(before) if before is not None else []
    start = 4 + len(arrays)
    return launch(
        deps,
        functools.partial(
            layer_kernel, seq=seq, tp_count=len(att), gate_w=gate_w, up_w=up_w, down_w=down_w, out_w=out_w,
            out_count=len(outs), step=512, own_cols=own_cols,
        ),
        grid_spec=pltpu.PrefetchScalarGridSpec(
            num_scalar_prefetch=1,
            grid=(1,),
            in_specs=[vec, ANY, ANY] + [ANY] * (len(arrays) + len(prior)),
            out_specs=[ANY] * len(outs) + [pl.BlockSpec((8, 128), lambda *_: (0, 0))],
            scratch_shapes=[
                pltpu.VMEM((rows, width), BF16),
                pltpu.VMEM((rows, width), BF16),
                pltpu.VMEM((rows, inner), BF16),
                pltpu.VMEM((inner, width), BF16),
                pltpu.VMEM((width, ff), BF16),
                pltpu.VMEM((width, ff), BF16),
                pltpu.VMEM((ff, width), BF16),
                pltpu.VMEM((rows, width), F32),
                pltpu.VMEM((rows, width), BF16),
                pltpu.VMEM((rows, ff), BF16),
                pltpu.VMEM((rows, ff), BF16),
                pltpu.VMEM((rows, ff), BF16),
                pltpu.VMEM((rows, width), F32),
                pltpu.VMEM((rows, width), BF16),
                pltpu.VMEM((rows, width), BF16),
                pltpu.VMEM((rows, own_cols), BF16),
                pltpu.VMEM((rows, 2 * own_cols), BF16),
                pltpu.VMEM((rows, q_cols), BF16),
                pltpu.SemaphoreType.DMA((count,)),
                pltpu.SemaphoreType.DMA((1,)),
                pltpu.SemaphoreType.DMA((6,)),
            ],
        ),
        out_shape=outs + [jax.ShapeDtypeStruct((8, 128), F32)],
        input_output_aliases={start + i: i for i in range(len(prior))},
        compiler_params=params(),
        cost_estimate=cost(2 * rows * width * (6 * ff + inner + q_cols), rows * width * 12 + 8 * width * ff),
        name="layer",
    )(place, gain, tokens, out_grad, *arrays, *prior)


def head_back_kernel(
    raw_ref, dq_ref, dkv_ref, hgain_ref, cos_ref, sin_ref, out_ref, gsum_ref, *, head_dim, rot_cols
):
    raw = raw_ref[0]
    grad = jnp.concatenate([dq_ref[0], dkv_ref[0]], axis=1)
    lane = lax.broadcasted_iota(jnp.int32, raw.shape, 1)
    turned, low = half_turn(grad * sin_ref[...], head_dim)
    dn = grad * cos_ref[...] + jnp.where(low, turned, -turned)
    r = lax.rsqrt(group_mean(raw * raw, head_dim) + EPSILON)
    u = dn * hgain_ref[...]
    mean = group_mean(raw * u, head_dim)
    draw = r * u - raw * (r * r * r * mean)
    out_ref[...] = jnp.where(lane < rot_cols, draw, grad).astype(BF16)
    gsum_ref[...] = jnp.broadcast_to(jnp.sum(dn * raw * r, axis=0, keepdims=True), gsum_ref.shape)


def head_back(raw, dq, dkv, hgain, cos, sin, head_dim, rot_cols, seq, deps):
    _, rows, cols = raw.shape
    row_spec = lambda last, at: pl.BlockSpec((1, rows, last), lambda i: (at, 0, 0))
    flat = lambda shape: pl.BlockSpec(shape, lambda i: (0, 0))
    return launch(
        deps,
        functools.partial(head_back_kernel, head_dim=head_dim, rot_cols=rot_cols),
        grid_spec=pltpu.PrefetchScalarGridSpec(
            num_scalar_prefetch=0,
            grid=(1,),
            in_specs=[
                row_spec(cols, seq), row_spec(dq.shape[2], 0), row_spec(dkv.shape[2], 0), flat((1, cols)),
                flat((rows, cols)), flat((rows, cols)),
            ],
            out_specs=[flat((rows, cols)), flat((SPARE, cols))],
        ),
        out_shape=[jax.ShapeDtypeStruct((rows, cols), BF16), jax.ShapeDtypeStruct((SPARE, cols), F32)],
        compiler_params=params(),
        cost_estimate=cost(rows * cols * cols * 12, rows * cols * 14),
        name="head_back",
    )(raw, dq, dkv, hgain, cos, sin)


def input_kernel(*refs, tp_count, qkv_w, step):
    place, tok_ref, dres_ref, gain_ref = refs[:4]
    refs = refs[4:]
    d_in, refs = refs[:tp_count], refs[tp_count:]
    w_in, refs = refs[: len(qkv_w.arrays)], refs[len(qkv_w.arrays) :]
    out_ref, token_ref, dall, w, lift, sems = refs[-6:]
    tile, width = lift.shape
    cols = d_in[0].shape[1]
    moves = []
    for k in range(tp_count):
        col = lax.rem(place[2] + (tp_count - k), tp_count) * cols
        moves.append((d_in[k], dall.at[:, pl.ds(pl.multiple_of(col, cols), cols)]))
    moves += list(qkv_w.copies(place, w_in, w))
    started = fetch(moves, sems)

    def lanes_of(i):
        return pl.ds(pl.multiple_of(i * step, step), step)

    token_ref[...] = jnp.zeros_like(token_ref)

    def square(i, total):
        x = tok_ref[0, :, lanes_of(i)].astype(F32)
        return total + x * x

    total = lax.fori_loop(0, width // step, square, jnp.zeros((tile, step), F32))
    r = lax.rsqrt(jnp.sum(total, axis=-1, keepdims=True) / width + EPSILON)
    for copy in started:
        copy.wait()

    def outer(i, total):
        lanes = lanes_of(i)
        x = tok_ref[0, :, lanes].astype(F32)
        grad = mm_t(dall[...], w[lanes, :])
        u = grad * gain_ref[:, lanes]
        lift[:, lanes] = u
        return total + x * u

    total = lax.fori_loop(0, width // step, outer, jnp.zeros((tile, step), F32))
    pull = r * r * r * (jnp.sum(total, axis=-1, keepdims=True) / width)

    def finish(i, carry):
        lanes = lanes_of(i)
        x = tok_ref[0, :, lanes].astype(F32)
        grad = dres_ref[0, :, lanes].astype(F32) + r * lift[:, lanes] - x * pull
        out_ref[0, :, lanes] = grad.astype(BF16)
        return carry

    lax.fori_loop(0, width // step, finish, 0)


def input_part(place, tokens, dres, gain, pieces, qkv_w, seq, before, deps):
    seqs, rows, width = tokens.shape
    inner = pieces[0].shape[1] * len(pieces)
    row_spec = pl.BlockSpec((1, rows, width), lambda *_: (seq, 0, 0))
    vec = pl.BlockSpec((1, width), lambda *_: (0, 0))
    arrays = list(pieces) + qkv_w.arrays
    prior = [] if before is None else [before]
    return launch(
        deps,
        functools.partial(input_kernel, tp_count=len(pieces), qkv_w=qkv_w, step=512),
        grid_spec=pltpu.PrefetchScalarGridSpec(
            num_scalar_prefetch=1,
            grid=(1,),
            in_specs=[row_spec, row_spec, vec] + [ANY] * (len(arrays) + len(prior)),
            out_specs=[row_spec, pl.BlockSpec((8, 128), lambda *_: (0, 0))],
            scratch_shapes=[
                pltpu.VMEM((rows, inner), BF16),
                pltpu.VMEM((width, inner), BF16),
                pltpu.VMEM((rows, width), F32),
                pltpu.SemaphoreType.DMA((len(pieces) + len(qkv_w.listing),)),
            ],
        ),
        out_shape=[
            jax.ShapeDtypeStruct((seqs, rows, width), BF16),
            jax.ShapeDtypeStruct((8, 128), F32),
        ],
        input_output_aliases={4 + len(arrays): 0} if prior else {},
        compiler_params=params(),
        cost_estimate=cost(2 * rows * width * inner, rows * width * 6 + width * inner * 2),
        name="input_part",
    )(place, tokens, dres, gain, *arrays, *prior)


def weight_grad_kernel(place, *refs, count, tails):
    keep_ref, give_ref = refs[-2:]
    step = pl.program_id(0)
    for i in range(count):
        grad = outer_sum(refs[2 * i][...], refs[2 * i + 1][...])
        if tails:
            grad = jnp.concatenate([grad, sum(ref[...] for ref in refs[2 * count : -2])], axis=0)

        @pl.when(step < 2)
        def _():
            keep_ref[0, i] = grad

        @pl.when(step >= 2)
        def _():
            give_ref[0, i] = grad.astype(BF16)


def weight_grad(place, pairs, cut_left, name, deps, tails=()):
    rows = pairs[0][0].shape[0]
    left_cols, right_cols = pairs[0][0].shape[1], pairs[0][1].shape[1]

    def piece(step, place):
        return place[0] ^ (2 * (step & 1) + (step >> 1))

    moving = lambda cols: pl.BlockSpec((rows, cols // 4), lambda m, place: (0, piece(m, place)))
    fixed = lambda cols: pl.BlockSpec((rows, cols), lambda m, place: (0, 0))
    if cut_left:
        specs = [moving(left_cols), fixed(right_cols)]
        shape = (left_cols // 4 + (SPARE if tails else 0), right_cols)
    else:
        specs = [fixed(left_cols), moving(right_cols)]
        shape = (left_cols, right_cols // 4)
    count = len(pairs)
    block = (1, count) + shape
    return launch(
        deps,
        functools.partial(weight_grad_kernel, count=count, tails=len(tails)),
        grid_spec=pltpu.PrefetchScalarGridSpec(
            num_scalar_prefetch=1,
            grid=(4,),
            in_specs=specs * count + [pl.BlockSpec(tail.shape, lambda m, place: (0, 0)) for tail in tails],
            out_specs=[
                pl.BlockSpec(block, lambda m, place: (jnp.minimum(m, 1), 0, 0, 0)),
                pl.BlockSpec(block, lambda m, place: (jnp.maximum(m - 2, 0), 0, 0, 0)),
            ],
        ),
        out_shape=[
            jax.ShapeDtypeStruct((2,) + block[1:], F32),
            jax.ShapeDtypeStruct((2,) + block[1:], BF16),
        ],
        compiler_params=params(),
        cost_estimate=cost(2 * count * rows * left_cols * right_cols, count * rows * (left_cols + right_cols) * 2),
        name=name,
    )(place, *[array for pair in pairs for array in pair], *tails)


def join_core(parts):
    keep, give = parts
    got = swap(give, "fsdp", 1)
    return got, keep + got.astype(F32)


def join_far(total, deps=()):
    give = total[1].astype(BF16)
    got = swap(gate(give, deps) if deps else give, "fsdp", 2)
    return got, total[0] + got.astype(F32)


def join_ctx(value, before, after=()):
    for bit in bits_of(lax.axis_size("ctx")):
        low = gate(value.astype(BF16), before) if before else value.astype(BF16)
        got = swap(low, "ctx", bit)
        if after:
            got = gate(got, after)
        value = low.astype(F32) + got.astype(F32)
    return value


def shards(
    tokens, attn_gain, w_query, key_matrix, value_matrix, query_gain, key_gain, w_out, ffn_gain,
    w_gate, w_up, w_down, prefix_len, out_grad,
):
    seqs, block_len, width = tokens.shape
    rows = seqs * block_len
    place = place_of()
    ctx_count = lax.axis_size("ctx")
    fsdp_count = lax.axis_size("fsdp")
    tp_count = lax.axis_size("tp")
    head_dim = query_gain.shape[0] * fsdp_count
    q_cols = w_query.shape[1]
    kv_cols = key_matrix.shape[1]
    cols = q_cols + 2 * kv_cols
    heads = q_cols // head_dim
    own_ff = w_gate.shape[1]
    rot_cols = q_cols + kv_cols
    shard_rows = w_query.shape[0]

    gains = jnp.concatenate([attn_gain, ffn_gain, query_gain, key_gain])
    gain_rows = -(-gains.size // cols)
    extra = jnp.pad(gains, (0, gain_rows * cols - gains.size)).reshape(gain_rows, cols)
    w_qkv = jnp.concatenate([w_query, key_matrix, value_matrix], axis=1)
    carried = jnp.concatenate([w_qkv, jnp.pad(extra, ((0, 16 - gain_rows), (0, 0)))], axis=0)
    from_x = swap(carried, "fsdp", 2)
    near = jnp.stack([carried, from_x])
    if ctx_count == 2:
        half = w_out.shape[0] // 2
        halves = jnp.stack([lax.dynamic_slice_in_dim(w, place[1] * half, half, 0) for w in (w_out, w_down)])
        sent = send_all(halves, "tp")
        near = gate(near, sent[1:2])
    far = swap(near, "fsdp", 1)
    own_qkv = jnp.stack([near[0], far[0], near[1], far[1]])

    gate_up = lax.all_gather(jnp.stack([w_gate, w_up]), ("fsdp", "tp"), axis=0)
    gate_w = gathered_columns(gate_up, (0,), fsdp_count, tp_count, w_gate.shape)
    up_w = gathered_columns(gate_up, (1,), fsdp_count, tp_count, w_up.shape)

    gains = in_order(own_qkv[:, shard_rows : shard_rows + gain_rows].reshape(fsdp_count, -1), "fsdp").astype(F32)
    a, q = attn_gain.size, query_gain.size
    attn_gain32 = gains[:, :a].reshape(1, -1)
    ffn_gain32 = gains[:, a : 2 * a].reshape(1, -1)
    query_gain32 = gains[:, 2 * a : 2 * a + q].reshape(1, -1)
    key_gain32 = gains[:, 2 * a + q : 2 * a + 2 * q].reshape(1, -1)
    hgain = jnp.concatenate(
        [query_gain32] * heads + [key_gain32] * (kv_cols // head_dim) + [jnp.ones((1, kv_cols), F32)], axis=1
    )
    query_pos = place[1] * block_len + jnp.arange(block_len, dtype=jnp.int32)
    cos_half, sin_half = rotary_tables(query_pos, head_dim)
    copies = 2 * cols // head_dim
    cos = jnp.concatenate([cos_half] * copies, axis=1)
    sin = jnp.concatenate([sin_half] * copies, axis=1)

    normed, raw, query_low, kv_low = project(
        place, tokens, attn_gain32, hgain, cos, sin, own_qkv, head_dim, q_cols, rot_cols, []
    )
    kv_all = cube(kv_low, "ctx")
    att_own, lse, att = [None] * seqs, [None] * seqs, [None] * seqs
    whole_y, deps = [], []
    if ctx_count == 2:
        near_x = jnp.stack(sent[:1] + [gate(piece, [kv_low]) for piece in sent[1:]])
        far_x = swap(near_x, "fsdp", 2)
        near_y = swap(gate(near_x, [kv_all]), "ctx", 1)
    for seq in range(seqs):
        att_own[seq], lse[seq] = attend(place, prefix_len, query_low, kv_all, heads, head_dim, seq, deps)
        att[seq] = send_all(att_own[seq][0], "tp")
        deps = [lse[seq]] + att[seq][1:]
        if seq == 0 and ctx_count == 2:
            far_x = gate(far_x, deps + [near_y])
            far_y = swap(far_x, "ctx", 1)
            whole_y = [near_y, far_y]
            deps = deps + [far_x]

    if ctx_count == 2:
        out_w, down_w = travelled_rows([near_x, far_x, near_y, far_y], range(2), tp_count)
    else:
        out_down = lax.all_gather(jnp.stack([w_out, w_down]), ("fsdp", "tp"), axis=0)
        out_w = gathered_rows(out_down, (0,), fsdp_count, tp_count, w_out.shape)
        down_w = gathered_rows(out_down, (1,), fsdp_count, tp_count, w_down.shape)
    w_later = gate(w_qkv, [lse[-1]] + whole_y)
    qkv_all = lax.all_gather(w_later, ("fsdp", "tp"), axis=0)
    qkv_w = gathered_columns(qkv_all, (), fsdp_count, tp_count, w_qkv.shape)

    results = None
    dquery, owned, dqkv, head_sums, pieces = ([None] * seqs for _ in range(5))

    def finish_heads(seq, deps):
        dqkv[seq], head_sums[seq] = head_back(
            raw, dquery[seq], owned[seq], hgain, cos, sin, head_dim, rot_cols, seq, deps
        )
        pieces[seq] = send_all(dqkv[seq], "tp")

    deps = [w_later]
    for seq in range(seqs):
        *results, done = layer(
            place, tokens, out_grad, ffn_gain32, att[seq], gate_w, up_w, down_w, out_w, own_ff, seq, results, deps
        )
        deps = [done]
        if seq + 1 < seqs:
            deps = deps + att[seq + 1][1:]
        layer_low, dres_low, ffn_in, hidden, dgate_up, dattended = results
        dquery[seq], dkv = attend_back(
            place, prefix_len, query_low, kv_all, dattended, lse[seq], heads, head_dim, seq, deps
        )
        owned[seq] = cube_own(dkv, "ctx")
        deps = [dquery[seq]]
        if seq + 1 < seqs:
            finish_heads(seq, deps)
            deps = [head_sums[seq]]
    flat = lambda value: value.reshape(rows, -1)
    gate_up_parts = weight_grad(
        place, [(flat(ffn_in), flat(dgate_up))], True, "grad_gate_up",
        deps + [qkv_all] + [array for piece in pieces[:-1] for array in piece[1:]],
    )
    gate_up_got, gate_up_sum = join_core(gate_up_parts)
    finish_heads(seqs - 1, [gate_up_parts[0]])
    attended = jnp.concatenate([value[0] for value in att_own], axis=0)
    joined = jnp.concatenate(dqkv, axis=0)
    qkv_parts = weight_grad(place, [(flat(normed), joined)], True, "grad_qkv", [head_sums[-1]], head_sums)
    qkv_got, qkv_sum = join_core(qkv_parts)
    down_out_parts = weight_grad(
        place, [(flat(hidden), flat(out_grad)), (attended, flat(dres_low))], False, "grad_down_out",
        [qkv_parts[0], qkv_got, gate_up_got],
    )
    down_out_got, down_out_sum = join_core(down_out_parts)
    gate_up_far, gate_up_sum = join_far(gate_up_sum)
    qkv_far, qkv_sum = join_far(qkv_sum)
    deps = [down_out_parts[0], down_out_got]
    input_grad, done = None, [None] * seqs
    for seq in range(seqs):
        input_grad, done[seq] = input_part(
            place, tokens, dres_low, attn_gain32, pieces[seq], qkv_w, seq, input_grad, deps
        )
        deps = [done[seq], gate_up_far, qkv_far]
    gate_up_grad = join_ctx(gate_up_sum, done[:1], done[-1:])[0]
    qkv_grad = join_ctx(qkv_sum, done[:1], done[-1:])[0]
    down_low = gate(join_far(down_out_sum)[1].astype(BF16), done[-1:])
    down_out = join_ctx(down_low, ())

    head_sum = qkv_grad[shard_rows].reshape(-1, head_dim)
    qkv_grad = qkv_grad[:shard_rows]
    weighted = lambda weight, grad: jnp.sum(weight.astype(F32) * grad, axis=1)
    grad_gate, grad_up = gate_up_grad[:, :own_ff], gate_up_grad[:, own_ff:]
    sums = jnp.concatenate(
        [
            weighted(w_qkv, qkv_grad),
            weighted(w_gate, grad_gate) + weighted(w_up, grad_up),
            jnp.sum(head_sum[:heads], axis=0),
            jnp.sum(head_sum[heads : heads + kv_cols // head_dim], axis=0),
        ]
    )
    sums = paired_sum(send_all(gate(sums.reshape(1, -1), [down_low]), "tp"))[0]
    member = lax.axis_index("fsdp")
    head_share = lambda start: lax.dynamic_slice_in_dim(sums, start + member * q, q, 0)
    return (
        layer_low,
        input_grad,
        sums[:a] / attn_gain.astype(F32),
        qkv_grad[:, :q_cols],
        qkv_grad[:, q_cols : q_cols + kv_cols],
        qkv_grad[:, q_cols + kv_cols :],
        head_share(2 * a),
        head_share(2 * a + head_dim),
        down_out[1],
        sums[a : 2 * a] / ffn_gain.astype(F32),
        grad_gate,
        grad_up,
        down_out[0],
    )


def solution(mesh):
    columns = P("fsdp", "tp")
    across = P("tp", "fsdp")
    vector = P("fsdp")
    data = P("fsdp", "ctx", None)
    return jax.shard_map(
        shards,
        mesh=mesh,
        in_specs=(
            data, vector, columns, columns, columns, vector, vector, across, vector,
            columns, columns, across, vector, data,
        ),
        out_specs=(
            data, data, vector, columns, columns, columns, vector, vector, across, vector,
            columns, columns, across,
        ),
        check_vma=False,
    )
```
